32 devices in a mesh: wide: 8 (over y, x, core), narrow: 4 (over z).
Axes of the slice: x: 2, y: 2, z: 4, core: 2. Of those that a mesh axis runs over, the one named last changes fastest.
Arguments:
- tokens: bfloat16 [32768, 1024], P(('wide', 'narrow')), may hold values from -6 to 6
- cotangent: bfloat16 [32768, 1024], P(('wide', 'narrow')), may hold values from -6 to 6
- gain_mix: bfloat16 [1024], P(('wide', 'narrow')), may hold values from 0.099609375 to 1.8984375
- in_weight: bfloat16 [1024, 3072], P(('wide', 'narrow')), may hold values from -0.1875 to 0.1875
- conv_taps: bfloat16 [3, 1024], P(None, ('wide', 'narrow')), may hold values from -3 to 3
- out_weight: bfloat16 [1024, 1024], P(('wide', 'narrow')), may hold values from -0.1875 to 0.1875
- gain_ffn: bfloat16 [1024], P(('wide', 'narrow')), may hold values from 0.099609375 to 1.8984375
- gate_weight: bfloat16 [1024, 4608], P(('wide', 'narrow')), may hold values from -0.1875 to 0.1875
- up_weight: bfloat16 [1024, 4608], P(('wide', 'narrow')), may hold values from -0.1875 to 0.1875
- down_weight: bfloat16 [4608, 1024], P(('wide', 'narrow')), may hold values from -0.1875 to 0.1875
- doc_lengths: int32 [8, 16], replicated, may hold values from 1 to 2048, as said below
- valid_count: int32 [8], replicated, may hold values from 3584 to 4096
Outputs:
- output: float32 [32768, 1024], P(('wide', 'narrow'))
- grad_tokens: float32 [32768, 1024], P(('wide', 'narrow'))
- grad_gain_mix: float32 [1024], P(('wide', 'narrow'))
- grad_in_weight: float32 [1024, 3072], P(('wide', 'narrow'))
- grad_conv_taps: float32 [3, 1024], P(None, ('wide', 'narrow'))
- grad_out_weight: float32 [1024, 1024], P(('wide', 'narrow'))
- grad_gain_ffn: float32 [1024], P(('wide', 'narrow'))
- grad_gate_weight: float32 [1024, 4608], P(('wide', 'narrow'))
- grad_up_weight: float32 [1024, 4608], P(('wide', 'narrow'))
- grad_down_weight: float32 [4608, 1024], P(('wide', 'narrow'))
The draws below stay inside these ranges and needn't reach their ends.
Inputs may be any that keep to these rules, and one draw needn't show every extreme that they name: Each row of doc_lengths fills its packed row of 4096 tokens exactly; the longest document of every row has exactly 2048 tokens; no document starts at a place p > 0 with p % 1024 < 2.
All inputs are finite; a program needn't handle non-finite values.
Results may differ from the reference program's by a relative error of at most 0.0084.
Values may be sent and summed in bfloat16 or wider, within the bound.
A program may use at most 320 MiB of HBM per device.

```python
import jax
import jax.numpy as jnp
from jax import lax

D = 1024
FF = 4608
ROW_LEN = 4096
TOK_DEV = 1024
DOCS = 16
DOC_MOST = 2048
TOKENS = 32768
ROWS = 8


def draw_one_row(row_key):
    key_block, key_rest, key_order = jax.random.split(row_key, 3)
    residue = jax.random.randint(key_rest, (), 2, TOK_DEV).astype(jnp.int32)
    block_pick = jax.random.randint(key_block, (), 0, DOC_MOST // TOK_DEV).astype(jnp.int32)
    big_start = block_pick * TOK_DEV + residue
    big_end = big_start + DOC_MOST
    places = jnp.arange(ROW_LEN, dtype=jnp.int32)
    allowed = (places % TOK_DEV >= 2) & ((places < big_start) | (places > big_end))
    order = jax.random.permutation(key_order, ROW_LEN).astype(jnp.int32)
    scores = jnp.where(allowed, order, -1)
    picked = lax.top_k(scores, DOCS - 3)[1].astype(jnp.int32)
    starts = jnp.concatenate([jnp.zeros((1,), jnp.int32), big_start[None], big_end[None], picked])
    starts = jnp.sort(starts)
    ends = jnp.concatenate([starts[1:], jnp.full((1,), ROW_LEN, jnp.int32)])
    return (ends - starts).astype(jnp.int32)


def draw_doc_lengths(key, part):
    row_keys = jax.random.split(jax.random.fold_in(key, 17), ROWS)
    return jax.vmap(draw_one_row)(row_keys)


def place_ends(values, rng, least, high):
    longest = values.shape.index(max(values.shape))
    spots = []
    for shift in (0, 1):
        where = [jax.random.randint(jax.random.fold_in(rng, axis), (), 0, length) for axis, length in enumerate(values.shape)]
        where[longest] = (where[longest] + shift) % values.shape[longest]
        spots.append(tuple(where))
    return values.at[spots[0]].set(least).at[spots[1]].set(high)


def strengthened(array, rng, source, target, parts, factor):
    owner, partner = [(jnp.arange(array.shape[position]) // (array.shape[position] // parts)).reshape([-1 if axis == position else 1 for axis in range(array.ndim)]) for position in (source, target)]
    chosen = jax.random.permutation(rng, parts)[partner]
    strong = (owner == chosen) | (owner == (partner + parts // 2) % parts)
    return jnp.where(strong, factor * array, array)


def level_of(key, dims, cuts, low, largest):
    def one(axis_at, shards_of):
        heights = jax.random.uniform(jax.random.fold_in(jax.random.fold_in(key, 6), axis_at), (shards_of,), jnp.float32, low / len(cuts), largest / len(cuts))
        return jnp.repeat(jnp.exp(heights), dims[axis_at] // shards_of).reshape((-1,) + (1,) * (len(dims) - axis_at - 1))

    factor_of = one(*cuts[0])
    for cut in cuts[1:]:
        factor_of = factor_of * one(*cut)
    return factor_of


def centred(stream_key, shape, deviation, most, cuts=(), kind=jnp.bfloat16):
    array = deviation * jax.random.normal(stream_key, shape, jnp.float32)
    if cuts:
        array = array * level_of(stream_key, shape, cuts, -0.22, 0.18)
    return jnp.clip(array, -most, most).astype(kind)


def heavy_noise(own_key, extent, scale, limit, cuts, heavy, kind=jnp.bfloat16):
    values = scale * jax.random.normal(own_key, extent, jnp.float32)
    if cuts:
        values = values * level_of(own_key, extent, cuts, -0.22, 0.18)
    return jnp.clip(strengthened(values, jax.random.fold_in(own_key, 3), *heavy), -limit, limit).astype(kind)


def setup_inputs(seed: int = 0) -> dict:
    arg_keys = jax.random.split(jax.random.key(seed), 13)
    tokens = heavy_noise(arg_keys[0], (TOKENS, D), 1.0, 6.0, ((0, 32),), (0, 1, 32, 2.75))
    cotangent = centred(arg_keys[1], (TOKENS, D), 1.0, 6.0, ((0, 32),))
    gain_mix = jnp.clip(1.0 + 0.18 * jax.random.normal(arg_keys[2], (D,), jnp.float32), 0.099609375, 1.8984375).astype(jnp.bfloat16)
    in_weight = centred(arg_keys[3], (D, 3 * D), D ** -0.5, 0.1875, ((0, 32),))
    conv_taps = centred(arg_keys[4], (3, D), 0.6, 3.0, ((1, 32),))
    out_weight = centred(arg_keys[5], (D, D), D ** -0.5, 0.1875, ((0, 32),))
    gain_ffn = jnp.clip(1.0 + 0.18 * jax.random.normal(arg_keys[6], (D,), jnp.float32), 0.099609375, 1.8984375).astype(jnp.bfloat16)
    gate_weight = centred(arg_keys[7], (D, FF), D ** -0.5, 0.1875, ((0, 32),))
    up_weight = centred(arg_keys[8], (D, FF), D ** -0.5, 0.1875, ((0, 32),))
    down_weight = centred(arg_keys[9], (FF, D), (FF // 4) ** -0.5, 0.1875, ((0, 32),))
    doc_lengths = draw_doc_lengths(jax.random.fold_in(arg_keys[12], 71), 0)
    valid_count = place_ends(jax.random.randint(arg_keys[11], (ROWS,), ROW_LEN - TOK_DEV // 2, ROW_LEN + 1), jax.random.fold_in(arg_keys[11], 1), ROW_LEN - TOK_DEV // 2, ROW_LEN).astype(jnp.int32)
    return {"tokens": tokens, "cotangent": cotangent, "gain_mix": gain_mix, "in_weight": in_weight, "conv_taps": conv_taps, "out_weight": out_weight, "gain_ffn": gain_ffn, "gate_weight": gate_weight, "up_weight": up_weight, "down_weight": down_weight, "doc_lengths": doc_lengths, "valid_count": valid_count}


@jax.custom_vjp
def low(v):
    return lax.optimization_barrier(v.astype(jnp.bfloat16)).astype(jnp.float32)

@jax.custom_vjp
def low_back(v):
    return v

def low_keep(v):
    return (low(v), None)

def low_pass(kept, grad):
    return (grad,)

def back_keep(v):
    return (v, None)

def back_low(kept, grad):
    return (low(grad),)
low.defvjp(low_keep, low_pass)
low_back.defvjp(back_keep, back_low)
epsilon = 1e-05

def product(left, right):
    return jnp.dot(left, right, precision=lax.Precision.HIGHEST, preferred_element_type=jnp.float32)

def rms_norm(values, gain_vec):
    inv_rms = lax.rsqrt(lax.optimization_barrier(jnp.mean(values * values, axis=1, keepdims=True)) + epsilon)
    return values * inv_rms * gain_vec[None, :]

def doc_masks(lengths, limit_count):
    lengths = lengths.astype(jnp.int32)
    offsets = (jnp.cumsum(lengths) - lengths).astype(jnp.int32)
    places = jnp.arange(ROW_LEN, dtype=jnp.int32)
    begins = jnp.any(offsets[None, :] == places[:, None], axis=1)
    before = jnp.any(offsets[None, :] == places[:, None] - 1, axis=1)
    keep_one = jnp.where(begins, 0.0, 1.0).astype(jnp.float32)
    keep_two = jnp.where(begins | before, 0.0, 1.0).astype(jnp.float32)
    live_mask = jnp.where(places < limit_count, 1.0, 0.0).astype(jnp.float32)
    return (keep_one[:, None], keep_two[:, None], live_mask[:, None])

def block(tok_row, mix_gain, w_in, taps, w_out, ffn_gain, w_gate, w_up, w_down, keep_one, keep_two, live_mask):
    normed_mix = low(rms_norm(tok_row, mix_gain))
    projected = low_back(product(normed_mix, w_in))
    b_part = projected[:, :D]
    c_part = projected[:, D:2 * D]
    x_part = projected[:, 2 * D:]
    gated = b_part * x_part
    extended = jnp.pad(gated, ((2, 0), (0, 0)))
    conv_out = taps[2][None, :] * gated + taps[1][None, :] * keep_one * extended[1:-1] + taps[0][None, :] * keep_two * extended[:-2]
    mixed = low(c_part * conv_out)
    hidden = tok_row + low_back(product(mixed, w_out))
    normed_ffn = low(rms_norm(hidden, ffn_gain))
    gate_val = low_back(product(normed_ffn, w_gate))
    up_val = low_back(product(normed_ffn, w_up))
    act = low(jax.nn.silu(gate_val) * up_val)
    ffn_out = low_back(product(act, w_down))
    return live_mask * (hidden + ffn_out)

def reference(tokens, cotangent, gain_mix, in_weight, conv_taps, out_weight, gain_ffn, gate_weight, up_weight, down_weight, doc_lengths, valid_count):
    weights = tuple((weight_arr.astype(jnp.float32) for weight_arr in (gain_mix, in_weight, conv_taps, out_weight, gain_ffn, gate_weight, up_weight, down_weight)))
    rows_in = tokens.astype(jnp.float32).reshape(-1, ROW_LEN, D)
    rows_cot = cotangent.astype(jnp.float32).reshape(-1, ROW_LEN, D)

    def one_row(totals, packed):
        tok_row, cot_row, lengths, limit_count = packed
        keep_one, keep_two, live_mask = doc_masks(lengths, limit_count)

        def run_block(tok_in, *params):
            return block(tok_in, *params, keep_one, keep_two, live_mask)
        out_row, pull = jax.vjp(run_block, tok_row, *weights)
        grads = pull(cot_row)
        totals = tuple((total + grad_part for total, grad_part in zip(totals, grads[1:])))
        return (totals, (out_row, grads[0]))
    zeros = tuple((jnp.zeros_like(weight_arr) for weight_arr in weights))
    totals, (out_rows, grad_rows) = lax.scan(one_row, zeros, (rows_in, rows_cot, doc_lengths, valid_count))
    output = out_rows.reshape(-1, D)
    grad_tokens = grad_rows.reshape(-1, D)
    return (output, grad_tokens, totals[0], totals[1], totals[2], totals[3], totals[4], totals[5], totals[6], totals[7])
```

```python
import functools

import jax
import jax.numpy as jnp
from jax import lax
from jax.experimental import pallas as pl
from jax.experimental.pallas import tpu as pltpu
from jax.sharding import PartitionSpec as P

ROW_LEN = 4096
epsilon = 1e-05
F32 = jnp.float32
BF = jnp.bfloat16
MESH = pl.DeviceIdType.MESH
ANY = pl.BlockSpec(memory_space=pl.ANY)
VM = pl.BlockSpec(memory_space=pltpu.VMEM)


def dg(a, b, ca, cb):
    return lax.dot_general(a, b, (((ca,), (cb,)), ((), ())), preferred_element_type=F32)


class Place:
    def __init__(self):
        w = lax.axis_index("wide")
        z = lax.axis_index("narrow")
        c = lax.rem(w, 2)
        x = lax.rem(w // 2, 2)
        y = w // 4
        self.w, self.z, self.c, self.x, self.y = w, z, c, x, y
        self.core = (w + 1 - 2 * c, z)
        self.xn = (w + 2 - 4 * x, z)
        self.yn = (w + 4 - 8 * y, z)
        self.zs = [(w, lax.rem(z + k, 4)) for k in (1, 2, 3)]
        self.zto = [lax.rem(z + k, 4) for k in (1, 2, 3)]
        self.zfrom = [lax.rem(z + 4 - k, 4) for k in (1, 2, 3)]

        def base(yy, xx, cc):
            return 16 * yy + 8 * xx + 4 * cc

        self.own, self.xb = base(y, x, c), base(y, 1 - x, c)
        self.yb, self.db = base(1 - y, x, c), base(1 - y, 1 - x, c)
        self.sown, self.sxb = base(y, x, 1 - c), base(y, 1 - x, 1 - c)
        self.syb, self.sdb = base(1 - y, x, 1 - c), base(1 - y, 1 - x, 1 - c)
        self.me = self.own + z

    def greet(self):
        bar = pltpu.get_barrier_semaphore()
        peers = [self.core, self.xn, self.yn] + self.zs
        for p in peers:
            pl.semaphore_signal(bar, inc=1, device_id=p, device_id_type=MESH)
        pl.semaphore_wait(bar, len(peers))


def remote(src, dst, ss, rs, dev):
    return pltpu.make_async_remote_copy(
        src_ref=src, dst_ref=dst, send_sem=ss, recv_sem=rs, device_id=dev, device_id_type=MESH
    )


class Gather:
    def __init__(self, pc, shard, full, ss, rs):
        self.pc, self.shard, self.full, self.ss, self.rs = pc, shard, full, ss, rs

    def zc(self, k):
        return remote(self.shard(), self.full(self.pc.me, 1), self.ss.at[k], self.rs.at[k], self.pc.zs[k])

    def zr(self, k):
        v = self.full(self.pc.own + self.pc.zfrom[k], 1)
        return remote(v, v, self.ss.at[k], self.rs.at[k], self.pc.zs[k])

    def loc(self):
        return pltpu.make_async_copy(self.shard(), self.full(self.pc.me, 1), self.ss.at[11])

    def cp(self, k, b, n, dev):
        v = self.full(b, n)
        return remote(v, v, self.ss.at[k], self.rs.at[k], dev)

    def s0(self):
        self.loc().start()
        for k in range(3):
            self.zc(k).start()

    def s1(self):
        p = self.pc
        self.loc().wait()
        for k in range(3):
            self.zr(k).wait_recv()
        self.cp(3, p.own, 4, p.xn).start()
        self.cp(4, p.own, 4, p.yn).start()
        self.cp(5, p.own, 4, p.core).start()

    def s2(self):
        p = self.pc
        self.cp(3, p.xb, 4, p.xn).wait_recv()
        self.cp(6, p.xb, 2, p.yn).start()
        self.cp(7, p.xb, 4, p.core).start()
        self.cp(4, p.yb, 4, p.yn).wait_recv()
        self.cp(8, p.yb + 2, 2, p.xn).start()
        self.cp(9, p.yb, 4, p.core).start()

    def s3(self):
        p = self.pc
        self.cp(6, p.db, 2, p.yn).wait_recv()
        self.cp(8, p.db + 2, 2, p.xn).wait_recv()
        self.cp(10, p.db, 4, p.core).start()

    def s4(self):
        p = self.pc
        for k, b in ((5, p.sown), (7, p.sxb), (9, p.syb), (10, p.sdb)):
            self.cp(k, b, 4, p.core).wait_recv()

    def fin(self):
        p = self.pc
        for k in range(3):
            self.zc(k).wait_send()
        for k, b, n in (
            (3, p.own, 4), (4, p.own, 4), (5, p.own, 4), (6, p.xb, 2),
            (7, p.xb, 4), (8, p.yb + 2, 2), (9, p.yb, 4), (10, p.db, 4),
        ):
            self.cp(k, b, n, p.core).wait_send()


NG = 12


class Scatter:
    def __init__(self, pc, bufs, h, out):
        self.pc, self.h, self.out = pc, h, out
        (self.part, self.l0, self.ldx, self.ldy, self.lx, self.ly, self.lz,
         self.sd, self.sx, self.sy, self.so, self.sz, self.ob, self.ss, self.rs, self.os) = bufs

    def hr(self):
        return pl.ds(0, self.h)

    def c0(self, j, s):
        p = self.pc
        return remote(self.part.at[s, :, :, :, 1 - p.c, :, self.hr()], self.l0.at[j, :, :, :, :, self.hr()],
                      self.ss.at[j, 0], self.rs.at[j, 0], p.core)

    def cdx(self, j, s):
        return remote(self.sd.at[s, :, pl.ds(0, 2), self.hr()], self.ldx.at[j, :, :, self.hr()],
                      self.ss.at[j, 1], self.rs.at[j, 1], self.pc.xn)

    def cdy(self, j, s):
        return remote(self.sd.at[s, :, pl.ds(2, 2), self.hr()], self.ldy.at[j, :, :, self.hr()],
                      self.ss.at[j, 2], self.rs.at[j, 2], self.pc.yn)

    def cx(self, j, s):
        return remote(self.sx.at[s, :, :, self.hr()], self.lx.at[j, :, :, self.hr()],
                      self.ss.at[j, 3], self.rs.at[j, 3], self.pc.xn)

    def cy(self, j, s):
        return remote(self.sy.at[s, :, :, self.hr()], self.ly.at[j, :, :, self.hr()],
                      self.ss.at[j, 4], self.rs.at[j, 4], self.pc.yn)

    def cz(self, j, s, k):
        return remote(self.sz.at[s, :, self.pc.zto[k], self.hr()], self.lz.at[j, k, :, self.hr()],
                      self.ss.at[j, 5 + k], self.rs.at[j, 5 + k], self.pc.zs[k])

    def r0(self, j, s):
        self.c0(j, s).start()

    def q(self, j, s, a, yy, xx):
        hr = self.hr()
        return (self.part[s, a, yy, xx, self.pc.c, :, hr].astype(F32)
                + self.l0[j, a, yy, xx, :, hr].astype(F32))

    def r1(self, j, s):
        p, hr = self.pc, self.hr()
        self.c0(j, s).wait()
        for a in range(2):
            self.sd[s, a, :, hr] = self.q(j, s, a, 1 - p.y, 1 - p.x).astype(BF)
        self.cdx(j, s).start()
        self.cdy(j, s).start()
        for a in range(2):
            self.sx[s, a, :, hr] = self.q(j, s, a, p.y, 1 - p.x).astype(BF)
            self.sy[s, a, :, hr] = self.q(j, s, a, 1 - p.y, p.x).astype(BF)
            self.so[s, a, :, hr] = self.q(j, s, a, p.y, p.x)

    def r2(self, j, s):
        hr = self.hr()
        lo, hi = pl.ds(0, 2), pl.ds(2, 2)
        self.cdx(j, s).wait()
        for a in range(2):
            self.sy[s, a, lo, hr] = (self.sy[s, a, lo, hr].astype(F32) + self.ldx[j, a, :, hr].astype(F32)).astype(BF)
        self.cy(j, s).start()
        self.cdy(j, s).wait()
        for a in range(2):
            self.sx[s, a, hi, hr] = (self.sx[s, a, hi, hr].astype(F32) + self.ldy[j, a, :, hr].astype(F32)).astype(BF)
        self.cx(j, s).start()

    def r3(self, j, s):
        hr = self.hr()
        self.cy(j, s).wait()
        self.cx(j, s).wait()
        for a in range(2):
            t = self.so[s, a, :, hr] + self.lx[j, a, :, hr].astype(F32) + self.ly[j, a, :, hr].astype(F32)
            self.so[s, a, :, hr] = t
            self.sz[s, a, :, hr] = t.astype(BF)
        for k in range(3):
            self.cz(j, s, k).start()

    def r4(self, j, s):
        hr = self.hr()
        for k in range(3):
            self.cz(j, s, k).wait()
        for a in range(2):
            t = self.so[s, a, self.pc.z, hr]
            for k in range(3):
                t = t + self.lz[j, k, a, hr].astype(F32)
            self.ob[s, a, hr] = t
        for o in self.out(j, s, self.ob, self.os):
            o.start()

    def drain(self, j, s):
        for o in self.out(j, s, self.ob, self.os):
            o.wait()


def scatter_scratch(n, h, w):
    return [
        pltpu.VMEM((2, 2, 2, 2, 2, 4, h, w), BF),
        pltpu.VMEM((n, 2, 2, 2, 4, h, w), BF),
        pltpu.VMEM((n, 2, 2, h, w), BF),
        pltpu.VMEM((n, 2, 2, h, w), BF),
        pltpu.VMEM((n, 2, 4, h, w), BF),
        pltpu.VMEM((n, 2, 4, h, w), BF),
        pltpu.VMEM((n, 3, 2, h, w), BF),
        pltpu.VMEM((2, 2, 4, h, w), BF),
        pltpu.VMEM((2, 2, 4, h, w), BF),
        pltpu.VMEM((2, 2, 4, h, w), BF),
        pltpu.VMEM((2, 2, 4, h, w), F32),
        pltpu.VMEM((2, 2, 4, h, w), BF),
        pltpu.VMEM((2, 2, h, w), F32),
        pltpu.SemaphoreType.DMA((n, 8)),
        pltpu.SemaphoreType.DMA((n, 8)),
        pltpu.SemaphoreType.DMA((2, 2)),
    ]


NSC = 16


def gather_kernel(units, nin, *refs):
    ins, outs = refs[:nin], refs[nin : 2 * nin]
    ss, rs = refs[2 * nin :]
    pc = Place()
    pc.greet()

    def make(u):
        a, (r0, rn), (c0, cn) = units[u]
        nd = len(ins[a].shape)
        mid = (slice(None),) * (nd - 3)
        tail = mid + (pl.ds(r0, rn), pl.ds(c0, cn))
        return Gather(pc, lambda: ins[a].at[(slice(None),) + tail],
                      lambda b, n: outs[a].at[(pl.ds(b, n),) + tail], ss.at[u], rs.at[u])

    us = [make(u) for u in range(len(units))]
    n, ahead = len(us), 4
    for t in range(-ahead, n + 4):
        if 0 <= t + ahead < n:
            us[t + ahead].s0()
        if 0 <= t < n:
            us[t].s1()
        if 0 <= t - 1 < n:
            us[t - 1].s2()
        if 0 <= t - 2 < n:
            us[t - 2].s3()
        if 0 <= t - 3 < n:
            us[t - 3].s4()
    for u in us:
        u.fin()


def gather_call(shards, units, cid):
    n = len(shards)
    sh = [s[None] for s in shards]
    return pl.pallas_call(
        functools.partial(gather_kernel, units, n),
        out_shape=[jax.ShapeDtypeStruct((32,) + s.shape, s.dtype) for s in shards],
        in_specs=[ANY] * n,
        out_specs=[ANY] * n,
        scratch_shapes=[pltpu.SemaphoreType.DMA((len(units), NG)), pltpu.SemaphoreType.DMA((len(units), NG))],
        name="gather_first",
        compiler_params=pltpu.CompilerParams(collective_id=cid, has_side_effects=True),
    )(*sh)


def ffn_kernel(ready, gu_ref, wgu_in, wd_ref, nf_ref, gf_ref, hid_ref,
               o_ref, gn_ref, ggate_ref, gup_ref, gdown_ref, wgu_ref,
               gw, uw, dw, act, gg, gu, nt, b3, insem, b3sem, hsem, gss, grs, *sc):
    pc = Place()
    f = gw.shape[-1]
    tok, dim = nf_ref.shape
    n = gu_ref.shape[-1] // f
    tm = td = 512
    pc.greet()

    def cols(j):
        return pl.ds(pl.multiple_of(j * f, f), f)

    def unit(j):
        return Gather(pc, lambda: gu_ref.at[:, :, :, cols(j)],
                      lambda b, m: wgu_ref.at[pl.ds(b, m), :, :, cols(j)], gss.at[j], grs.at[j])

    def out(j, s, ob, osem):
        return [pltpu.make_async_copy(ob.at[s, 0], ggate_ref.at[:, cols(j)], osem.at[s, 0]),
                pltpu.make_async_copy(ob.at[s, 1], gup_ref.at[:, cols(j)], osem.at[s, 1])]

    rs = Scatter(pc, sc, 32, out)
    part = sc[0]

    def fetch(j, s):
        return [pltpu.make_async_copy(wgu_ref.at[:, 0, :, cols(j)], gw.at[s], insem.at[s, 0]),
                pltpu.make_async_copy(wgu_ref.at[:, 1, :, cols(j)], uw.at[s], insem.at[s, 1]),
                pltpu.make_async_copy(wd_ref.at[cols(j), :], dw.at[s], insem.at[s, 2])]

    def put(j, s):
        return pltpu.make_async_copy(b3.at[s], gdown_ref.at[cols(j), :], b3sem.at[s])

    def on(cond, fn):
        pl.when(cond)(fn)

    hcopy = pltpu.make_async_copy(hid_ref, o_ref, hsem)
    hcopy.start()
    for c in fetch(0, 0):
        c.start()
    for j in range(ready, min(ready + 4, n)):
        unit(j).s0()
    gn_ref[...] = jnp.zeros_like(gn_ref)
    for i in range(4):
        nt[:, i * 256 : (i + 1) * 256] = nf_ref[i * 256 : (i + 1) * 256, :].T
    hcopy.wait()

    def body(j, carry):
        s = lax.rem(j, 2)

        def stage(fn, k, lo=0):
            @pl.when(jnp.logical_and(j + k >= lo, j + k < n))
            def _():
                fn(j + k)

        stage(lambda u: [c.wait() for c in fetch(u, s)], 0)

        def tile(i):
            r = pl.ds(i * tm, tm)
            x = nf_ref[r, :]
            g_w, u_w = gw[s].reshape(dim, f), uw[s].reshape(dim, f)
            g = dg(x, g_w, 1, 0)
            u = dg(x, u_w, 1, 0)
            ga = dg(gf_ref[r, :], dw[s], 1, 1)
            sg = jax.nn.sigmoid(g)
            si = g * sg
            a = (si * u).astype(BF)
            act[r, :] = a
            ggv = (ga * u * sg * (1.0 + g * (1.0 - sg))).astype(BF)
            guv = (ga * si).astype(BF)
            gg[r, :] = ggv
            gu[r, :] = guv
            o_ref[r, :] += dg(a, dw[s], 1, 0)
            gn_ref[r, :] += dg(ggv, g_w, 1, 1) + dg(guv, u_w, 1, 1)

        on(j < n, lambda: tile(0))
        stage(lambda u: rs.r2(u, 1 - s), -1)
        stage(lambda u: unit(u).s2(), 2, ready)
        on(j < n, lambda: tile(1))
        stage(lambda u: rs.r4(u, s), -2)
        stage(lambda u: unit(u).s1(), 3, ready + 1)
        stage(lambda u: unit(u).s0(), 4, ready + 4)

        @pl.when(j < n)
        def _():
            for i in range(dim // td):
                x = nt[i * td : (i + 1) * td, :]
                part[s, 0, i] = dg(x, gg[...], 1, 0).astype(BF).reshape(2, 2, 4, 32, f)
                part[s, 1, i] = dg(x, gu[...], 1, 0).astype(BF).reshape(2, 2, 4, 32, f)
            rs.r0(j, s)

        stage(lambda u: unit(u).s3(), 2, ready)
        stage(lambda u: unit(u).s4(), 1, ready)
        stage(lambda u: [c.start() for c in fetch(u, 1 - s)], 1)

        @pl.when(j < n)
        def _():
            on(j >= 2, lambda: put(j - 2, s).wait())
            for i in range(f // 256):
                b3[s, i * 256 : (i + 1) * 256, :] = dg(act[:, i * 256 : (i + 1) * 256].T, gf_ref[...], 1, 0).astype(BF)
            put(j, s).start()
            rs.r1(j, s)

        stage(lambda u: rs.r3(u, 1 - s), -1)
        stage(lambda u: rs.drain(u, s), -2)
        return carry

    unit(ready).s1()
    lax.fori_loop(0, n + 2, body, 0)
    for j in (n - 2, n - 1):
        put(j, j % 2).wait()

    def last(j, carry):
        unit(j).fin()
        return carry

    lax.fori_loop(ready, n, last, 0)


def ffn_call(ready, gu, wgu, wd, nf, gf, hid, cid):
    tok, dim = nf.shape
    ff = wd.shape[0]
    f = 512
    n = ff // f
    return pl.pallas_call(
        functools.partial(ffn_kernel, ready),
        out_shape=[
            jax.ShapeDtypeStruct((tok, dim), F32),
            jax.ShapeDtypeStruct((tok, dim), F32),
            jax.ShapeDtypeStruct((32, ff), F32),
            jax.ShapeDtypeStruct((32, ff), F32),
            jax.ShapeDtypeStruct((ff, dim), BF),
            jax.ShapeDtypeStruct(wgu.shape, BF),
        ],
        in_specs=[ANY, ANY, ANY, VM, VM, ANY],
        out_specs=[VM, VM, ANY, ANY, ANY, ANY],
        input_output_aliases={1: 5},
        scratch_shapes=[
            pltpu.VMEM((2, 32, 32, f), BF),
            pltpu.VMEM((2, 32, 32, f), BF),
            pltpu.VMEM((2, f, dim), BF),
            pltpu.VMEM((tok, f), BF),
            pltpu.VMEM((tok, f), BF),
            pltpu.VMEM((tok, f), BF),
            pltpu.VMEM((dim, tok), BF),
            pltpu.VMEM((2, f, dim), BF),
            pltpu.SemaphoreType.DMA((2, 3)),
            pltpu.SemaphoreType.DMA((2,)),
            pltpu.SemaphoreType.DMA,
            pltpu.SemaphoreType.DMA((n, NG)),
            pltpu.SemaphoreType.DMA((n, NG)),
        ] + scatter_scratch(n, 32, f),
        name="ffn",
        compiler_params=pltpu.CompilerParams(
            collective_id=cid, has_side_effects=True, vmem_limit_bytes=60 * 2**20
        ),
    )(gu, wgu, wd, nf, gf, hid)


def reduce_kernel(gd_ref, go_ref, gi_ref, sm_ref, od_ref, oo_ref, oi_ref, osm_ref, lsem, gss, grs, *sc):
    pc = Place()
    pc.greet()
    small = Gather(pc, lambda: sm_ref, lambda b, m: osm_ref.at[pl.ds(b, m)], gss, grs)
    small.s0()
    part = sc[0]
    units = [(gd_ref, od_ref, 48, 48 * i, 0) for i in range(3)] + [(go_ref, oo_ref, 32, 0, 0)]
    units += [(gi_ref, oi_ref, 32, 0, 1024 * i) for i in range(3)]
    n = len(units)

    def load(u):
        src, _, h, r0, c0 = units[u]
        s = u % 2
        return [pltpu.make_async_copy(src.at[:, :, :, :, pl.ds(r0, h), pl.ds(c0 + 512 * a, 512)],
                                      part.at[s, a, :, :, :, :, pl.ds(0, h)], lsem.at[s, a]) for a in range(2)]

    def eng(u):
        _, dst, h, r0, c0 = units[u]

        def out(j, s, ob, osem):
            return [pltpu.make_async_copy(ob.at[s, a, pl.ds(0, h)],
                                          dst.at[pl.ds(r0, h), pl.ds(c0 + 512 * a, 512)], osem.at[s, a]) for a in range(2)]

        return Scatter(pc, sc, h, out)

    es = [eng(u) for u in range(n)]
    for c in load(0):
        c.start()
    for t in range(n + 4):
        if t < n:
            for c in load(t):
                c.wait()
            es[t].r0(t, t % 2)
        if 0 <= t - 2 < n:
            es[t - 2].r2(t - 2, t % 2)
        if 0 <= t - 3 < n:
            es[t - 3].r4(t - 3, (t - 3) % 2)
        if 0 <= t - 1 < n:
            es[t - 1].r1(t - 1, (t - 1) % 2)
        if t + 1 < n:
            for c in load(t + 1):
                c.start()
        if 0 <= t - 2 < n:
            es[t - 2].r3(t - 2, t % 2)
        if 0 <= t - 3 < n:
            es[t - 3].drain(t - 3, (t - 3) % 2)
        if t == 1:
            small.s1()
        if t == 2:
            small.s2()
        if t == 3:
            small.s3()
    small.s4()
    small.fin()


def reduce_call(gd, go, gi, sm, cid):
    n = 7
    view = lambda a: a.reshape(2, 2, 2, 4, a.shape[0] // 32, a.shape[1])
    return pl.pallas_call(
        reduce_kernel,
        out_shape=[
            jax.ShapeDtypeStruct((gd.shape[0] // 32, gd.shape[1]), F32),
            jax.ShapeDtypeStruct((go.shape[0] // 32, go.shape[1]), F32),
            jax.ShapeDtypeStruct((gi.shape[0] // 32, gi.shape[1]), F32),
            jax.ShapeDtypeStruct((32,) + sm.shape, F32),
        ],
        in_specs=[ANY] * 4,
        out_specs=[ANY] * 4,
        scratch_shapes=[
            pltpu.SemaphoreType.DMA((2, 2)),
            pltpu.SemaphoreType.DMA((NG,)),
            pltpu.SemaphoreType.DMA((NG,)),
        ] + scatter_scratch(n, 48, 512),
        name="reduce_last",
        compiler_params=pltpu.CompilerParams(
            collective_id=cid, has_side_effects=True, vmem_limit_bytes=60 * 2**20
        ),
    )(view(gd), view(go), view(gi), sm[None])


def passed_along(array, axis, by):
    size = lax.axis_size(axis)
    pairs = [(i, i + by) for i in range(size) if 0 <= i + by < size]
    return lax.ppermute(array, axis, pairs)


def rms_forward(values, gain_vec):
    inv_rms = lax.rsqrt(jnp.mean(values * values, axis=1, keepdims=True) + epsilon)
    return (values * inv_rms * gain_vec[None, :], inv_rms)


def rms_backward(values, inv_rms, gain_vec, grad_normed):
    weighted = grad_normed * gain_vec[None, :]
    features = values.shape[1]
    total_dot = jnp.sum(weighted * values, axis=1, keepdims=True)
    grad_values = inv_rms * weighted - values * (inv_rms * inv_rms * inv_rms) * total_dot / features
    grad_gain = jnp.sum(grad_normed * values * inv_rms, axis=0)
    return (grad_values, grad_gain)


def outer_sum(left, right):
    return lax.dot_general(
        left, right, (((0,), (0,)), ((), ())), preferred_element_type=jnp.float32
    )


def back_product(grad_low, weight_mat):
    return lax.dot_general(
        grad_low, weight_mat, (((1,), (1,)), ((), ())), preferred_element_type=jnp.float32
    )


def doc_masks(doc_lengths, valid_count, first_pos, tok_count):
    packed_row = first_pos // ROW_LEN
    lengths = lax.dynamic_index_in_dim(doc_lengths, packed_row, 0, keepdims=False)
    limit_count = lax.dynamic_index_in_dim(valid_count, packed_row, 0, keepdims=False)
    offsets = jnp.cumsum(lengths) - lengths
    places = first_pos % ROW_LEN + jnp.arange(tok_count, dtype=jnp.int32)
    begins = jnp.any(offsets[None, :] == places[:, None], axis=1)
    before = jnp.any(offsets[None, :] == places[:, None] - 1, axis=1)
    keep_one = jnp.where(begins, 0.0, 1.0).astype(jnp.float32)
    keep_two = jnp.where(begins | before, 0.0, 1.0).astype(jnp.float32)
    live_mask = jnp.where(places < limit_count, 1.0, 0.0).astype(jnp.float32)
    return (keep_one[:, None], keep_two[:, None], live_mask[:, None])


def shards_plain(
    tokens,
    cotangent,
    gain_mix,
    in_weight,
    conv_taps,
    out_weight,
    gain_ffn,
    gate_weight,
    up_weight,
    down_weight,
    doc_lengths,
    valid_count,
):
    tok_count = tokens.shape[0]
    first_pos = lax.axis_index(("wide", "narrow")) * tok_count
    keep_one, keep_two, live_mask = doc_masks(doc_lengths, valid_count, first_pos, tok_count)
    full_gm, w_in, full_taps, w_out, full_gf, w_gate, w_up, w_down = (
        lax.all_gather(gain_mix, ("wide", "narrow"), axis=0, tiled=True),
        lax.all_gather(in_weight, ("wide", "narrow"), axis=0, tiled=True),
        lax.all_gather(conv_taps, ("wide", "narrow"), axis=1, tiled=True),
        lax.all_gather(out_weight, ("wide", "narrow"), axis=0, tiled=True),
        lax.all_gather(gain_ffn, ("wide", "narrow"), axis=0, tiled=True),
        lax.all_gather(gate_weight, ("wide", "narrow"), axis=0, tiled=True),
        lax.all_gather(up_weight, ("wide", "narrow"), axis=0, tiled=True),
        lax.all_gather(down_weight, ("wide", "narrow"), axis=0, tiled=True),
    )
    mix_gain = full_gm.astype(jnp.float32)
    ffn_gain = full_gf.astype(jnp.float32)
    taps = full_taps.astype(jnp.float32)
    features = tokens.shape[1]
    tok_float = tokens.astype(jnp.float32)
    normed_mix, inv_mix = rms_forward(tok_float, mix_gain)
    normed_low = normed_mix.astype(jnp.bfloat16)
    projected = jnp.dot(normed_low, w_in, preferred_element_type=jnp.float32)
    b_part = projected[:, :features]
    c_part = projected[:, features : 2 * features]
    x_part = projected[:, 2 * features :]
    gated = b_part * x_part
    edge_rows = passed_along(gated[-2:], "narrow", 1)
    extended = jnp.concatenate([edge_rows, gated], axis=0)
    lag_one = keep_one * extended[1:-1]
    lag_two = keep_two * extended[:-2]
    conv_out = taps[2][None, :] * gated + taps[1][None, :] * lag_one + taps[0][None, :] * lag_two
    mixed_low = (c_part * conv_out).astype(jnp.bfloat16)
    hidden_res = tok_float + jnp.dot(mixed_low, w_out, preferred_element_type=jnp.float32)
    normed_ffn, inv_ffn = rms_forward(hidden_res, ffn_gain)
    ffn_low = normed_ffn.astype(jnp.bfloat16)
    gate_val = jnp.dot(ffn_low, w_gate, preferred_element_type=jnp.float32)
    up_val = jnp.dot(ffn_low, w_up, preferred_element_type=jnp.float32)
    sigmoid_gate = jax.nn.sigmoid(gate_val)
    silu_val = gate_val * sigmoid_gate
    act_low = (silu_val * up_val).astype(jnp.bfloat16)
    ffn_out = jnp.dot(act_low, w_down, preferred_element_type=jnp.float32)
    output = live_mask * (hidden_res + ffn_out)
    again_gm, w_in, again_taps, w_out, again_gf, w_gate, w_up, w_down = (
        lax.all_gather(gain_mix, ("wide", "narrow"), axis=0, tiled=True),
        lax.all_gather(in_weight, ("wide", "narrow"), axis=0, tiled=True),
        lax.all_gather(conv_taps, ("wide", "narrow"), axis=1, tiled=True),
        lax.all_gather(out_weight, ("wide", "narrow"), axis=0, tiled=True),
        lax.all_gather(gain_ffn, ("wide", "narrow"), axis=0, tiled=True),
        lax.all_gather(gate_weight, ("wide", "narrow"), axis=0, tiled=True),
        lax.all_gather(up_weight, ("wide", "narrow"), axis=0, tiled=True),
        lax.all_gather(down_weight, ("wide", "narrow"), axis=0, tiled=True),
    )
    mix_gain = again_gm.astype(jnp.float32)
    ffn_gain = again_gf.astype(jnp.float32)
    taps = again_taps.astype(jnp.float32)
    grad_res = live_mask * cotangent.astype(jnp.float32)
    grad_ffn_low = grad_res.astype(jnp.bfloat16)
    grad_down = outer_sum(act_low, grad_ffn_low)
    grad_act = back_product(grad_ffn_low, w_down)
    grad_gate_low = (
        grad_act * up_val * sigmoid_gate * (1.0 + gate_val * (1.0 - sigmoid_gate))
    ).astype(jnp.bfloat16)
    grad_up_low = (grad_act * silu_val).astype(jnp.bfloat16)
    grad_gate = outer_sum(ffn_low, grad_gate_low)
    grad_up = outer_sum(ffn_low, grad_up_low)
    grad_nffn = back_product(grad_gate_low, w_gate) + back_product(grad_up_low, w_up)
    grad_hnorm, grad_gf = rms_backward(hidden_res, inv_ffn, ffn_gain, grad_nffn)
    grad_hidden = grad_res + grad_hnorm
    grad_mix_low = grad_hidden.astype(jnp.bfloat16)
    grad_out = outer_sum(mixed_low, grad_mix_low)
    grad_mixed = back_product(grad_mix_low, w_out)
    grad_c = grad_mixed * conv_out
    grad_conv = grad_mixed * c_part
    grad_taps = jnp.stack(
        [
            jnp.sum(grad_conv * lag_two, axis=0),
            jnp.sum(grad_conv * lag_one, axis=0),
            jnp.sum(grad_conv * gated, axis=0),
        ],
        axis=0,
    )
    lag_grad_one = taps[1][None, :] * keep_one * grad_conv
    lag_grad_two = taps[0][None, :] * keep_two * grad_conv
    grad_ext = (
        jnp.pad(taps[2][None, :] * grad_conv, ((2, 0), (0, 0)))
        + jnp.pad(lag_grad_one, ((1, 1), (0, 0)))
        + jnp.pad(lag_grad_two, ((0, 2), (0, 0)))
    )
    from_right = passed_along(grad_ext[:2], "narrow", -1)
    grad_gated = jnp.concatenate([grad_ext[2:-2], grad_ext[-2:] + from_right], axis=0)
    grad_b = grad_gated * x_part
    grad_x = grad_gated * b_part
    grad_proj_low = jnp.concatenate([grad_b, grad_c, grad_x], axis=1).astype(jnp.bfloat16)
    grad_in = outer_sum(normed_low, grad_proj_low)
    grad_nmix = back_product(grad_proj_low, w_in)
    grad_tnorm, grad_gm = rms_backward(tok_float, inv_mix, mix_gain, grad_nmix)
    grad_tokens = grad_hidden + grad_tnorm
    sum_gm, sum_in, sum_taps, sum_out, sum_gf, sum_gate, sum_up, sum_down = (
        lax.psum_scatter(grad_gm, ("wide", "narrow"), scatter_dimension=0, tiled=True),
        lax.psum_scatter(grad_in, ("wide", "narrow"), scatter_dimension=0, tiled=True),
        lax.psum_scatter(grad_taps, ("wide", "narrow"), scatter_dimension=1, tiled=True),
        lax.psum_scatter(grad_out, ("wide", "narrow"), scatter_dimension=0, tiled=True),
        lax.psum_scatter(grad_gf, ("wide", "narrow"), scatter_dimension=0, tiled=True),
        lax.psum_scatter(grad_gate, ("wide", "narrow"), scatter_dimension=0, tiled=True),
        lax.psum_scatter(grad_up, ("wide", "narrow"), scatter_dimension=0, tiled=True),
        lax.psum_scatter(grad_down, ("wide", "narrow"), scatter_dimension=0, tiled=True),
    )
    return (
        output,
        grad_tokens,
        sum_gm,
        sum_in,
        sum_taps,
        sum_out,
        sum_gf,
        sum_gate,
        sum_up,
        sum_down,
    )


def shards(
    tokens, cotangent, gain_mix, in_weight, conv_taps, out_weight, gain_ffn,
    gate_weight, up_weight, down_weight, doc_lengths, valid_count,
):
    tok_count, features = tokens.shape
    first_pos = lax.axis_index(("wide", "narrow")) * tok_count
    keep_one, keep_two, live_mask = doc_masks(doc_lengths, valid_count, first_pos, tok_count)
    own = gain_mix.shape[0]
    vecs = jnp.concatenate([gain_mix[None], gain_ffn[None], conv_taps], axis=0)
    vecs = jnp.pad(vecs, ((0, 11), (0, 128 - own)))
    gu_shard = jnp.stack([gate_weight, up_weight])
    units = [(4, (0, 16), (0, 128))]
    units += [(0, (0, 32), (1024 * i, 1024)) for i in range(3)] + [(1, (0, 32), (0, 1024))]
    units += [(2, (0, 32), (0, 1024)), (2, (32, 32), (0, 1024)), (2, (64, 32), (0, 1024)), (2, (96, 48), (0, 1024))]
    units += [(3, (0, 32), (512 * i, 512)) for i in range(2)]
    w_in, w_out, w_down, w_gu, all_vecs = gather_call(
        [in_weight, out_weight, down_weight, gu_shard, vecs], units, 1
    )
    w_in = w_in.reshape(features, -1)
    w_out = w_out.reshape(features, features)
    w_down = w_down.reshape(-1, features)
    vec = all_vecs[:, :5, :own].transpose(1, 0, 2).reshape(5, features).astype(F32)
    mix_gain, ffn_gain, taps = vec[0], vec[1], vec[2:]
    tok_float = tokens.astype(F32)
    normed_mix, inv_mix = rms_forward(tok_float, mix_gain)
    normed_low = normed_mix.astype(BF)
    projected = jnp.dot(normed_low, w_in, preferred_element_type=F32)
    b_part = projected[:, :features]
    c_part = projected[:, features : 2 * features]
    x_part = projected[:, 2 * features :]
    gated = b_part * x_part
    edge_rows = passed_along(gated[-2:], "narrow", 1)
    extended = jnp.concatenate([edge_rows, gated], axis=0)
    lag_one = keep_one * extended[1:-1]
    lag_two = keep_two * extended[:-2]
    conv_out = taps[2][None, :] * gated + taps[1][None, :] * lag_one + taps[0][None, :] * lag_two
    mixed_low = (c_part * conv_out).astype(BF)
    hidden_res = tok_float + jnp.dot(mixed_low, w_out, preferred_element_type=F32)
    normed_ffn, inv_ffn = rms_forward(hidden_res, ffn_gain)
    ffn_low = normed_ffn.astype(BF)
    grad_res = live_mask * cotangent.astype(F32)
    grad_ffn_low = grad_res.astype(BF)
    summed, grad_nffn, sum_gate, sum_up, grad_down, _ = ffn_call(
        2, gu_shard[None], w_gu, w_down, ffn_low, grad_ffn_low, hidden_res, 2
    )
    output = live_mask * summed
    grad_hnorm, grad_gf = rms_backward(hidden_res, inv_ffn, ffn_gain, grad_nffn)
    grad_hidden = grad_res + grad_hnorm
    grad_mix_low = grad_hidden.astype(BF)
    grad_out = outer_sum(mixed_low, grad_mix_low).astype(BF)
    grad_mixed = back_product(grad_mix_low, w_out)
    grad_c = grad_mixed * conv_out
    grad_conv = grad_mixed * c_part
    grad_taps = [
        jnp.sum(grad_conv * lag_two, axis=0),
        jnp.sum(grad_conv * lag_one, axis=0),
        jnp.sum(grad_conv * gated, axis=0),
    ]
    lag_grad_one = taps[1][None, :] * keep_one * grad_conv
    lag_grad_two = taps[0][None, :] * keep_two * grad_conv
    grad_ext = (
        jnp.pad(taps[2][None, :] * grad_conv, ((2, 0), (0, 0)))
        + jnp.pad(lag_grad_one, ((1, 1), (0, 0)))
        + jnp.pad(lag_grad_two, ((0, 2), (0, 0)))
    )
    from_right = passed_along(grad_ext[:2], "narrow", -1)
    grad_gated = jnp.concatenate([grad_ext[2:-2], grad_ext[-2:] + from_right], axis=0)
    grad_b = grad_gated * x_part
    grad_x = grad_gated * b_part
    grad_proj_low = jnp.concatenate([grad_b, grad_c, grad_x], axis=1).astype(BF)
    grad_in = outer_sum(normed_low, grad_proj_low).astype(BF)
    grad_nmix = back_product(grad_proj_low, w_in)
    grad_tnorm, grad_gm = rms_backward(tok_float, inv_mix, mix_gain, grad_nmix)
    grad_tokens = grad_hidden + grad_tnorm
    zero = jnp.zeros_like(grad_gm)
    small = jnp.stack([grad_gm, grad_gf] + grad_taps + [zero] * 3)
    sum_down, sum_out, sum_in, all_small = reduce_call(grad_down, grad_out, grad_in, small, 3)
    mine = lax.dynamic_slice_in_dim(jnp.sum(all_small, axis=0), lax.axis_index(("wide", "narrow")) * own, own, 1)
    return (output, grad_tokens, mine[0], sum_in, mine[2:5], sum_out, mine[1], sum_gate, sum_up, sum_down)


def solution(mesh):
    both = ("wide", "narrow")
    rows, vec, flat = P(both, None), P(both), P(None, both)
    step = shards if (mesh.shape["wide"], mesh.shape["narrow"]) == (8, 4) else shards_plain
    return jax.shard_map(
        step,
        mesh=mesh,
        in_specs=(rows, rows, vec, rows, flat, rows, vec, rows, rows, rows, P(), P()),
        out_specs=(rows, rows, vec, rows, flat, rows, vec, rows, rows, rows),
        check_vma=False,
    )
```

```python
import functools

import jax
import jax.numpy as jnp
from jax import lax
from jax.experimental import pallas as pl
from jax.experimental.pallas import tpu as pltpu
from jax.sharding import PartitionSpec as P

ROW_LEN = 4096
epsilon = 1e-05
F32 = jnp.float32
BF = jnp.bfloat16
MESH = pl.DeviceIdType.MESH
ANY = pl.BlockSpec(memory_space=pl.ANY)
VM = pl.BlockSpec(memory_space=pltpu.VMEM)


def dg(a, b, ca, cb):
    return lax.dot_general(a, b, (((ca,), (cb,)), ((), ())), preferred_element_type=F32)


class Place:
    def __init__(self):
        w = lax.axis_index("wide")
        z = lax.axis_index("narrow")
        c = lax.rem(w, 2)
        x = lax.rem(w // 2, 2)
        y = w // 4
        self.w, self.z, self.c, self.x, self.y = w, z, c, x, y
        self.core = (w + 1 - 2 * c, z)
        self.xn = (w + 2 - 4 * x, z)
        self.yn = (w + 4 - 8 * y, z)
        self.zs = [(w, lax.rem(z + k, 4)) for k in (1, 2, 3)]
        self.zto = [lax.rem(z + k, 4) for k in (1, 2, 3)]
        self.zfrom = [lax.rem(z + 4 - k, 4) for k in (1, 2, 3)]

        def base(yy, xx, cc):
            return 16 * yy + 8 * xx + 4 * cc

        self.own, self.xb = base(y, x, c), base(y, 1 - x, c)
        self.yb, self.db = base(1 - y, x, c), base(1 - y, 1 - x, c)
        self.sown, self.sxb = base(y, x, 1 - c), base(y, 1 - x, 1 - c)
        self.syb, self.sdb = base(1 - y, x, 1 - c), base(1 - y, 1 - x, 1 - c)
        self.me = self.own + z

    def greet(self):
        bar = pltpu.get_barrier_semaphore()
        peers = [self.core, self.xn, self.yn] + self.zs
        for p in peers:
            pl.semaphore_signal(bar, inc=1, device_id=p, device_id_type=MESH)
        pl.semaphore_wait(bar, len(peers))


def remote(src, dst, ss, rs, dev):
    return pltpu.make_async_remote_copy(
        src_ref=src, dst_ref=dst, send_sem=ss, recv_sem=rs, device_id=dev, device_id_type=MESH
    )


class Gather:
    def __init__(self, pc, src, dst, full, ss, rs):
        self.pc, self.src, self.dst, self.full, self.ss, self.rs = pc, src, dst, full, ss, rs
        self.parts = range(len(src))

    def zc(self, i, k):
        q = 3 * i + k
        return remote(self.src[i](), self.dst[i](self.pc.me, 1), self.ss.at[q], self.rs.at[q], self.pc.zs[k])

    def zr(self, i, k):
        q = 3 * i + k
        v = self.dst[i](self.pc.own + self.pc.zfrom[k], 1)
        return remote(v, v, self.ss.at[q], self.rs.at[q], self.pc.zs[k])

    def loc(self, i):
        return pltpu.make_async_copy(self.src[i](), self.dst[i](self.pc.me, 1), self.ss.at[14 + i])

    def cp(self, k, b, n, dev):
        v = self.full(b, n)
        return remote(v, v, self.ss.at[k], self.rs.at[k], dev)

    def s0(self):
        for i in self.parts:
            self.loc(i).start()
            for k in range(3):
                self.zc(i, k).start()

    def s1(self):
        p = self.pc
        for i in self.parts:
            self.loc(i).wait()
            for k in range(3):
                self.zr(i, k).wait_recv()
        self.cp(6, p.own, 4, p.xn).start()
        self.cp(7, p.own, 4, p.yn).start()
        self.cp(8, p.own, 4, p.core).start()

    def s2(self):
        p = self.pc
        self.cp(6, p.xb, 4, p.xn).wait_recv()
        self.cp(9, p.xb, 2, p.yn).start()
        self.cp(10, p.xb, 4, p.core).start()
        self.cp(7, p.yb, 4, p.yn).wait_recv()
        self.cp(11, p.yb + 2, 2, p.xn).start()
        self.cp(12, p.yb, 4, p.core).start()

    def s3(self):
        p = self.pc
        self.cp(9, p.db, 2, p.yn).wait_recv()
        self.cp(11, p.db + 2, 2, p.xn).wait_recv()
        self.cp(13, p.db, 4, p.core).start()

    def s4(self):
        p = self.pc
        for k, b in ((8, p.sown), (10, p.sxb), (12, p.syb), (13, p.sdb)):
            self.cp(k, b, 4, p.core).wait_recv()

    def fin(self):
        p = self.pc
        for i in self.parts:
            for k in range(3):
                self.zc(i, k).wait_send()
        for k, b, n in (
            (6, p.own, 4), (7, p.own, 4), (8, p.own, 4), (9, p.xb, 2),
            (10, p.xb, 4), (11, p.yb + 2, 2), (12, p.yb, 4), (13, p.db, 4),
        ):
            self.cp(k, b, n, p.core).wait_send()


NG = 16
NL = 4


class Scatter:
    def __init__(self, pc, bufs, h, out):
        self.pc, self.h, self.out = pc, h, out
        (self.part, self.l0, self.ldx, self.ldy, self.lx, self.ly, self.lz,
         self.sd, self.sx, self.sy, self.so, self.sz, self.ob, self.ss, self.rs, self.os) = bufs

    def hr(self):
        return pl.ds(0, self.h)

    def c0(self, j, s):
        p = self.pc
        return remote(self.part.at[s, :, :, :, 1 - p.c, :, self.hr()], self.l0.at[lax.rem(j, NL), :, :, :, :, self.hr()],
                      self.ss.at[j, 0], self.rs.at[j, 0], p.core)

    def cdx(self, j, s):
        return remote(self.sd.at[s, :, pl.ds(0, 2), self.hr()], self.ldx.at[lax.rem(j, NL), :, :, self.hr()],
                      self.ss.at[j, 1], self.rs.at[j, 1], self.pc.xn)

    def cdy(self, j, s):
        return remote(self.sd.at[s, :, pl.ds(2, 2), self.hr()], self.ldy.at[lax.rem(j, NL), :, :, self.hr()],
                      self.ss.at[j, 2], self.rs.at[j, 2], self.pc.yn)

    def cx(self, j, s):
        return remote(self.sx.at[s, :, :, self.hr()], self.lx.at[lax.rem(j, NL), :, :, self.hr()],
                      self.ss.at[j, 3], self.rs.at[j, 3], self.pc.xn)

    def cy(self, j, s):
        return remote(self.sy.at[s, :, :, self.hr()], self.ly.at[lax.rem(j, NL), :, :, self.hr()],
                      self.ss.at[j, 4], self.rs.at[j, 4], self.pc.yn)

    def cz(self, j, s, k):
        return remote(self.sz.at[s, :, self.pc.zto[k], self.hr()], self.lz.at[lax.rem(j, NL), k, :, self.hr()],
                      self.ss.at[j, 5 + k], self.rs.at[j, 5 + k], self.pc.zs[k])

    def r0(self, j, s):
        self.c0(j, s).start()

    def q(self, j, s, a, yy, xx):
        hr = self.hr()
        return (self.part[s, a, yy, xx, self.pc.c, :, hr].astype(F32)
                + self.l0[lax.rem(j, NL), a, yy, xx, :, hr].astype(F32))

    def r1(self, j, s):
        p, hr = self.pc, self.hr()
        self.c0(j, s).wait()
        for a in range(2):
            self.sd[s, a, :, hr] = self.q(j, s, a, 1 - p.y, 1 - p.x).astype(BF)
        self.cdx(j, s).start()
        self.cdy(j, s).start()
        for a in range(2):
            self.sx[s, a, :, hr] = self.q(j, s, a, p.y, 1 - p.x).astype(BF)
            self.sy[s, a, :, hr] = self.q(j, s, a, 1 - p.y, p.x).astype(BF)
            self.so[s, a, :, hr] = self.q(j, s, a, p.y, p.x)

    def r2(self, j, s):
        hr = self.hr()
        lo, hi = pl.ds(0, 2), pl.ds(2, 2)
        self.cdx(j, s).wait()
        for a in range(2):
            self.sy[s, a, lo, hr] = (self.sy[s, a, lo, hr].astype(F32) + self.ldx[lax.rem(j, NL), a, :, hr].astype(F32)).astype(BF)
        self.cy(j, s).start()
        self.cdy(j, s).wait()
        for a in range(2):
            self.sx[s, a, hi, hr] = (self.sx[s, a, hi, hr].astype(F32) + self.ldy[lax.rem(j, NL), a, :, hr].astype(F32)).astype(BF)
        self.cx(j, s).start()

    def r3(self, j, s):
        hr = self.hr()
        self.cy(j, s).wait()
        self.cx(j, s).wait()
        for a in range(2):
            t = self.so[s, a, :, hr] + self.lx[lax.rem(j, NL), a, :, hr].astype(F32) + self.ly[lax.rem(j, NL), a, :, hr].astype(F32)
            self.so[s, a, :, hr] = t
            self.sz[s, a, :, hr] = t.astype(BF)
        for k in range(3):
            self.cz(j, s, k).start()

    def r4(self, j, s):
        hr = self.hr()
        for k in range(3):
            self.cz(j, s, k).wait()
        for a in range(2):
            t = self.so[s, a, self.pc.z, hr]
            for k in range(3):
                t = t + self.lz[lax.rem(j, NL), k, a, hr].astype(F32)
            self.ob[s, a, hr] = t
        self.out(j, s, self.ob, self.os, "start")

    def drain(self, j, s):
        self.out(j, s, self.ob, self.os, "wait")


def scatter_scratch(n, h, w):
    return [
        pltpu.VMEM((2, 2, 2, 2, 2, 4, h, w), BF),
        pltpu.VMEM((NL, 2, 2, 2, 4, h, w), BF),
        pltpu.VMEM((NL, 2, 2, h, w), BF),
        pltpu.VMEM((NL, 2, 2, h, w), BF),
        pltpu.VMEM((NL, 2, 4, h, w), BF),
        pltpu.VMEM((NL, 2, 4, h, w), BF),
        pltpu.VMEM((NL, 3, 2, h, w), BF),
        pltpu.VMEM((2, 2, 4, h, w), BF),
        pltpu.VMEM((2, 2, 4, h, w), BF),
        pltpu.VMEM((2, 2, 4, h, w), BF),
        pltpu.VMEM((2, 2, 4, h, w), F32),
        pltpu.VMEM((2, 2, 4, h, w), BF),
        pltpu.VMEM((2, 2, h, w), F32),
        pltpu.SemaphoreType.DMA((n, 8)),
        pltpu.SemaphoreType.DMA((n, 8)),
        pltpu.SemaphoreType.DMA((2, 2)),
    ]


def inverse_rms(v):
    return lax.rsqrt(jnp.mean(v * v, axis=1, keepdims=True) + epsilon)


def block_kernel(
    tok_ref, cot_ref, msk_ref, vec_ref, win_s, wout_s, wgate_s, wup_s, wdown_s,
    out_ref, gtok_ref, ggate_o, gup_o, gdown_o, gout_o, gin_o, small_o,
    win_h, wout_h, wd_h, wgu_h, vec_h, bcx_h, hid_h, mix_h, gdown_h,
    obuf, gn, nf, gf, nm, vec, sm, halo_t, halo_g, edge_s, edge_r,
    vsem, lsem, hsem, gss, grs, *sc,
):
    pc = Place()
    tok, dim = tok_ref.shape
    ff = wgate_s.shape[-1]
    f = 512
    n = ff // f
    tt = 256
    nt_ = tok // tt
    part = sc[0]

    def cols(j, w=f):
        return pl.ds(pl.multiple_of(j * w, w), w)

    def simple(u, src, dst, c0, w):
        at = lambda b, m: dst.at[pl.ds(b, m), :, pl.ds(c0, w)]
        return Gather(pc, [lambda: src.at[:, :, pl.ds(c0, w)]], [at], at, gss.at[u], grs.at[u])

    def down_unit(i):
        rows = ff // 32
        at = lambda b, m: wd_h.at[pl.ds(pl.multiple_of(b * rows, rows), m * rows), pl.ds(256 * i, 256)]
        return Gather(pc, [lambda: wdown_s.at[:, pl.ds(256 * i, 256)]], [at], at, gss.at[5 + i], grs.at[5 + i])

    def gu_unit(j):
        srcs = [lambda: wgate_s.at[:, :, cols(j)], lambda: wup_s.at[:, :, cols(j)]]
        dsts = [lambda b, m: wgu_h.at[pl.ds(b, m), 0, :, cols(j)], lambda b, m: wgu_h.at[pl.ds(b, m), 1, :, cols(j)]]
        return Gather(pc, srcs, dsts, lambda b, m: wgu_h.at[pl.ds(b, m), :, :, cols(j)], gss.at[9 + j], grs.at[9 + j])

    def unit(u):
        if u == 0:
            return simple(0, vec_ref, vec_h, 0, 128)
        if u < 4:
            return simple(u, win_s, win_h, 1024 * (u - 1), 1024)
        if u == 4:
            return simple(4, wout_s, wout_h, 0, 1024)
        if u < 9:
            return down_unit(u - 5)
        return gu_unit(u - 9)

    small = Gather(pc, [lambda: sm], [lambda b, m: small_o.at[pl.ds(b, m)]], lambda b, m: small_o.at[pl.ds(b, m)],
                   gss.at[9 + n], grs.at[9 + n])

    def step(t):
        if t + 4 < 9 + n:
            unit(t + 4).s0()
        unit(t).s1()
        if t >= 1:
            unit(t - 1).s2()
        if t >= 2:
            unit(t - 2).s3()
        if t >= 3:
            unit(t - 3).s4()

    ndn = n + 4
    gdown6 = gdown_h.reshape(2, 2, 2, 4, ff // 32, dim)

    def act_on(copies, what):
        for c in copies:
            getattr(c, what)()

    def out_gu(j, s, ob, osem, what):
        act_on([pltpu.make_async_copy(ob.at[s, 0], ggate_o.at[:, cols(j)], osem.at[s, 0]),
                pltpu.make_async_copy(ob.at[s, 1], gup_o.at[:, cols(j)], osem.at[s, 1])], what)

    def out_rows(dst, r0, c0, h):
        def go(j, s, ob, osem, what):
            act_on([pltpu.make_async_copy(ob.at[s, a, pl.ds(0, h)],
                                          dst.at[pl.ds(r0, h), pl.ds(c0 + 512 * a, 512)], osem.at[s, a])
                    for a in range(2)], what)
        return go

    def out_down(j, s, ob, osem, what):
        out_rows(gdown_o, pl.multiple_of((j - n) * 32, 32), 0, 32)(j, s, ob, osem, what)

    def out_mixed(j, s, ob, osem, what):
        pl.when(j < n)(lambda: out_gu(j, s, ob, osem, what))
        pl.when(j >= n)(lambda: out_down(j, s, ob, osem, what))

    eng_gu = Scatter(pc, sc, 32, out_gu)
    eng_mid = Scatter(pc, sc, 32, out_mixed)
    order = (1, 0, 2)

    def eng(u):
        if u < ndn:
            return Scatter(pc, sc, 32, out_down)
        if u == ndn:
            return Scatter(pc, sc, 16, out_rows(gdown_o, 128, 0, 16))
        if u == ndn + 1:
            return Scatter(pc, sc, 32, out_rows(gout_o, 0, 0, 32))
        return Scatter(pc, sc, 32, out_rows(gin_o, 0, 1024 * order[u - ndn - 2], 32))

    pc.greet()
    cot_copy = pltpu.make_async_copy(cot_ref, gf, hsem.at[0])
    cot_copy.start()
    for u in range(5):
        unit(u).s0()
    tail = remote(tok_ref.at[pl.ds(tok - 16, 16)], halo_t, hsem.at[1], hsem.at[2], pc.zs[0])
    tail.start()
    sm[...] = jnp.zeros_like(sm)
    edge_s[...] = jnp.zeros_like(edge_s)
    gn[...] = jnp.zeros_like(gn)
    cot_copy.wait()

    def live_rows(i, _):
        r = cols(i, tt)
        gf[r, :] = (gf[r, :].astype(F32) * msk_ref[r, 2:3]).astype(BF)
        return 0

    lax.fori_loop(0, nt_, live_rows, 0)
    unit(0).s1()
    unit(1).s1()
    unit(0).s2()
    unit(2).s1()
    unit(0).s3()
    unit(1).s2()
    unit(0).s4()

    def mixer_forward(vbuf, win, wout, st, mst, tb):
        vcopy = pltpu.make_async_copy(vec_h, vbuf, vsem.at[0])
        vcopy.start()
        for u in (5, 6, 7):
            unit(u).s0()
        vcopy.wait()
        for q in range(8):
            v = vbuf[4 * q].astype(F32)
            for k in range(1, 4):
                v = v + vbuf[4 * q + k].astype(F32)
            vec[:, 128 * q : 128 * q + 128] = v
        gain = vec[0:1, :]

        def normed(i, _):
            r = cols(i, tt)
            t = tok_ref[r, :].astype(F32)
            nm[r, :] = (t * inverse_rms(t) * gain).astype(BF)
            return 0

        lax.fori_loop(0, nt_, normed, 0)
        unit(3).s1()
        unit(2).s2()
        unit(1).s3()
        wl = [pltpu.make_async_copy(win_h.at[:, :, pl.ds(1024 * i, 1024)], win.at[i], vsem.at[i]) for i in range(3)]
        wl.append(pltpu.make_async_copy(wout_h, wout, vsem.at[3]))
        for t in (4, 5, 6, 7):
            step(t)
            wl[t - 4].start()
        tail.wait()
        th = halo_t[...].astype(F32)
        nh = (th * inverse_rms(th) * gain).astype(BF)
        for c in wl:
            c.wait()
        hb = dg(nh, win[0].reshape(dim, dim), 1, 0) * dg(nh, win[2].reshape(dim, dim), 1, 0)
        halo_g[...] = hb[8:16, :]
        tb[0:8, :] = halo_g[...]

        def stash(i, s):
            r = cols(i, tt)
            return [pltpu.make_async_copy(st.at[s, k], bcx_h.at[k, r], lsem.at[s, k]) for k in range(3)] + [
                pltpu.make_async_copy(mst.at[s], mix_h.at[r], lsem.at[s, 3]),
                pltpu.make_async_copy(obuf.at[r], hid_h.at[r], lsem.at[s, 4])]

        def tile(i, _):
            r = cols(i, tt)
            s = lax.rem(i, 2)
            pl.when(i >= 2)(lambda: act_on(stash(i - 2, s), "wait"))
            x = nm[r, :]
            bv = dg(x, win[0].reshape(dim, dim), 1, 0)
            st[s, 0] = bv
            xv = dg(x, win[2].reshape(dim, dim), 1, 0)
            st[s, 2] = xv
            tb[8 : 8 + tt, :] = bv * xv
            cv = dg(x, win[1].reshape(dim, dim), 1, 0)
            st[s, 1] = cv
            k1, k2 = msk_ref[r, 0:1], msk_ref[r, 1:2]
            conv = (vec[4:5, :] * tb[8 : 8 + tt, :] + vec[3:4, :] * (k1 * tb[7 : 7 + tt, :])
                    + vec[2:3, :] * (k2 * tb[6 : 6 + tt, :]))
            mixed = (cv * conv).astype(BF)
            mst[s] = mixed
            tb[0:8, :] = tb[tt : tt + 8, :]
            h = tok_ref[r, :].astype(F32) + dg(mixed, wout[...].reshape(dim, dim), 1, 0)
            obuf[r, :] = h
            nf[r, :] = (h * inverse_rms(h) * vec[1:2, :]).astype(BF)
            act_on(stash(i, s), "start")
            for k in range(4):
                pl.when(i == k)(functools.partial(step, 8 + k))
            return 0

        lax.fori_loop(0, nt_, tile, 0)
        for i in (nt_ - 2, nt_ - 1):
            act_on(stash(i, i % 2), "wait")

    pl.run_scoped(
        mixer_forward, pltpu.VMEM((32, 16, 128), BF), pltpu.VMEM((3, 32, 32, dim), BF), pltpu.VMEM((32, 32, dim), BF),
        pltpu.VMEM((2, 3, tt, dim), F32), pltpu.VMEM((2, tt, dim), BF), pltpu.VMEM((tt + 8, dim), F32),
    )
    step(12)

    def put(b3, j, s):
        return pltpu.make_async_copy(b3.at[s], gdown_h.at[cols(j), :], vsem.at[s])

    def ffn(gw, uw, dw, act, gg, gu, nt, b3):
        tm = td = 512

        def fetch(j, s):
            return [pltpu.make_async_copy(wgu_h.at[:, 0, :, cols(j)], gw.at[s], lsem.at[s, 0]),
                    pltpu.make_async_copy(wgu_h.at[:, 1, :, cols(j)], uw.at[s], lsem.at[s, 1]),
                    pltpu.make_async_copy(wd_h.at[cols(j), :], dw.at[s], lsem.at[s, 2])]

        act_on(fetch(0, 0), "start")

        def turned(i, _):
            nt[:, cols(i, tt)] = nf[cols(i, tt), :].T
            return 0

        lax.fori_loop(0, nt_, turned, 0)

        def body(j, carry):
            s = lax.rem(j, 2)

            def stage(fn, k, lo=0):
                pl.when(jnp.logical_and(j + k >= lo, j + k < n))(lambda: fn(j + k))

            act_on(fetch(j, s), "wait")

            def tile(i):
                r = pl.ds(i * tm, tm)
                x = nf[r, :]
                g_w, u_w = gw[s].reshape(dim, f), uw[s].reshape(dim, f)
                g = dg(x, g_w, 1, 0)
                u = dg(x, u_w, 1, 0)
                ga = dg(gf[r, :], dw[s], 1, 1)
                sg = jax.nn.sigmoid(g)
                si = g * sg
                a = (si * u).astype(BF)
                act[r, :] = a
                ggv = (ga * u * sg * (1.0 + g * (1.0 - sg))).astype(BF)
                guv = (ga * si).astype(BF)
                gg[r, :] = ggv
                gu[r, :] = guv
                obuf[r, :] += dg(a, dw[s], 1, 0)
                gn[r, :] += dg(ggv, g_w, 1, 1) + dg(guv, u_w, 1, 1)

            tile(0)
            stage(lambda u: eng_gu.r2(u, 1 - s), -1)
            stage(lambda u: gu_unit(u).s2(), 2, 3)
            tile(1)
            stage(lambda u: eng_gu.r4(u, s), -2)
            stage(lambda u: gu_unit(u).s1(), 3, 4)
            stage(lambda u: gu_unit(u).s0(), 8, 8)
            for i in range(dim // td):
                x = nt[i * td : (i + 1) * td, :]
                part[s, 0, i] = dg(x, gg[...], 1, 0).astype(BF).reshape(2, 2, 4, 32, f)
                part[s, 1, i] = dg(x, gu[...], 1, 0).astype(BF).reshape(2, 2, 4, 32, f)
            eng_gu.r0(j, s)
            stage(lambda u: gu_unit(u).s3(), 2, 2)
            stage(lambda u: gu_unit(u).s4(), 1, 1)
            stage(lambda u: act_on(fetch(u, 1 - s), "start"), 1)
            pl.when(j >= 2)(lambda: put(b3, j - 2, s).wait())
            for i in range(f // 256):
                b3[s, i * 256 : (i + 1) * 256, :] = dg(act[:, i * 256 : (i + 1) * 256].T, gf[...], 1, 0).astype(BF)
            put(b3, j, s).start()
            eng_gu.r1(j, s)
            stage(lambda u: eng_gu.r3(u, 1 - s), -1)
            stage(lambda u: eng_gu.drain(u, s), -2)
            return carry

        lax.fori_loop(0, n, body, 0)
        for j in (n - 2, n - 1):
            put(b3, j, j % 2).wait()

    pl.run_scoped(
        ffn, pltpu.VMEM((2, 32, 32, f), BF), pltpu.VMEM((2, 32, 32, f), BF), pltpu.VMEM((2, f, dim), BF),
        pltpu.VMEM((tok, f), BF), pltpu.VMEM((tok, f), BF), pltpu.VMEM((tok, f), BF),
        pltpu.VMEM((dim, tok), BF), pltpu.VMEM((2, f, dim), BF),
    )

    def load_down(u, r0, h):
        s = lax.rem(u, 2)
        return [pltpu.make_async_copy(gdown6.at[:, :, :, :, pl.ds(r0, h), pl.ds(512 * a, 512)],
                                      part.at[s, a, :, :, :, :, pl.ds(0, h)], vsem.at[2 + a]) for a in range(2)]

    def load_mid(u):
        return load_down(u, pl.multiple_of((u - n) * 32, 32), 32)

    def mixer_backward(gp, turn, wout):
        wcopy = pltpu.make_async_copy(wout_h, wout, vsem.at[0])
        wcopy.start()
        act_on(load_mid(n), "start")

        def turned(i, _):
            turn[:, cols(i, tt)] = nm[cols(i, tt), :].T
            return 0

        lax.fori_loop(0, nt_, turned, 0)
        mcopy = pltpu.make_async_copy(mix_h, nm, vsem.at[1])
        mcopy.start()
        wcopy.wait()

        def grad_in(k, s):
            for i in range(2):
                for a in range(2):
                    t = dg(turn[512 * i : 512 * i + 512, :], gp[:, 1024 * k + 512 * a : 1024 * k + 512 * a + 512], 1, 0)
                    part[s, a, i] = t.astype(BF).reshape(2, 2, 4, 32, 512)

        def passes(ld, ost, tb):
            def fetch(i, s):
                r = cols(i, tt)
                return [pltpu.make_async_copy(bcx_h.at[k, r], ld.at[s, k], lsem.at[s, k]) for k in range(3)] + [
                    pltpu.make_async_copy(hid_h.at[r], ld.at[s, 3], lsem.at[s, 3])]

            def put_out(i):
                return pltpu.make_async_copy(ost, out_ref.at[cols(i, tt)], lsem.at[0, 4])

            act_on(fetch(0, 0), "start")
            tb[0:8, :] = halo_g[...]

            def one(i, _):
                u = n + i
                su = lax.rem(u, 2)
                s = lax.rem(i, 2)
                r = cols(i, tt)
                act_on(load_mid(u), "wait")
                eng_mid.r0(u, su)
                pl.when(i + 1 < nt_)(lambda: act_on(load_mid(u + 1), "start"))
                pl.when(i + 1 < nt_)(lambda: act_on(fetch(i + 1, 1 - s), "start"))
                eng_mid.r2(u - 1, 1 - su)
                act_on(fetch(i, s), "wait")
                pl.when(i >= 1)(lambda: put_out(i - 1).wait())
                ost[...] = obuf[r, :] * msk_ref[r, 2:3]
                put_out(i).start()
                v = ld[s, 3]
                g = gn[r, :]
                inv = inverse_rms(v)
                a = g * vec[1:2, :]
                dot = jnp.sum(a * v, axis=1, keepdims=True) / dim
                ghid = gf[r, :].astype(F32) + (inv * a - v * (inv * inv * inv) * dot)
                sm[0, 1:2, :] += jnp.sum(g * v * inv, axis=0, keepdims=True)
                gn[r, :] = ghid
                low = ghid.astype(BF)
                nf[r, :] = low
                gm = dg(low, wout[...].reshape(dim, dim), 1, 1)
                tb[8 : 8 + tt, :] = ld[s, 0] * ld[s, 2]
                k1, k2 = msk_ref[r, 0:1], msk_ref[r, 1:2]
                gated, lag1, lag2 = tb[8 : 8 + tt, :], k1 * tb[7 : 7 + tt, :], k2 * tb[6 : 6 + tt, :]
                conv = vec[4:5, :] * gated + vec[3:4, :] * lag1 + vec[2:3, :] * lag2
                gp[r, 1024:2048] = (gm * conv).astype(BF)
                gc = gm * ld[s, 1]
                obuf[r, :] = gc
                sm[0, 2:3, :] += jnp.sum(gc * lag2, axis=0, keepdims=True)
                sm[0, 3:4, :] += jnp.sum(gc * lag1, axis=0, keepdims=True)
                sm[0, 4:5, :] += jnp.sum(gc * gated, axis=0, keepdims=True)
                tb[0:8, :] = tb[tt : tt + 8, :]
                eng_mid.r4(u - 2, su)
                eng_mid.r1(u, su)
                eng_mid.r3(u - 1, 1 - su)
                eng_mid.drain(u - 2, su)
                return 0

            lax.fori_loop(0, nt_, one, 0)
            u = ndn
            act_on(load_down(u, 128, 16), "start")
            put_out(nt_ - 1).wait()
            first, second = obuf[0:1, :], obuf[1:2, :]
            k1a, k2a, k2b = msk_ref[0:1, 0:1], msk_ref[0:1, 1:2], msk_ref[1:2, 1:2]
            edge_s[6:7, :] = vec[2:3, :] * (k2a * first)
            edge_s[7:8, :] = vec[3:4, :] * (k1a * first) + vec[2:3, :] * (k2b * second)
            edge = remote(edge_s, edge_r, hsem.at[3], hsem.at[4], pc.zs[2])
            edge.start()
            act_on(load_down(u, 128, 16), "wait")
            eng(u).r0(u, u % 2)
            eng(u - 1).r2(u - 1, (u - 1) % 2)
            mcopy.wait()
            so = (u + 1) % 2
            for i in range(4):
                t = dg(nm[:, 256 * i : 256 * i + 256].T, nf[...], 1, 0).astype(BF)
                for a in range(2):
                    part[so, a, i // 2, i % 2] = t[:, 512 * a : 512 * a + 512].reshape(2, 4, 32, 512)
            eng(u - 2).r4(u - 2, u % 2)
            eng(u).r1(u, u % 2)
            eng(u - 1).r3(u - 1, (u - 1) % 2)
            eng(u - 2).drain(u - 2, u % 2)
            u = ndn + 1
            eng(u).r0(u, u % 2)
            eng(u - 1).r2(u - 1, (u - 1) % 2)
            grad_in(1, (u + 1) % 2)
            eng(u - 2).r4(u - 2, u % 2)
            eng(u).r1(u, u % 2)
            eng(u - 1).r3(u - 1, (u - 1) % 2)
            eng(u - 2).drain(u - 2, u % 2)
            u = ndn + 2
            eng(u).r0(u, u % 2)
            eng(u - 1).r2(u - 1, (u - 1) % 2)
            edge.wait()

            def fetch2(i, s):
                r = cols(i, tt)
                return [pltpu.make_async_copy(bcx_h.at[k, r], ld.at[s, k], lsem.at[s, k]) for k in (0, 2)]

            obuf[tok : tok + 8, :] = jnp.zeros((8, dim), F32)
            act_on(fetch2(0, 0), "start")

            def two(i, _):
                s = lax.rem(i, 2)
                r = cols(i, tt)
                pl.when(i + 1 < nt_)(lambda: act_on(fetch2(i + 1, 1 - s), "start"))
                act_on(fetch2(i, s), "wait")
                tb[...] = obuf[pl.ds(pl.multiple_of(i * tt, tt), tt + 8), :]
                k1, k2 = msk_ref[r, 3:4], msk_ref[r, 4:5]
                ost[...] = (vec[4:5, :] * tb[0:tt, :] + vec[3:4, :] * (k1 * tb[1 : 1 + tt, :])
                            + vec[2:3, :] * (k2 * tb[2 : 2 + tt, :]))

                @pl.when(i == nt_ - 1)
                def _():
                    ost[tt - 8 : tt, :] += edge_r[...]

                gg = ost[...]
                gp[r, 0:1024] = (gg * ld[s, 2]).astype(BF)
                gp[r, 2048:3072] = (gg * ld[s, 0]).astype(BF)
                return 0

            lax.fori_loop(0, nt_, two, 0)
            grad_in(0, (u + 1) % 2)
            eng(u - 2).r4(u - 2, u % 2)
            eng(u).r1(u, u % 2)
            eng(u - 1).r3(u - 1, (u - 1) % 2)
            eng(u - 2).drain(u - 2, u % 2)

        pl.run_scoped(passes, pltpu.VMEM((2, 4, tt, dim), F32), pltpu.VMEM((tt, dim), F32), pltpu.VMEM((tt + 8, dim), F32))

        def ending(win, ost):
            wl = [pltpu.make_async_copy(win_h.at[:, :, pl.ds(1024 * i, 1024)], win.at[i], lsem.at[0, i]) for i in range(3)]
            act_on(wl, "start")
            u = ndn + 3
            eng(u).r0(u, u % 2)
            eng(u - 1).r2(u - 1, (u - 1) % 2)
            grad_in(2, (u + 1) % 2)
            eng(u - 2).r4(u - 2, u % 2)
            eng(u).r1(u, u % 2)
            eng(u - 1).r3(u - 1, (u - 1) % 2)
            eng(u - 2).drain(u - 2, u % 2)
            u = ndn + 4
            eng(u).r0(u, u % 2)
            eng(u - 1).r2(u - 1, (u - 1) % 2)
            act_on(wl, "wait")

            def put_tok(i, s):
                return pltpu.make_async_copy(ost.at[s], gtok_ref.at[cols(i, tt)], lsem.at[s, 4])

            def grad_tok(i, _):
                s = lax.rem(i, 2)
                r = cols(i, tt)
                g = dg(gp[r, 0:1024], win[0].reshape(dim, dim), 1, 1)
                g = g + dg(gp[r, 1024:2048], win[1].reshape(dim, dim), 1, 1)
                g = g + dg(gp[r, 2048:3072], win[2].reshape(dim, dim), 1, 1)
                v = tok_ref[r, :].astype(F32)
                inv = inverse_rms(v)
                a = g * vec[0:1, :]
                dot = jnp.sum(a * v, axis=1, keepdims=True) / dim
                pl.when(i >= 2)(lambda: put_tok(i - 2, s).wait())
                ost[s] = gn[r, :] + (inv * a - v * (inv * inv * inv) * dot)
                put_tok(i, s).start()
                sm[0, 0:1, :] += jnp.sum(g * v * inv, axis=0, keepdims=True)
                return 0

            lax.fori_loop(0, 2, grad_tok, 0)
            eng(u - 2).r4(u - 2, u % 2)
            eng(u).r1(u, u % 2)
            eng(u - 1).r3(u - 1, (u - 1) % 2)
            eng(u - 2).drain(u - 2, u % 2)
            lax.fori_loop(2, nt_, grad_tok, 0)
            small.s0()
            eng(u).r2(u, u % 2)
            eng(u - 1).r4(u - 1, (u - 1) % 2)
            small.s1()
            eng(u).r3(u, u % 2)
            eng(u - 1).drain(u - 1, (u - 1) % 2)
            small.s2()
            small.s3()
            eng(u).r4(u, u % 2)
            small.s4()
            eng(u).drain(u, u % 2)
            for i in (nt_ - 2, nt_ - 1):
                put_tok(i, i % 2).wait()

        pl.run_scoped(ending, pltpu.VMEM((3, 32, 32, dim), BF), pltpu.VMEM((2, tt, dim), F32))

    pl.run_scoped(mixer_backward, pltpu.VMEM((tok, 3 * dim), BF), pltpu.VMEM((dim, tok), BF), pltpu.VMEM((32, 32, dim), BF))

    for u in range(9):
        unit(u).fin()

    def last(j, carry):
        gu_unit(j).fin()
        return carry

    lax.fori_loop(0, n, last, 0)
    small.fin()


def block_call(tokens, cot, masks, vecs, w_in, w_out, w_gate, w_up, w_down):
    tok, dim = tokens.shape
    ff = w_gate.shape[1]
    n = ff // 512
    sd = jax.ShapeDtypeStruct
    outs = [
        sd((tok, dim), F32), sd((tok, dim), F32), sd((32, ff), F32), sd((32, ff), F32), sd((ff // 32, dim), F32),
        sd((32, dim), F32), sd((32, 3 * dim), F32), sd((32, 8, dim), F32),
        sd((32, 32, 3 * dim), BF), sd((32, 32, dim), BF), sd((ff, dim), BF), sd((32, 2, 32, ff), BF),
        sd((32, 16, 128), BF), sd((3, tok, dim), F32), sd((tok, dim), F32), sd((tok, dim), BF), sd((ff, dim), BF),
    ]
    return pl.pallas_call(
        block_kernel,
        out_shape=outs,
        in_specs=[VM, ANY, VM, ANY, ANY, ANY, ANY, ANY, ANY],
        out_specs=[ANY] * len(outs),
        scratch_shapes=[
            pltpu.VMEM((tok + 8, dim), F32),
            pltpu.VMEM((tok, dim), F32),
            pltpu.VMEM((tok, dim), BF),
            pltpu.VMEM((tok, dim), BF),
            pltpu.VMEM((tok, dim), BF),
            pltpu.VMEM((16, dim), F32),
            pltpu.VMEM((1, 8, dim), F32),
            pltpu.VMEM((16, dim), BF),
            pltpu.VMEM((8, dim), F32),
            pltpu.VMEM((8, dim), F32),
            pltpu.VMEM((8, dim), F32),
            pltpu.SemaphoreType.DMA((4,)),
            pltpu.SemaphoreType.DMA((2, 5)),
            pltpu.SemaphoreType.DMA((5,)),
            pltpu.SemaphoreType.DMA((n + 10, NG)),
            pltpu.SemaphoreType.DMA((n + 10, NG)),
        ] + scatter_scratch(n + 9, 32, 512),
        name="block",
        compiler_params=pltpu.CompilerParams(collective_id=1, has_side_effects=True, vmem_limit_bytes=61 * 2**20),
    )(tokens, cot, masks, vecs[None], w_in[None], w_out[None], w_gate[None], w_up[None], w_down)


def passed_along(array, axis, by):
    size = lax.axis_size(axis)
    pairs = [(i, i + by) for i in range(size) if 0 <= i + by < size]
    return lax.ppermute(array, axis, pairs)


def rms_forward(values, gain_vec):
    inv_rms = lax.rsqrt(jnp.mean(values * values, axis=1, keepdims=True) + epsilon)
    return (values * inv_rms * gain_vec[None, :], inv_rms)


def rms_backward(values, inv_rms, gain_vec, grad_normed):
    weighted = grad_normed * gain_vec[None, :]
    features = values.shape[1]
    total_dot = jnp.sum(weighted * values, axis=1, keepdims=True)
    grad_values = inv_rms * weighted - values * (inv_rms * inv_rms * inv_rms) * total_dot / features
    grad_gain = jnp.sum(grad_normed * values * inv_rms, axis=0)
    return (grad_values, grad_gain)


def outer_sum(left, right):
    return lax.dot_general(
        left, right, (((0,), (0,)), ((), ())), preferred_element_type=jnp.float32
    )


def back_product(grad_low, weight_mat):
    return lax.dot_general(
        grad_low, weight_mat, (((1,), (1,)), ((), ())), preferred_element_type=jnp.float32
    )


def doc_masks(doc_lengths, valid_count, first_pos, tok_count):
    packed_row = first_pos // ROW_LEN
    lengths = lax.dynamic_index_in_dim(doc_lengths, packed_row, 0, keepdims=False)
    limit_count = lax.dynamic_index_in_dim(valid_count, packed_row, 0, keepdims=False)
    offsets = jnp.cumsum(lengths) - lengths
    places = first_pos % ROW_LEN + jnp.arange(tok_count, dtype=jnp.int32)
    begins = jnp.any(offsets[None, :] == places[:, None], axis=1)
    before = jnp.any(offsets[None, :] == places[:, None] - 1, axis=1)
    keep_one = jnp.where(begins, 0.0, 1.0).astype(jnp.float32)
    keep_two = jnp.where(begins | before, 0.0, 1.0).astype(jnp.float32)
    live_mask = jnp.where(places < limit_count, 1.0, 0.0).astype(jnp.float32)
    return (keep_one[:, None], keep_two[:, None], live_mask[:, None])


def shards_plain(
    tokens,
    cotangent,
    gain_mix,
    in_weight,
    conv_taps,
    out_weight,
    gain_ffn,
    gate_weight,
    up_weight,
    down_weight,
    doc_lengths,
    valid_count,
):
    tok_count = tokens.shape[0]
    first_pos = lax.axis_index(("wide", "narrow")) * tok_count
    keep_one, keep_two, live_mask = doc_masks(doc_lengths, valid_count, first_pos, tok_count)
    full_gm, w_in, full_taps, w_out, full_gf, w_gate, w_up, w_down = (
        lax.all_gather(gain_mix, ("wide", "narrow"), axis=0, tiled=True),
        lax.all_gather(in_weight, ("wide", "narrow"), axis=0, tiled=True),
        lax.all_gather(conv_taps, ("wide", "narrow"), axis=1, tiled=True),
        lax.all_gather(out_weight, ("wide", "narrow"), axis=0, tiled=True),
        lax.all_gather(gain_ffn, ("wide", "narrow"), axis=0, tiled=True),
        lax.all_gather(gate_weight, ("wide", "narrow"), axis=0, tiled=True),
        lax.all_gather(up_weight, ("wide", "narrow"), axis=0, tiled=True),
        lax.all_gather(down_weight, ("wide", "narrow"), axis=0, tiled=True),
    )
    mix_gain = full_gm.astype(jnp.float32)
    ffn_gain = full_gf.astype(jnp.float32)
    taps = full_taps.astype(jnp.float32)
    features = tokens.shape[1]
    tok_float = tokens.astype(jnp.float32)
    normed_mix, inv_mix = rms_forward(tok_float, mix_gain)
    normed_low = normed_mix.astype(jnp.bfloat16)
    projected = jnp.dot(normed_low, w_in, preferred_element_type=jnp.float32)
    b_part = projected[:, :features]
    c_part = projected[:, features : 2 * features]
    x_part = projected[:, 2 * features :]
    gated = b_part * x_part
    edge_rows = passed_along(gated[-2:], "narrow", 1)
    extended = jnp.concatenate([edge_rows, gated], axis=0)
    lag_one = keep_one * extended[1:-1]
    lag_two = keep_two * extended[:-2]
    conv_out = taps[2][None, :] * gated + taps[1][None, :] * lag_one + taps[0][None, :] * lag_two
    mixed_low = (c_part * conv_out).astype(jnp.bfloat16)
    hidden_res = tok_float + jnp.dot(mixed_low, w_out, preferred_element_type=jnp.float32)
    normed_ffn, inv_ffn = rms_forward(hidden_res, ffn_gain)
    ffn_low = normed_ffn.astype(jnp.bfloat16)
    gate_val = jnp.dot(ffn_low, w_gate, preferred_element_type=jnp.float32)
    up_val = jnp.dot(ffn_low, w_up, preferred_element_type=jnp.float32)
    sigmoid_gate = jax.nn.sigmoid(gate_val)
    silu_val = gate_val * sigmoid_gate
    act_low = (silu_val * up_val).astype(jnp.bfloat16)
    ffn_out = jnp.dot(act_low, w_down, preferred_element_type=jnp.float32)
    output = live_mask * (hidden_res + ffn_out)
    again_gm, w_in, again_taps, w_out, again_gf, w_gate, w_up, w_down = (
        lax.all_gather(gain_mix, ("wide", "narrow"), axis=0, tiled=True),
        lax.all_gather(in_weight, ("wide", "narrow"), axis=0, tiled=True),
        lax.all_gather(conv_taps, ("wide", "narrow"), axis=1, tiled=True),
        lax.all_gather(out_weight, ("wide", "narrow"), axis=0, tiled=True),
        lax.all_gather(gain_ffn, ("wide", "narrow"), axis=0, tiled=True),
        lax.all_gather(gate_weight, ("wide", "narrow"), axis=0, tiled=True),
        lax.all_gather(up_weight, ("wide", "narrow"), axis=0, tiled=True),
        lax.all_gather(down_weight, ("wide", "narrow"), axis=0, tiled=True),
    )
    mix_gain = again_gm.astype(jnp.float32)
    ffn_gain = again_gf.astype(jnp.float32)
    taps = again_taps.astype(jnp.float32)
    grad_res = live_mask * cotangent.astype(jnp.float32)
    grad_ffn_low = grad_res.astype(jnp.bfloat16)
    grad_down = outer_sum(act_low, grad_ffn_low)
    grad_act = back_product(grad_ffn_low, w_down)
    grad_gate_low = (
        grad_act * up_val * sigmoid_gate * (1.0 + gate_val * (1.0 - sigmoid_gate))
    ).astype(jnp.bfloat16)
    grad_up_low = (grad_act * silu_val).astype(jnp.bfloat16)
    grad_gate = outer_sum(ffn_low, grad_gate_low)
    grad_up = outer_sum(ffn_low, grad_up_low)
    grad_nffn = back_product(grad_gate_low, w_gate) + back_product(grad_up_low, w_up)
    grad_hnorm, grad_gf = rms_backward(hidden_res, inv_ffn, ffn_gain, grad_nffn)
    grad_hidden = grad_res + grad_hnorm
    grad_mix_low = grad_hidden.astype(jnp.bfloat16)
    grad_out = outer_sum(mixed_low, grad_mix_low)
    grad_mixed = back_product(grad_mix_low, w_out)
    grad_c = grad_mixed * conv_out
    grad_conv = grad_mixed * c_part
    grad_taps = jnp.stack(
        [
            jnp.sum(grad_conv * lag_two, axis=0),
            jnp.sum(grad_conv * lag_one, axis=0),
            jnp.sum(grad_conv * gated, axis=0),
        ],
        axis=0,
    )
    lag_grad_one = taps[1][None, :] * keep_one * grad_conv
    lag_grad_two = taps[0][None, :] * keep_two * grad_conv
    grad_ext = (
        jnp.pad(taps[2][None, :] * grad_conv, ((2, 0), (0, 0)))
        + jnp.pad(lag_grad_one, ((1, 1), (0, 0)))
        + jnp.pad(lag_grad_two, ((0, 2), (0, 0)))
    )
    from_right = passed_along(grad_ext[:2], "narrow", -1)
    grad_gated = jnp.concatenate([grad_ext[2:-2], grad_ext[-2:] + from_right], axis=0)
    grad_b = grad_gated * x_part
    grad_x = grad_gated * b_part
    grad_proj_low = jnp.concatenate([grad_b, grad_c, grad_x], axis=1).astype(jnp.bfloat16)
    grad_in = outer_sum(normed_low, grad_proj_low)
    grad_nmix = back_product(grad_proj_low, w_in)
    grad_tnorm, grad_gm = rms_backward(tok_float, inv_mix, mix_gain, grad_nmix)
    grad_tokens = grad_hidden + grad_tnorm
    sum_gm, sum_in, sum_taps, sum_out, sum_gf, sum_gate, sum_up, sum_down = (
        lax.psum_scatter(grad_gm, ("wide", "narrow"), scatter_dimension=0, tiled=True),
        lax.psum_scatter(grad_in, ("wide", "narrow"), scatter_dimension=0, tiled=True),
        lax.psum_scatter(grad_taps, ("wide", "narrow"), scatter_dimension=1, tiled=True),
        lax.psum_scatter(grad_out, ("wide", "narrow"), scatter_dimension=0, tiled=True),
        lax.psum_scatter(grad_gf, ("wide", "narrow"), scatter_dimension=0, tiled=True),
        lax.psum_scatter(grad_gate, ("wide", "narrow"), scatter_dimension=0, tiled=True),
        lax.psum_scatter(grad_up, ("wide", "narrow"), scatter_dimension=0, tiled=True),
        lax.psum_scatter(grad_down, ("wide", "narrow"), scatter_dimension=0, tiled=True),
    )
    return (
        output,
        grad_tokens,
        sum_gm,
        sum_in,
        sum_taps,
        sum_out,
        sum_gf,
        sum_gate,
        sum_up,
        sum_down,
    )


def shards(
    tokens, cotangent, gain_mix, in_weight, conv_taps, out_weight, gain_ffn,
    gate_weight, up_weight, down_weight, doc_lengths, valid_count,
):
    tok_count = tokens.shape[0]
    me = lax.axis_index(("wide", "narrow"))
    keep_one, keep_two, live_mask = doc_masks(doc_lengths, valid_count, me * tok_count, tok_count)
    later_one = jnp.pad(keep_one[1:], ((0, 1), (0, 0)))
    later_two = jnp.pad(keep_two[2:], ((0, 2), (0, 0)))
    masks = jnp.concatenate([keep_one, keep_two, live_mask, later_one, later_two], axis=1)
    masks = jnp.pad(masks, ((0, 0), (0, 123)))
    own = gain_mix.shape[0]
    vecs = jnp.concatenate([gain_mix[None], gain_ffn[None], conv_taps, jnp.zeros((11, own), BF)], axis=0)
    here = lax.broadcasted_iota(jnp.int32, (16, 128), 1) // own == lax.axis_index("narrow")
    vecs = jnp.where(here, jnp.concatenate([vecs] * 4, axis=1), jnp.zeros((), BF))
    output, grad_tokens, sum_gate, sum_up, sum_down, sum_out, sum_in, all_small = block_call(
        tokens, cotangent, masks, vecs, in_weight, out_weight, gate_weight, up_weight, down_weight
    )[:8]
    mine = lax.dynamic_slice_in_dim(jnp.sum(all_small, axis=0), me * own, own, 1)
    return (output, grad_tokens, mine[0], sum_in, mine[2:5], sum_out, mine[1], sum_gate, sum_up, sum_down)


def solution(mesh):
    both = ("wide", "narrow")
    rows, vec, flat = P(both, None), P(both), P(None, both)
    step = shards if (mesh.shape["wide"], mesh.shape["narrow"]) == (8, 4) else shards_plain
    return jax.shard_map(
        step,
        mesh=mesh,
        in_specs=(rows, rows, vec, rows, flat, rows, vec, rows, rows, rows, P(), P()),
        out_specs=(rows, rows, vec, rows, flat, rows, vec, rows, rows, rows),
        check_vma=False,
    )
```

```python
import functools

import jax
import jax.numpy as jnp
from jax import lax
from jax.experimental import pallas as pl
from jax.experimental.pallas import tpu as pltpu
from jax.sharding import PartitionSpec as P

ROW_LEN = 4096
epsilon = 1e-05
F32 = jnp.float32
BF = jnp.bfloat16
MESH = pl.DeviceIdType.MESH
ANY = pl.BlockSpec(memory_space=pl.ANY)
VM = pl.BlockSpec(memory_space=pltpu.VMEM)


def dg(a, b, ca, cb):
    return lax.dot_general(a, b, (((ca,), (cb,)), ((), ())), preferred_element_type=F32)


class Place:
    def __init__(self):
        w = lax.axis_index("wide")
        z = lax.axis_index("narrow")
        c = lax.rem(w, 2)
        x = lax.rem(w // 2, 2)
        y = w // 4
        self.w, self.z, self.c, self.x, self.y = w, z, c, x, y
        self.core = (w + 1 - 2 * c, z)
        self.xn = (w + 2 - 4 * x, z)
        self.yn = (w + 4 - 8 * y, z)
        self.zs = [(w, lax.rem(z + k, 4)) for k in (1, 2, 3)]
        self.zto = [lax.rem(z + k, 4) for k in (1, 2, 3)]
        self.zfrom = [lax.rem(z + 4 - k, 4) for k in (1, 2, 3)]

        def base(yy, xx, cc):
            return 16 * yy + 8 * xx + 4 * cc

        self.own, self.xb = base(y, x, c), base(y, 1 - x, c)
        self.yb, self.db = base(1 - y, x, c), base(1 - y, 1 - x, c)
        self.sown, self.sxb = base(y, x, 1 - c), base(y, 1 - x, 1 - c)
        self.syb, self.sdb = base(1 - y, x, 1 - c), base(1 - y, 1 - x, 1 - c)
        self.me = self.own + z

    def greet(self):
        bar = pltpu.get_barrier_semaphore()
        peers = [self.core, self.xn, self.yn] + self.zs
        for p in peers:
            pl.semaphore_signal(bar, inc=1, device_id=p, device_id_type=MESH)
        pl.semaphore_wait(bar, len(peers))


def remote(src, dst, ss, rs, dev):
    return pltpu.make_async_remote_copy(
        src_ref=src, dst_ref=dst, send_sem=ss, recv_sem=rs, device_id=dev, device_id_type=MESH
    )


class Gather:
    def __init__(self, pc, src, dst, full, ss, rs):
        self.pc, self.src, self.dst, self.full, self.ss, self.rs = pc, src, dst, full, ss, rs
        self.parts = range(len(src))

    def zc(self, i, k):
        q = 3 * i + k
        return remote(self.src[i](), self.dst[i](self.pc.me, 1), self.ss.at[q], self.rs.at[q], self.pc.zs[k])

    def zr(self, i, k):
        q = 3 * i + k
        v = self.dst[i](self.pc.own + self.pc.zfrom[k], 1)
        return remote(v, v, self.ss.at[q], self.rs.at[q], self.pc.zs[k])

    def loc(self, i):
        return pltpu.make_async_copy(self.src[i](), self.dst[i](self.pc.me, 1), self.ss.at[14 + i])

    def cp(self, k, b, n, dev):
        v = self.full(b, n)
        return remote(v, v, self.ss.at[k], self.rs.at[k], dev)

    def s0(self):
        for i in self.parts:
            self.loc(i).start()
            for k in range(3):
                self.zc(i, k).start()

    def s1(self):
        p = self.pc
        for i in self.parts:
            self.loc(i).wait()
            for k in range(3):
                self.zr(i, k).wait_recv()
        self.cp(6, p.own, 4, p.xn).start()
        self.cp(7, p.own, 4, p.yn).start()
        self.cp(8, p.own, 4, p.core).start()

    def s2(self):
        p = self.pc
        self.cp(6, p.xb, 4, p.xn).wait_recv()
        self.cp(9, p.xb, 2, p.yn).start()
        self.cp(10, p.xb, 4, p.core).start()
        self.cp(7, p.yb, 4, p.yn).wait_recv()
        self.cp(11, p.yb + 2, 2, p.xn).start()
        self.cp(12, p.yb, 4, p.core).start()

    def s3(self):
        p = self.pc
        self.cp(9, p.db, 2, p.yn).wait_recv()
        self.cp(11, p.db + 2, 2, p.xn).wait_recv()
        self.cp(13, p.db, 4, p.core).start()

    def s4(self):
        p = self.pc
        for k, b in ((8, p.sown), (10, p.sxb), (12, p.syb), (13, p.sdb)):
            self.cp(k, b, 4, p.core).wait_recv()

    def fin(self):
        p = self.pc
        for i in self.parts:
            for k in range(3):
                self.zc(i, k).wait_send()
        for k, b, n in (
            (6, p.own, 4), (7, p.own, 4), (8, p.own, 4), (9, p.xb, 2),
            (10, p.xb, 4), (11, p.yb + 2, 2), (12, p.yb, 4), (13, p.db, 4),
        ):
            self.cp(k, b, n, p.core).wait_send()


NG = 16
NL = 4
AHEAD = 2
NS = 4


class Scatter:
    def __init__(self, pc, bufs, h, out):
        self.pc, self.h, self.out = pc, h, out
        (self.part, self.l0, self.ldx, self.ldy, self.lx, self.ly, self.lz,
         self.sd, self.sx, self.sy, self.so, self.sz, self.ob, self.ss, self.rs, self.os) = bufs

    def hr(self):
        return pl.ds(0, self.h)

    def c0(self, j, s):
        p = self.pc
        return remote(self.part.at[lax.rem(j, 2), :, :, :, 1 - p.c, :, self.hr()], self.l0.at[lax.rem(j, 3), :, :, :, :, self.hr()],
                      self.ss.at[j, 0], self.rs.at[j, 0], p.core)

    def cdx(self, j, s):
        return remote(self.sd.at[lax.rem(j, 2), :, pl.ds(0, 2), self.hr()], self.ldx.at[lax.rem(j, NL), :, :, self.hr()],
                      self.ss.at[j, 1], self.rs.at[j, 1], self.pc.xn)

    def cdy(self, j, s):
        return remote(self.sd.at[lax.rem(j, 2), :, pl.ds(2, 2), self.hr()], self.ldy.at[lax.rem(j, NL), :, :, self.hr()],
                      self.ss.at[j, 2], self.rs.at[j, 2], self.pc.yn)

    def cx(self, j, s):
        return remote(self.sx.at[s, :, :, self.hr()], self.lx.at[lax.rem(j, NL), :, :, self.hr()],
                      self.ss.at[j, 3], self.rs.at[j, 3], self.pc.xn)

    def cy(self, j, s):
        return remote(self.sy.at[s, :, :, self.hr()], self.ly.at[lax.rem(j, NL), :, :, self.hr()],
                      self.ss.at[j, 4], self.rs.at[j, 4], self.pc.yn)

    def cz(self, j, s, k):
        return remote(self.sz.at[lax.rem(j, 2), :, self.pc.zto[k], self.hr()], self.lz.at[lax.rem(j, NL), k, :, self.hr()],
                      self.ss.at[j, 5 + k], self.rs.at[j, 5 + k], self.pc.zs[k])

    def r0(self, j, s):
        self.c0(j, s).start()

    def q(self, j, s, a, yy, xx):
        hr = self.hr()
        return (self.part[lax.rem(j, 2), a, yy, xx, self.pc.c, :, hr].astype(F32)
                + self.l0[lax.rem(j, 3), a, yy, xx, :, hr].astype(F32))

    def r1(self, j, s):
        p, hr = self.pc, self.hr()
        self.c0(j, s).wait()
        for a in range(2):
            self.sd[lax.rem(j, 2), a, :, hr] = self.q(j, s, a, 1 - p.y, 1 - p.x).astype(BF)
        self.cdx(j, s).start()
        self.cdy(j, s).start()
        for a in range(2):
            self.sx[s, a, :, hr] = self.q(j, s, a, p.y, 1 - p.x).astype(BF)
            self.sy[s, a, :, hr] = self.q(j, s, a, 1 - p.y, p.x).astype(BF)
            self.so[s, a, :, hr] = self.q(j, s, a, p.y, p.x)

    def r2(self, j, s):
        hr = self.hr()
        lo, hi = pl.ds(0, 2), pl.ds(2, 2)
        self.cdx(j, s).wait()
        for a in range(2):
            self.sy[s, a, lo, hr] = (self.sy[s, a, lo, hr].astype(F32) + self.ldx[lax.rem(j, NL), a, :, hr].astype(F32)).astype(BF)
        self.cy(j, s).start()
        self.cdy(j, s).wait()
        for a in range(2):
            self.sx[s, a, hi, hr] = (self.sx[s, a, hi, hr].astype(F32) + self.ldy[lax.rem(j, NL), a, :, hr].astype(F32)).astype(BF)
        self.cx(j, s).start()

    def r3(self, j, s):
        hr = self.hr()
        self.cy(j, s).wait()
        self.cx(j, s).wait()
        for a in range(2):
            t = self.so[s, a, :, hr] + self.lx[lax.rem(j, NL), a, :, hr].astype(F32) + self.ly[lax.rem(j, NL), a, :, hr].astype(F32)
            self.so[s, a, :, hr] = t
            self.sz[lax.rem(j, 2), a, :, hr] = t.astype(BF)
        for k in range(3):
            self.cz(j, s, k).start()

    def r4(self, j, s):
        hr = self.hr()
        for k in range(3):
            self.cz(j, s, k).wait()
        for a in range(2):
            t = self.so[s, a, self.pc.z, hr]
            for k in range(3):
                t = t + self.lz[lax.rem(j, NL), k, a, hr].astype(F32)
            self.ob[s, a, hr] = t
        self.out(j, s, self.ob, self.os, "start")

    def go(self, stage, j):
        (self.r1, self.r2, self.r3, self.r4)[stage - 1](j, lax.rem(j, NS))

    def begin(self, j):
        self.r0(j, lax.rem(j, NS))

    def end(self, j):
        self.drain(j, lax.rem(j, NS))

    def drain(self, j, s):
        self.out(j, s, self.ob, self.os, "wait")


def scatter_scratch(n, h, w):
    return [
        pltpu.VMEM((2, 2, 2, 2, 2, 4, h, w), BF),
        pltpu.VMEM((3, 2, 2, 2, 4, h, w), BF),
        pltpu.VMEM((NL, 2, 2, h, w), BF),
        pltpu.VMEM((NL, 2, 2, h, w), BF),
        pltpu.VMEM((NL, 2, 4, h, w), BF),
        pltpu.VMEM((NL, 2, 4, h, w), BF),
        pltpu.VMEM((NL, 3, 2, h, w), BF),
        pltpu.VMEM((2, 2, 4, h, w), BF),
        pltpu.VMEM((NS, 2, 4, h, w), BF),
        pltpu.VMEM((NS, 2, 4, h, w), BF),
        pltpu.VMEM((NS, 2, 4, h, w), F32),
        pltpu.VMEM((2, 2, 4, h, w), BF),
        pltpu.VMEM((NS, 2, h, w), F32),
        pltpu.SemaphoreType.DMA((n, 8)),
        pltpu.SemaphoreType.DMA((n, 8)),
        pltpu.SemaphoreType.DMA((NS, 2)),
    ]


def inverse_rms(v):
    return lax.rsqrt(jnp.mean(v * v, axis=1, keepdims=True) + epsilon)


def block_kernel(
    tok_ref, cot_ref, doc_ref, count_ref, vec_ref, win_s, wout_s, wgate_s, wup_s, wdown_s,
    out_ref, gtok_ref, ggate_o, gup_o, gdown_o, gout_o, gin_o, small_o,
    win_h, wout_h, wd_h, wgu_h, vec_h, bcx_h, hid_h, mix_h, gdown_h,
    obuf, gn, nf, gf, nm, msk_ref, vec, vown, sm, sml, halo_t, halo_g, edge_s, edge_r,
    vsem, lsem, hsem, esem, gss, grs, *sc,
):
    pc = Place()
    tok, dim = tok_ref.shape
    ff = wgate_s.shape[-1]
    f = 512
    n = ff // f
    tt = 256
    nt_ = tok // tt
    part = sc[0]

    def cols(j, w=f):
        return pl.ds(pl.multiple_of(j * w, w), w)

    def simple(u, src, dst, c0, w):
        at = lambda b, m: dst.at[pl.ds(b, m), :, pl.ds(c0, w)]
        return Gather(pc, [lambda: src.at[:, :, pl.ds(c0, w)]], [at], at, gss.at[u], grs.at[u])

    def down_unit(i):
        rows = ff // 32
        at = lambda b, m: wd_h.at[pl.ds(pl.multiple_of(b * rows, rows), m * rows), pl.ds(256 * i, 256)]
        return Gather(pc, [lambda: wdown_s.at[:, pl.ds(256 * i, 256)]], [at], at, gss.at[5 + i], grs.at[5 + i])

    def gu_unit(j):
        srcs = [lambda: wgate_s.at[:, :, cols(j)], lambda: wup_s.at[:, :, cols(j)]]
        dsts = [lambda b, m: wgu_h.at[pl.ds(b, m), 0, :, cols(j)], lambda b, m: wgu_h.at[pl.ds(b, m), 1, :, cols(j)]]
        return Gather(pc, srcs, dsts, lambda b, m: wgu_h.at[pl.ds(b, m), :, :, cols(j)], gss.at[9 + j], grs.at[9 + j])

    def unit(u):
        if u == 0:
            return simple(0, vown, vec_h, 0, 128)
        if u < 4:
            return simple(u, win_s, win_h, 1024 * (u - 1), 1024)
        if u == 4:
            return simple(4, wout_s, wout_h, 0, 1024)
        if u < 9:
            return down_unit(u - 5)
        return gu_unit(u - 9)

    def small_copies(k):
        peers = [pc.core, pc.xn, pc.yn] + pc.zs
        return [remote(sm, sml.at[q], esem.at[q], esem.at[6 + q], peers[q]) for q in ((0,), (1,), (2,), (3, 4, 5))[k]]

    def small_begin(k):
        for c in small_copies(k):
            c.start()

    def small_end(k):
        for c in small_copies(k):
            c.wait()
        t = sm[...]
        for q in ((0,), (1,), (2,), (3, 4, 5))[k]:
            t = t + sml[q]
        sm[...] = t

    def step(t):
        unit(t).s1()
        if t + AHEAD < 9 + n:
            unit(t + AHEAD).s0()
        if t >= 2:
            unit(t - 1).s2()
        if t >= 3:
            unit(t - 2).s3()
        if t >= 4:
            unit(t - 3).s4()

    ndn = n + 4
    gdown6 = gdown_h.reshape(2, 2, 2, 4, ff // 32, dim)

    def act_on(copies, what):
        for c in copies:
            getattr(c, what)()

    def out_gu(j, s, ob, osem, what):
        act_on([pltpu.make_async_copy(ob.at[s, 0], ggate_o.at[:, cols(j)], osem.at[s, 0]),
                pltpu.make_async_copy(ob.at[s, 1], gup_o.at[:, cols(j)], osem.at[s, 1])], what)

    def out_rows(dst, r0, c0, h):
        def go(j, s, ob, osem, what):
            act_on([pltpu.make_async_copy(ob.at[s, a, pl.ds(0, h)],
                                          dst.at[pl.ds(r0, h), pl.ds(c0 + 512 * a, 512)], osem.at[s, a])
                    for a in range(2)], what)
        return go

    def out_down(j, s, ob, osem, what):
        out_rows(gdown_o, pl.multiple_of((j - n) * 32, 32), 0, 32)(j, s, ob, osem, what)

    def out_mixed(j, s, ob, osem, what):
        pl.when(j < n)(lambda: out_gu(j, s, ob, osem, what))
        pl.when(j >= n)(lambda: out_down(j, s, ob, osem, what))

    eng_gu = Scatter(pc, sc, 32, out_gu)
    eng_mid = Scatter(pc, sc, 32, out_mixed)
    order = (1, 0, 2)

    def eng(u):
        if u < ndn:
            return Scatter(pc, sc, 32, out_down)
        if u == ndn:
            return Scatter(pc, sc, 32, out_rows(gout_o, 0, 0, 32))
        if u < ndn + 4:
            return Scatter(pc, sc, 32, out_rows(gin_o, 0, 1024 * order[u - ndn - 1], 32))
        return Scatter(pc, sc, 16, out_rows(gdown_o, 128, 0, 16))

    pc.greet()
    vown[0] = pltpu.roll(vec_ref[...], 32 * pc.z, 1)
    unit(0).s0()
    unit(1).s0()
    cot_copy = pltpu.make_async_copy(cot_ref, gf, hsem.at[0])
    cot_copy.start()
    tail = remote(tok_ref.at[pl.ds(tok - 16, 16)], halo_t, hsem.at[1], hsem.at[2], pc.zs[0])
    tail.start()
    sm[...] = jnp.zeros_like(sm)
    edge_s[...] = jnp.zeros_like(edge_s)
    gn[...] = jnp.zeros_like(gn)
    row_devs = ROW_LEN // tok
    row = pc.me // row_devs
    lens = jnp.broadcast_to(doc_ref[pl.ds(row, 1), :], (8, 128))
    lane = lax.broadcasted_iota(jnp.int32, (8, 128), 1)
    sums = lens
    for k in (1, 2, 4, 8):
        sums = sums + jnp.where(lane >= k, pltpu.roll(sums, k, 1), 0)
    starts = jnp.where(lane < 16, sums - lens, -8)[0:1, :]
    limit = count_ref[row]
    cot_copy.wait()

    def live_rows(i, _):
        r = cols(i, tt)
        t = i * tt + lax.broadcasted_iota(jnp.int32, (tt, 128), 0)
        place = lax.rem(pc.me, row_devs) * tok + t

        def begins(by):
            return jnp.max(jnp.where(starts == place + by, 1.0, 0.0), axis=1, keepdims=True)

        b0, b1, b2, bm = begins(0), begins(1), begins(2), begins(-1)
        ln = lax.broadcasted_iota(jnp.int32, (tt, 128), 1)
        m = jnp.where(ln == 0, 1.0 - b0, 1.0 - jnp.maximum(b0, bm))
        m = jnp.where(ln == 2, jnp.where(place < limit, 1.0, 0.0), m)
        m = jnp.where(ln == 3, jnp.where(t + 1 < tok, 1.0 - b1, 0.0), m)
        msk_ref[r, :] = jnp.where(ln == 4, jnp.where(t + 2 < tok, 1.0 - jnp.maximum(b2, b1), 0.0), m)
        gf[r, :] = (gf[r, :].astype(F32) * msk_ref[r, 2:3]).astype(BF)
        return 0

    lax.fori_loop(0, nt_, live_rows, 0)
    unit(0).s1()
    unit(2).s0()
    unit(0).s2()
    unit(0).s3()
    unit(1).s1()
    unit(3).s0()
    unit(0).s4()

    def mixer_forward(vbuf, win, wout, st, mst, tb):
        vcopy = pltpu.make_async_copy(vec_h, vbuf, vsem.at[0])
        vcopy.start()
        vcopy.wait()
        for q in range(8):
            v = vbuf[4 * q] + vbuf[4 * q + 1] + vbuf[4 * q + 2] + vbuf[4 * q + 3]
            vec[:, 128 * q : 128 * q + 128] = v
        gain = vec[0:1, :]

        def normed(i, _):
            r = cols(i, tt)
            t = tok_ref[r, :].astype(F32)
            nm[r, :] = (t * inverse_rms(t) * gain).astype(BF)
            return 0

        lax.fori_loop(0, nt_, normed, 0)
        step(2)
        step(3)
        wl = [pltpu.make_async_copy(win_h.at[:, :, pl.ds(1024 * i, 1024)], win.at[i], vsem.at[i]) for i in range(3)]
        wl.append(pltpu.make_async_copy(wout_h, wout, vsem.at[3]))
        for t in (4, 5, 6, 7):
            step(t)
            wl[t - 4].start()
        tail.wait()
        th = halo_t[...].astype(F32)
        nh = (th * inverse_rms(th) * gain).astype(BF)
        for c in wl:
            c.wait()
        hb = dg(nh, win[0].reshape(dim, dim), 1, 0) * dg(nh, win[2].reshape(dim, dim), 1, 0)
        halo_g[...] = hb[8:16, :]
        tb[0:8, :] = halo_g[...]

        def stash(i, s):
            r = cols(i, tt)
            return [pltpu.make_async_copy(st.at[s, k], bcx_h.at[k, r], lsem.at[s, k]) for k in range(3)] + [
                pltpu.make_async_copy(mst.at[s], mix_h.at[r], lsem.at[s, 3]),
                pltpu.make_async_copy(obuf.at[r], hid_h.at[r], lsem.at[s, 4])]

        def tile(i, _):
            r = cols(i, tt)
            s = lax.rem(i, 2)
            pl.when(i >= 2)(lambda: act_on(stash(i - 2, s), "wait"))
            x = nm[r, :]
            bv = dg(x, win[0].reshape(dim, dim), 1, 0)
            st[s, 0] = bv
            xv = dg(x, win[2].reshape(dim, dim), 1, 0)
            st[s, 2] = xv
            tb[8 : 8 + tt, :] = bv * xv
            cv = dg(x, win[1].reshape(dim, dim), 1, 0)
            st[s, 1] = cv
            k1, k2 = msk_ref[r, 0:1], msk_ref[r, 1:2]
            conv = (vec[4:5, :] * tb[8 : 8 + tt, :] + vec[3:4, :] * (k1 * tb[7 : 7 + tt, :])
                    + vec[2:3, :] * (k2 * tb[6 : 6 + tt, :]))
            mixed = (cv * conv).astype(BF)
            mst[s] = mixed
            tb[0:8, :] = tb[tt : tt + 8, :]
            h = tok_ref[r, :].astype(F32) + dg(mixed, wout[...].reshape(dim, dim), 1, 0)
            obuf[r, :] = h
            nf[r, :] = (h * inverse_rms(h) * vec[1:2, :]).astype(BF)
            act_on(stash(i, s), "start")
            for k in range(4):
                pl.when(i == k)(functools.partial(step, 8 + k))
            return 0

        lax.fori_loop(0, nt_, tile, 0)
        for i in (nt_ - 2, nt_ - 1):
            act_on(stash(i, i % 2), "wait")

    pl.run_scoped(
        mixer_forward, pltpu.VMEM((32, 8, 128), F32), pltpu.VMEM((3, 32, 32, dim), BF), pltpu.VMEM((32, 32, dim), BF),
        pltpu.VMEM((2, 3, tt, dim), F32), pltpu.VMEM((2, tt, dim), BF), pltpu.VMEM((tt + 8, dim), F32),
    )
    step(12)

    def put(b3, j, s):
        return pltpu.make_async_copy(b3.at[s], gdown_h.at[cols(j), :], vsem.at[s])

    def ffn(gw, uw, dw, act, gg, gu, nt, b3):
        tm = td = 512

        def fetch(j, s):
            return [pltpu.make_async_copy(wgu_h.at[:, 0, :, cols(j)], gw.at[s], lsem.at[s, 0]),
                    pltpu.make_async_copy(wgu_h.at[:, 1, :, cols(j)], uw.at[s], lsem.at[s, 1]),
                    pltpu.make_async_copy(wd_h.at[cols(j), :], dw.at[s], lsem.at[s, 2])]

        act_on(fetch(0, 0), "start")

        def turned(i, _):
            nt[:, cols(i, tt)] = nf[cols(i, tt), :].T
            return 0

        lax.fori_loop(0, nt_, turned, 0)

        def body(j, carry):
            s = lax.rem(j, 2)

            def stage(fn, k, lo=0):
                pl.when(jnp.logical_and(j + k >= lo, j + k < n))(lambda: fn(j + k))

            act_on(fetch(j, s), "wait")

            def tile(i):
                r = pl.ds(i * tm, tm)
                x = nf[r, :]
                g_w, u_w = gw[s].reshape(dim, f), uw[s].reshape(dim, f)
                g = dg(x, g_w, 1, 0)
                u = dg(x, u_w, 1, 0)
                ga = dg(gf[r, :], dw[s], 1, 1)
                sg = jax.nn.sigmoid(g)
                si = g * sg
                a = (si * u).astype(BF)
                act[r, :] = a
                ggv = (ga * u * sg * (1.0 + g * (1.0 - sg))).astype(BF)
                guv = (ga * si).astype(BF)
                gg[r, :] = ggv
                gu[r, :] = guv
                obuf[r, :] += dg(a, dw[s], 1, 0)
                gn[r, :] += dg(ggv, g_w, 1, 1) + dg(guv, u_w, 1, 1)

            tile(0)
            stage(lambda u: eng_gu.go(2, u), -1)
            stage(lambda u: gu_unit(u).s2(), 2, 3)
            tile(1)
            stage(lambda u: eng_gu.go(4, u), -2)
            stage(lambda u: gu_unit(u).s1(), 3, 4)
            stage(lambda u: gu_unit(u).s0(), 4 + AHEAD, 4 + AHEAD)
            for i in range(dim // td):
                x = nt[i * td : (i + 1) * td, :]
                part[s, 0, i] = dg(x, gg[...], 1, 0).astype(BF).reshape(2, 2, 4, 32, f)
                part[s, 1, i] = dg(x, gu[...], 1, 0).astype(BF).reshape(2, 2, 4, 32, f)
            eng_gu.begin(j)
            stage(lambda u: gu_unit(u).s3(), 2, 2)
            stage(lambda u: gu_unit(u).s4(), 1, 1)
            stage(lambda u: act_on(fetch(u, 1 - s), "start"), 1)
            pl.when(j >= 2)(lambda: put(b3, j - 2, s).wait())
            for i in range(f // 256):
                b3[s, i * 256 : (i + 1) * 256, :] = dg(act[:, i * 256 : (i + 1) * 256].T, gf[...], 1, 0).astype(BF)
            put(b3, j, s).start()
            eng_gu.go(1, j)
            stage(lambda u: eng_gu.go(3, u), -1)
            stage(lambda u: eng_gu.end(u), -2)
            return carry

        lax.fori_loop(0, n, body, 0)
        for j in (n - 2, n - 1):
            put(b3, j, j % 2).wait()

    pl.run_scoped(
        ffn, pltpu.VMEM((2, 32, 32, f), BF), pltpu.VMEM((2, 32, 32, f), BF), pltpu.VMEM((2, f, dim), BF),
        pltpu.VMEM((tok, f), BF), pltpu.VMEM((tok, f), BF), pltpu.VMEM((tok, f), BF),
        pltpu.VMEM((dim, tok), BF), pltpu.VMEM((2, f, dim), BF),
    )

    def load_down(u, r0, h):
        s = lax.rem(u, 2)
        return [pltpu.make_async_copy(gdown6.at[:, :, :, :, pl.ds(r0, h), pl.ds(512 * a, 512)],
                                      part.at[s, a, :, :, :, :, pl.ds(0, h)], vsem.at[2 + a]) for a in range(2)]

    def load_mid(u):
        return load_down(u, pl.multiple_of((u - n) * 32, 32), 32)

    def mixer_backward(gp, turn, wout):
        wcopy = pltpu.make_async_copy(wout_h, wout, vsem.at[0])
        act_on(load_mid(n), "start")
        wcopy.start()
        act_on(load_mid(n), "wait")
        eng_mid.begin(n)

        def turned(i, _):
            turn[:, cols(i, tt)] = nm[cols(i, tt), :].T
            return 0

        lax.fori_loop(0, nt_, turned, 0)
        mcopy = pltpu.make_async_copy(mix_h, nm, vsem.at[1])
        mcopy.start()
        wcopy.wait()

        def advance(u):
            for k, stage in ((0, 1), (1, 2), (2, 3), (3, 4)):
                if u - k < ndn + 5:
                    eng(u - k).go(stage, u - k)

        def grad_in(k, s):
            for i in range(2):
                for a in range(2):
                    t = dg(turn[512 * i : 512 * i + 512, :], gp[:, 1024 * k + 512 * a : 1024 * k + 512 * a + 512], 1, 0)
                    part[s, a, i] = t.astype(BF).reshape(2, 2, 4, 32, 512)

        def part_of(u):
            if u == ndn:
                for i in range(4):
                    t = dg(nm[:, 256 * i : 256 * i + 256].T, nf[...], 1, 0).astype(BF)
                    for a in range(2):
                        part[u % 2, a, i // 2, i % 2] = t[:, 512 * a : 512 * a + 512].reshape(2, 4, 32, 512)
            elif u < ndn + 4:
                grad_in(order[u - ndn - 1], u % 2)
            else:
                act_on(load_down(u, 128, 16), "start")
                act_on(load_down(u, 128, 16), "wait")

        def passes(ld, ost, tb, tb2):
            def fetch(i, s):
                r = cols(i, tt)
                return [pltpu.make_async_copy(bcx_h.at[k, r], ld.at[s, k], lsem.at[s, k]) for k in range(3)] + [
                    pltpu.make_async_copy(hid_h.at[r], ld.at[s, 3], lsem.at[s, 3])]

            def put_out(i):
                return pltpu.make_async_copy(ost, out_ref.at[cols(i, tt)], lsem.at[0, 4])

            act_on(fetch(0, 0), "start")
            tb[0:8, :] = halo_g[...]
            obuf[tok : tok + 8, :] = jnp.zeros((8, dim), F32)

            def two(i, s):
                r = cols(i, tt)
                tb2[...] = obuf[pl.ds(pl.multiple_of(i * tt, tt), tt + 8), :]
                k1, k2 = msk_ref[r, 3:4], msk_ref[r, 4:5]
                tb2[0:tt, :] = (vec[4:5, :] * tb2[0:tt, :] + vec[3:4, :] * (k1 * tb2[1 : 1 + tt, :])
                                + vec[2:3, :] * (k2 * tb2[2 : 2 + tt, :]))

                @pl.when(i == nt_ - 1)
                def _():
                    tb2[tt - 8 : tt, :] += edge_r[...]

                gg = tb2[0:tt, :]
                gp[r, 0:1024] = (gg * ld[s, 2]).astype(BF)
                gp[r, 2048:3072] = (gg * ld[s, 0]).astype(BF)

            def one(i, _):
                u = n + i
                s = lax.rem(i, 2)
                r = cols(i, tt)
                eng_mid.go(1, u)
                eng_mid.go(2, u - 1)
                pl.when(i >= 1)(lambda: eng_mid.go(3, u - 2))
                pl.when(i != 1)(lambda: eng_mid.go(4, jnp.where(i == 0, n - 2, u - 3)))
                pl.when(i + 1 < nt_)(lambda: act_on(load_mid(u + 1), "start"))
                act_on(fetch(i, s), "wait")
                pl.when(i >= 1)(lambda: put_out(i - 1).wait())
                ost[...] = obuf[r, :] * msk_ref[r, 2:3]
                put_out(i).start()
                v = ld[s, 3]
                g = gn[r, :]
                inv = inverse_rms(v)
                a = g * vec[1:2, :]
                dot = jnp.sum(a * v, axis=1, keepdims=True) / dim
                ghid = gf[r, :].astype(F32) + (inv * a - v * (inv * inv * inv) * dot)
                sm[1:2, :] += jnp.sum(g * v * inv, axis=0, keepdims=True)
                gn[r, :] = ghid
                low = ghid.astype(BF)
                nf[r, :] = low
                gm = dg(low, wout[...].reshape(dim, dim), 1, 1)
                tb[8 : 8 + tt, :] = ld[s, 0] * ld[s, 2]
                k1, k2 = msk_ref[r, 0:1], msk_ref[r, 1:2]
                gated, lag1, lag2 = tb[8 : 8 + tt, :], k1 * tb[7 : 7 + tt, :], k2 * tb[6 : 6 + tt, :]
                conv = vec[4:5, :] * gated + vec[3:4, :] * lag1 + vec[2:3, :] * lag2
                gp[r, 1024:2048] = (gm * conv).astype(BF)
                gc = gm * ld[s, 1]
                obuf[r, :] = gc
                sm[2:3, :] += jnp.sum(gc * lag2, axis=0, keepdims=True)
                sm[3:4, :] += jnp.sum(gc * lag1, axis=0, keepdims=True)
                sm[4:5, :] += jnp.sum(gc * gated, axis=0, keepdims=True)
                tb[0:8, :] = tb[tt : tt + 8, :]

                @pl.when(i == 0)
                def _():
                    first, second = obuf[0:1, :], obuf[1:2, :]
                    k1a, k2a, k2b = msk_ref[0:1, 0:1], msk_ref[0:1, 1:2], msk_ref[1:2, 1:2]
                    edge_s[6:7, :] = vec[2:3, :] * (k2a * first)
                    edge_s[7:8, :] = vec[3:4, :] * (k1a * first) + vec[2:3, :] * (k2b * second)
                    edge.start()

                pl.when(i >= 1)(lambda: two(i - 1, 1 - s))

                @pl.when(i + 1 < nt_)
                def _():
                    act_on(fetch(i + 1, 1 - s), "start")
                    act_on(load_mid(u + 1), "wait")
                    eng_mid.begin(u + 1)

                pl.when(i != 1)(lambda: eng_mid.end(jnp.where(i == 0, n - 2, u - 3)))
                return 0

            lax.fori_loop(0, nt_, one, 0)
            mcopy.wait()
            part_of(ndn)
            eng(ndn).begin(ndn)
            put_out(nt_ - 1).wait()
            edge.wait()
            two(nt_ - 1, (nt_ - 1) % 2)

        edge = remote(edge_s, edge_r, hsem.at[3], hsem.at[4], pc.zs[2])
        pl.run_scoped(passes, pltpu.VMEM((2, 4, tt, dim), F32), pltpu.VMEM((tt, dim), F32),
                      pltpu.VMEM((tt + 8, dim), F32), pltpu.VMEM((tt + 8, dim), F32))

        def ending(win, ost):
            wl = [pltpu.make_async_copy(win_h.at[:, :, pl.ds(1024 * i, 1024)], win.at[i], lsem.at[0, i]) for i in range(3)]
            act_on(wl, "start")

            def put_tok(i, s):
                return pltpu.make_async_copy(ost.at[s], gtok_ref.at[cols(i, tt)], lsem.at[s, 4])

            def grad_tok(i, _):
                s = lax.rem(i, 2)
                r = cols(i, tt)
                g = dg(gp[r, 0:1024], win[0].reshape(dim, dim), 1, 1)
                g = g + dg(gp[r, 1024:2048], win[1].reshape(dim, dim), 1, 1)
                g = g + dg(gp[r, 2048:3072], win[2].reshape(dim, dim), 1, 1)
                v = tok_ref[r, :].astype(F32)
                inv = inverse_rms(v)
                a = g * vec[0:1, :]
                dot = jnp.sum(a * v, axis=1, keepdims=True) / dim
                pl.when(i >= 2)(lambda: put_tok(i - 2, s).wait())
                ost[s] = gn[r, :] + (inv * a - v * (inv * inv * inv) * dot)
                put_tok(i, s).start()
                sm[0:1, :] += jnp.sum(g * v * inv, axis=0, keepdims=True)
                return 0

            for u in range(ndn, ndn + 8):
                advance(u)
                if u < ndn + 4:
                    part_of(u + 1)
                    eng(u + 1).begin(u + 1)
                if u == ndn:
                    act_on(wl, "wait")
                if u in (ndn + 1, ndn + 2):
                    lax.fori_loop(2 * (u - ndn - 1), 2 * (u - ndn), grad_tok, 0)
                if u == ndn + 2:
                    small_begin(0)
                elif u > ndn + 2 and u < ndn + 6:
                    small_end(u - ndn - 3)
                    small_begin(u - ndn - 2)
                elif u == ndn + 6:
                    small_end(3)
                    outs = pltpu.make_async_copy(sm, small_o, hsem.at[0])
                    outs.start()
                eng(u - 3).end(u - 3)
            outs.wait()
            for i in (nt_ - 2, nt_ - 1):
                put_tok(i, i % 2).wait()

        pl.run_scoped(ending, pltpu.VMEM((3, 32, 32, dim), BF), pltpu.VMEM((2, tt, dim), F32))

    pl.run_scoped(mixer_backward, pltpu.VMEM((tok, 3 * dim), BF), pltpu.VMEM((dim, tok), BF), pltpu.VMEM((32, 32, dim), BF))

    for u in range(9):
        unit(u).fin()

    def last(j, carry):
        gu_unit(j).fin()
        return carry

    lax.fori_loop(0, n, last, 0)


def block_call(tokens, cot, lengths, counts, vecs, w_in, w_out, w_gate, w_up, w_down):
    tok, dim = tokens.shape
    ff = w_gate.shape[1]
    n = ff // 512
    sd = jax.ShapeDtypeStruct
    outs = [
        sd((tok, dim), F32), sd((tok, dim), F32), sd((32, ff), F32), sd((32, ff), F32), sd((ff // 32, dim), F32),
        sd((32, dim), F32), sd((32, 3 * dim), F32), sd((8, dim), F32),
        sd((32, 32, 3 * dim), BF), sd((32, 32, dim), BF), sd((ff, dim), BF), sd((32, 2, 32, ff), BF),
        sd((32, 8, 128), F32), sd((3, tok, dim), F32), sd((tok, dim), F32), sd((tok, dim), BF), sd((ff, dim), BF),
    ]
    return pl.pallas_call(
        block_kernel,
        out_shape=outs,
        in_specs=[VM, ANY, VM, pl.BlockSpec(memory_space=pltpu.SMEM), VM, ANY, ANY, ANY, ANY, ANY],
        out_specs=[ANY] * len(outs),
        scratch_shapes=[
            pltpu.VMEM((tok + 8, dim), F32),
            pltpu.VMEM((tok, dim), F32),
            pltpu.VMEM((tok, dim), BF),
            pltpu.VMEM((tok, dim), BF),
            pltpu.VMEM((tok, dim), BF),
            pltpu.VMEM((tok, 128), F32),
            pltpu.VMEM((8, dim), F32),
            pltpu.VMEM((1, 8, 128), F32),
            pltpu.VMEM((8, dim), F32),
            pltpu.VMEM((6, 8, dim), F32),
            pltpu.VMEM((16, dim), BF),
            pltpu.VMEM((8, dim), F32),
            pltpu.VMEM((8, dim), F32),
            pltpu.VMEM((8, dim), F32),
            pltpu.SemaphoreType.DMA((4,)),
            pltpu.SemaphoreType.DMA((2, 5)),
            pltpu.SemaphoreType.DMA((5,)),
            pltpu.SemaphoreType.DMA((12,)),
            pltpu.SemaphoreType.DMA((n + 9, NG)),
            pltpu.SemaphoreType.DMA((n + 9, NG)),
        ] + scatter_scratch(n + 9, 32, 512),
        name="block",
        compiler_params=pltpu.CompilerParams(collective_id=1, has_side_effects=True, vmem_limit_bytes=62 * 2**20 + 2**19),
    )(tokens, cot, lengths, counts, vecs, w_in[None], w_out[None], w_gate[None], w_up[None], w_down)


def passed_along(array, axis, by):
    size = lax.axis_size(axis)
    pairs = [(i, i + by) for i in range(size) if 0 <= i + by < size]
    return lax.ppermute(array, axis, pairs)


def rms_forward(values, gain_vec):
    inv_rms = lax.rsqrt(jnp.mean(values * values, axis=1, keepdims=True) + epsilon)
    return (values * inv_rms * gain_vec[None, :], inv_rms)


def rms_backward(values, inv_rms, gain_vec, grad_normed):
    weighted = grad_normed * gain_vec[None, :]
    features = values.shape[1]
    total_dot = jnp.sum(weighted * values, axis=1, keepdims=True)
    grad_values = inv_rms * weighted - values * (inv_rms * inv_rms * inv_rms) * total_dot / features
    grad_gain = jnp.sum(grad_normed * values * inv_rms, axis=0)
    return (grad_values, grad_gain)


def outer_sum(left, right):
    return lax.dot_general(
        left, right, (((0,), (0,)), ((), ())), preferred_element_type=jnp.float32
    )


def back_product(grad_low, weight_mat):
    return lax.dot_general(
        grad_low, weight_mat, (((1,), (1,)), ((), ())), preferred_element_type=jnp.float32
    )


def doc_masks(doc_lengths, valid_count, first_pos, tok_count):
    packed_row = first_pos // ROW_LEN
    lengths = lax.dynamic_index_in_dim(doc_lengths, packed_row, 0, keepdims=False)
    limit_count = lax.dynamic_index_in_dim(valid_count, packed_row, 0, keepdims=False)
    offsets = jnp.cumsum(lengths) - lengths
    places = first_pos % ROW_LEN + jnp.arange(tok_count, dtype=jnp.int32)
    begins = jnp.any(offsets[None, :] == places[:, None], axis=1)
    before = jnp.any(offsets[None, :] == places[:, None] - 1, axis=1)
    keep_one = jnp.where(begins, 0.0, 1.0).astype(jnp.float32)
    keep_two = jnp.where(begins | before, 0.0, 1.0).astype(jnp.float32)
    live_mask = jnp.where(places < limit_count, 1.0, 0.0).astype(jnp.float32)
    return (keep_one[:, None], keep_two[:, None], live_mask[:, None])


def shards_plain(
    tokens,
    cotangent,
    gain_mix,
    in_weight,
    conv_taps,
    out_weight,
    gain_ffn,
    gate_weight,
    up_weight,
    down_weight,
    doc_lengths,
    valid_count,
):
    tok_count = tokens.shape[0]
    first_pos = lax.axis_index(("wide", "narrow")) * tok_count
    keep_one, keep_two, live_mask = doc_masks(doc_lengths, valid_count, first_pos, tok_count)
    full_gm, w_in, full_taps, w_out, full_gf, w_gate, w_up, w_down = (
        lax.all_gather(gain_mix, ("wide", "narrow"), axis=0, tiled=True),
        lax.all_gather(in_weight, ("wide", "narrow"), axis=0, tiled=True),
        lax.all_gather(conv_taps, ("wide", "narrow"), axis=1, tiled=True),
        lax.all_gather(out_weight, ("wide", "narrow"), axis=0, tiled=True),
        lax.all_gather(gain_ffn, ("wide", "narrow"), axis=0, tiled=True),
        lax.all_gather(gate_weight, ("wide", "narrow"), axis=0, tiled=True),
        lax.all_gather(up_weight, ("wide", "narrow"), axis=0, tiled=True),
        lax.all_gather(down_weight, ("wide", "narrow"), axis=0, tiled=True),
    )
    mix_gain = full_gm.astype(jnp.float32)
    ffn_gain = full_gf.astype(jnp.float32)
    taps = full_taps.astype(jnp.float32)
    features = tokens.shape[1]
    tok_float = tokens.astype(jnp.float32)
    normed_mix, inv_mix = rms_forward(tok_float, mix_gain)
    normed_low = normed_mix.astype(jnp.bfloat16)
    projected = jnp.dot(normed_low, w_in, preferred_element_type=jnp.float32)
    b_part = projected[:, :features]
    c_part = projected[:, features : 2 * features]
    x_part = projected[:, 2 * features :]
    gated = b_part * x_part
    edge_rows = passed_along(gated[-2:], "narrow", 1)
    extended = jnp.concatenate([edge_rows, gated], axis=0)
    lag_one = keep_one * extended[1:-1]
    lag_two = keep_two * extended[:-2]
    conv_out = taps[2][None, :] * gated + taps[1][None, :] * lag_one + taps[0][None, :] * lag_two
    mixed_low = (c_part * conv_out).astype(jnp.bfloat16)
    hidden_res = tok_float + jnp.dot(mixed_low, w_out, preferred_element_type=jnp.float32)
    normed_ffn, inv_ffn = rms_forward(hidden_res, ffn_gain)
    ffn_low = normed_ffn.astype(jnp.bfloat16)
    gate_val = jnp.dot(ffn_low, w_gate, preferred_element_type=jnp.float32)
    up_val = jnp.dot(ffn_low, w_up, preferred_element_type=jnp.float32)
    sigmoid_gate = jax.nn.sigmoid(gate_val)
    silu_val = gate_val * sigmoid_gate
    act_low = (silu_val * up_val).astype(jnp.bfloat16)
    ffn_out = jnp.dot(act_low, w_down, preferred_element_type=jnp.float32)
    output = live_mask * (hidden_res + ffn_out)
    again_gm, w_in, again_taps, w_out, again_gf, w_gate, w_up, w_down = (
        lax.all_gather(gain_mix, ("wide", "narrow"), axis=0, tiled=True),
        lax.all_gather(in_weight, ("wide", "narrow"), axis=0, tiled=True),
        lax.all_gather(conv_taps, ("wide", "narrow"), axis=1, tiled=True),
        lax.all_gather(out_weight, ("wide", "narrow"), axis=0, tiled=True),
        lax.all_gather(gain_ffn, ("wide", "narrow"), axis=0, tiled=True),
        lax.all_gather(gate_weight, ("wide", "narrow"), axis=0, tiled=True),
        lax.all_gather(up_weight, ("wide", "narrow"), axis=0, tiled=True),
        lax.all_gather(down_weight, ("wide", "narrow"), axis=0, tiled=True),
    )
    mix_gain = again_gm.astype(jnp.float32)
    ffn_gain = again_gf.astype(jnp.float32)
    taps = again_taps.astype(jnp.float32)
    grad_res = live_mask * cotangent.astype(jnp.float32)
    grad_ffn_low = grad_res.astype(jnp.bfloat16)
    grad_down = outer_sum(act_low, grad_ffn_low)
    grad_act = back_product(grad_ffn_low, w_down)
    grad_gate_low = (
        grad_act * up_val * sigmoid_gate * (1.0 + gate_val * (1.0 - sigmoid_gate))
    ).astype(jnp.bfloat16)
    grad_up_low = (grad_act * silu_val).astype(jnp.bfloat16)
    grad_gate = outer_sum(ffn_low, grad_gate_low)
    grad_up = outer_sum(ffn_low, grad_up_low)
    grad_nffn = back_product(grad_gate_low, w_gate) + back_product(grad_up_low, w_up)
    grad_hnorm, grad_gf = rms_backward(hidden_res, inv_ffn, ffn_gain, grad_nffn)
    grad_hidden = grad_res + grad_hnorm
    grad_mix_low = grad_hidden.astype(jnp.bfloat16)
    grad_out = outer_sum(mixed_low, grad_mix_low)
    grad_mixed = back_product(grad_mix_low, w_out)
    grad_c = grad_mixed * conv_out
    grad_conv = grad_mixed * c_part
    grad_taps = jnp.stack(
        [
            jnp.sum(grad_conv * lag_two, axis=0),
            jnp.sum(grad_conv * lag_one, axis=0),
            jnp.sum(grad_conv * gated, axis=0),
        ],
        axis=0,
    )
    lag_grad_one = taps[1][None, :] * keep_one * grad_conv
    lag_grad_two = taps[0][None, :] * keep_two * grad_conv
    grad_ext = (
        jnp.pad(taps[2][None, :] * grad_conv, ((2, 0), (0, 0)))
        + jnp.pad(lag_grad_one, ((1, 1), (0, 0)))
        + jnp.pad(lag_grad_two, ((0, 2), (0, 0)))
    )
    from_right = passed_along(grad_ext[:2], "narrow", -1)
    grad_gated = jnp.concatenate([grad_ext[2:-2], grad_ext[-2:] + from_right], axis=0)
    grad_b = grad_gated * x_part
    grad_x = grad_gated * b_part
    grad_proj_low = jnp.concatenate([grad_b, grad_c, grad_x], axis=1).astype(jnp.bfloat16)
    grad_in = outer_sum(normed_low, grad_proj_low)
    grad_nmix = back_product(grad_proj_low, w_in)
    grad_tnorm, grad_gm = rms_backward(tok_float, inv_mix, mix_gain, grad_nmix)
    grad_tokens = grad_hidden + grad_tnorm
    sum_gm, sum_in, sum_taps, sum_out, sum_gf, sum_gate, sum_up, sum_down = (
        lax.psum_scatter(grad_gm, ("wide", "narrow"), scatter_dimension=0, tiled=True),
        lax.psum_scatter(grad_in, ("wide", "narrow"), scatter_dimension=0, tiled=True),
        lax.psum_scatter(grad_taps, ("wide", "narrow"), scatter_dimension=1, tiled=True),
        lax.psum_scatter(grad_out, ("wide", "narrow"), scatter_dimension=0, tiled=True),
        lax.psum_scatter(grad_gf, ("wide", "narrow"), scatter_dimension=0, tiled=True),
        lax.psum_scatter(grad_gate, ("wide", "narrow"), scatter_dimension=0, tiled=True),
        lax.psum_scatter(grad_up, ("wide", "narrow"), scatter_dimension=0, tiled=True),
        lax.psum_scatter(grad_down, ("wide", "narrow"), scatter_dimension=0, tiled=True),
    )
    return (
        output,
        grad_tokens,
        sum_gm,
        sum_in,
        sum_taps,
        sum_out,
        sum_gf,
        sum_gate,
        sum_up,
        sum_down,
    )


def shards(
    tokens, cotangent, gain_mix, in_weight, conv_taps, out_weight, gain_ffn,
    gate_weight, up_weight, down_weight, doc_lengths, valid_count,
):
    me = lax.axis_index(("wide", "narrow"))
    own = gain_mix.shape[0]
    vecs = jnp.concatenate([gain_mix[None], gain_ffn[None], conv_taps], axis=0).astype(F32)
    vecs = jnp.pad(vecs, ((0, 3), (0, 128 - own)))
    lengths = jnp.pad(doc_lengths, ((0, 0), (0, 128 - doc_lengths.shape[1])))
    output, grad_tokens, sum_gate, sum_up, sum_down, sum_out, sum_in, all_small = block_call(
        tokens, cotangent, lengths, valid_count, vecs, in_weight, out_weight, gate_weight, up_weight, down_weight
    )[:8]
    mine = lax.dynamic_slice_in_dim(all_small, me * own, own, 1)
    return (output, grad_tokens, mine[0], sum_in, mine[2:5], sum_out, mine[1], sum_gate, sum_up, sum_down)


def solution(mesh):
    both = ("wide", "narrow")
    rows, vec, flat = P(both, None), P(both), P(None, both)
    step = shards if (mesh.shape["wide"], mesh.shape["narrow"]) == (8, 4) else shards_plain
    return jax.shard_map(
        step,
        mesh=mesh,
        in_specs=(rows, rows, vec, rows, flat, rows, vec, rows, rows, rows, P(), P()),
        out_specs=(rows, rows, vec, rows, flat, rows, vec, rows, rows, rows),
        check_vma=False,
    )
```

```python
import functools

import jax
import jax.numpy as jnp
from jax import lax
from jax.experimental import pallas as pl
from jax.experimental.pallas import tpu as pltpu
from jax.sharding import PartitionSpec as P

ROW_LEN = 4096
epsilon = 1e-05
F32 = jnp.float32
BF = jnp.bfloat16
MESH = pl.DeviceIdType.MESH
ANY = pl.BlockSpec(memory_space=pl.ANY)
VM = pl.BlockSpec(memory_space=pltpu.VMEM)


def dg(a, b, ca, cb):
    return lax.dot_general(a, b, (((ca,), (cb,)), ((), ())), preferred_element_type=F32)


class Place:
    def __init__(self):
        w = lax.axis_index("wide")
        z = lax.axis_index("narrow")
        c = lax.rem(w, 2)
        x = lax.rem(w // 2, 2)
        y = w // 4
        self.w, self.z, self.c, self.x, self.y = w, z, c, x, y
        self.core = (w + 1 - 2 * c, z)
        self.xn = (w + 2 - 4 * x, z)
        self.yn = (w + 4 - 8 * y, z)
        self.zs = [(w, lax.rem(z + k, 4)) for k in (1, 2, 3)]
        self.zto = [lax.rem(z + k, 4) for k in (1, 2, 3)]
        self.zfrom = [lax.rem(z + 4 - k, 4) for k in (1, 2, 3)]

        def base(yy, xx, cc):
            return 16 * yy + 8 * xx + 4 * cc

        self.own, self.xb = base(y, x, c), base(y, 1 - x, c)
        self.yb, self.db = base(1 - y, x, c), base(1 - y, 1 - x, c)
        self.sown, self.sxb = base(y, x, 1 - c), base(y, 1 - x, 1 - c)
        self.syb, self.sdb = base(1 - y, x, 1 - c), base(1 - y, 1 - x, 1 - c)
        self.me = self.own + z

    def greet(self):
        bar = pltpu.get_barrier_semaphore()
        peers = [self.core, self.xn, self.yn] + self.zs
        for p in peers:
            pl.semaphore_signal(bar, inc=1, device_id=p, device_id_type=MESH)
        pl.semaphore_wait(bar, len(peers))


def remote(src, dst, ss, rs, dev):
    return pltpu.make_async_remote_copy(
        src_ref=src, dst_ref=dst, send_sem=ss, recv_sem=rs, device_id=dev, device_id_type=MESH
    )


class Gather:
    def __init__(self, pc, src, dst, full, ss, rs):
        self.pc, self.src, self.dst, self.full, self.ss, self.rs = pc, src, dst, full, ss, rs
        self.parts = range(len(src))

    def zc(self, i, k):
        q = 3 * i + k
        return remote(self.src[i](), self.dst[i](self.pc.me, 1), self.ss.at[q], self.rs.at[q], self.pc.zs[k])

    def zr(self, i, k):
        q = 3 * i + k
        v = self.dst[i](self.pc.own + self.pc.zfrom[k], 1)
        return remote(v, v, self.ss.at[q], self.rs.at[q], self.pc.zs[k])

    def loc(self, i):
        return pltpu.make_async_copy(self.src[i](), self.dst[i](self.pc.me, 1), self.ss.at[14 + i])

    def cp(self, k, b, n, dev):
        v = self.full(b, n)
        return remote(v, v, self.ss.at[k], self.rs.at[k], dev)

    def s0(self):
        for i in self.parts:
            self.loc(i).start()
            for k in range(3):
                self.zc(i, k).start()

    def s1(self):
        p = self.pc
        for i in self.parts:
            self.loc(i).wait()
            for k in range(3):
                self.zr(i, k).wait_recv()
        self.cp(6, p.own, 4, p.xn).start()
        self.cp(7, p.own, 4, p.yn).start()
        self.cp(8, p.own, 4, p.core).start()

    def s2(self):
        p = self.pc
        self.cp(6, p.xb, 4, p.xn).wait_recv()
        self.cp(9, p.xb, 2, p.yn).start()
        self.cp(10, p.xb, 4, p.core).start()
        self.cp(7, p.yb, 4, p.yn).wait_recv()
        self.cp(11, p.yb + 2, 2, p.xn).start()
        self.cp(12, p.yb, 4, p.core).start()

    def s3(self):
        p = self.pc
        self.cp(9, p.db, 2, p.yn).wait_recv()
        self.cp(11, p.db + 2, 2, p.xn).wait_recv()
        self.cp(13, p.db, 4, p.core).start()

    def s4(self):
        p = self.pc
        for k, b in ((8, p.sown), (10, p.sxb), (12, p.syb), (13, p.sdb)):
            self.cp(k, b, 4, p.core).wait_recv()

    def fin(self):
        p = self.pc
        for i in self.parts:
            for k in range(3):
                self.zc(i, k).wait_send()
        for k, b, n in (
            (6, p.own, 4), (7, p.own, 4), (8, p.own, 4), (9, p.xb, 2),
            (10, p.xb, 4), (11, p.yb + 2, 2), (12, p.yb, 4), (13, p.db, 4),
        ):
            self.cp(k, b, n, p.core).wait_send()


NG = 16
NL = 4
AHEAD = 2
NS = 4


class Scatter:
    def __init__(self, pc, bufs, h, out):
        self.pc, self.h, self.out = pc, h, out
        (self.part, self.l0, self.ldx, self.ldy, self.lx, self.ly, self.lz,
         self.sd, self.sx, self.sy, self.so, self.sz, self.ob, self.ss, self.rs, self.os) = bufs

    def hr(self):
        return pl.ds(0, self.h)

    def c0(self, j, s):
        p = self.pc
        return remote(self.part.at[lax.rem(j, 2), :, :, :, 1 - p.c, :, self.hr()], self.l0.at[lax.rem(j, 3), :, :, :, :, self.hr()],
                      self.ss.at[j, 0], self.rs.at[j, 0], p.core)

    def cdx(self, j, s):
        return remote(self.sd.at[lax.rem(j, 2), :, pl.ds(0, 2), self.hr()], self.ldx.at[lax.rem(j, NL), :, :, self.hr()],
                      self.ss.at[j, 1], self.rs.at[j, 1], self.pc.xn)

    def cdy(self, j, s):
        return remote(self.sd.at[lax.rem(j, 2), :, pl.ds(2, 2), self.hr()], self.ldy.at[lax.rem(j, NL), :, :, self.hr()],
                      self.ss.at[j, 2], self.rs.at[j, 2], self.pc.yn)

    def cx(self, j, s):
        return remote(self.sx.at[s, :, :, self.hr()], self.lx.at[lax.rem(j, NL), :, :, self.hr()],
                      self.ss.at[j, 3], self.rs.at[j, 3], self.pc.xn)

    def cy(self, j, s):
        return remote(self.sy.at[s, :, :, self.hr()], self.ly.at[lax.rem(j, NL), :, :, self.hr()],
                      self.ss.at[j, 4], self.rs.at[j, 4], self.pc.yn)

    def cz(self, j, s, k):
        return remote(self.sz.at[lax.rem(j, 2), :, self.pc.zto[k], self.hr()], self.lz.at[lax.rem(j, NL), k, :, self.hr()],
                      self.ss.at[j, 5 + k], self.rs.at[j, 5 + k], self.pc.zs[k])

    def r0(self, j, s):
        self.c0(j, s).start()

    def q(self, j, s, a, yy, xx):
        hr = self.hr()
        return (self.part[lax.rem(j, 2), a, yy, xx, self.pc.c, :, hr].astype(F32)
                + self.l0[lax.rem(j, 3), a, yy, xx, :, hr].astype(F32))

    def r1(self, j, s):
        p, hr = self.pc, self.hr()
        self.c0(j, s).wait()
        for a in range(2):
            self.sd[lax.rem(j, 2), a, :, hr] = self.q(j, s, a, 1 - p.y, 1 - p.x).astype(BF)
        self.cdx(j, s).start()
        self.cdy(j, s).start()
        for a in range(2):
            self.sx[s, a, :, hr] = self.q(j, s, a, p.y, 1 - p.x).astype(BF)
            self.sy[s, a, :, hr] = self.q(j, s, a, 1 - p.y, p.x).astype(BF)
            self.so[s, a, :, hr] = self.q(j, s, a, p.y, p.x)

    def r2(self, j, s):
        hr = self.hr()
        lo, hi = pl.ds(0, 2), pl.ds(2, 2)
        self.cdx(j, s).wait()
        for a in range(2):
            self.sy[s, a, lo, hr] = (self.sy[s, a, lo, hr].astype(F32) + self.ldx[lax.rem(j, NL), a, :, hr].astype(F32)).astype(BF)
        self.cy(j, s).start()
        self.cdy(j, s).wait()
        for a in range(2):
            self.sx[s, a, hi, hr] = (self.sx[s, a, hi, hr].astype(F32) + self.ldy[lax.rem(j, NL), a, :, hr].astype(F32)).astype(BF)
        self.cx(j, s).start()

    def r3(self, j, s):
        hr = self.hr()
        self.cy(j, s).wait()
        self.cx(j, s).wait()
        for a in range(2):
            t = self.so[s, a, :, hr] + self.lx[lax.rem(j, NL), a, :, hr].astype(F32) + self.ly[lax.rem(j, NL), a, :, hr].astype(F32)
            self.so[s, a, :, hr] = t
            self.sz[lax.rem(j, 2), a, :, hr] = t.astype(BF)
        for k in range(3):
            self.cz(j, s, k).start()

    def r4(self, j, s):
        hr = self.hr()
        for k in range(3):
            self.cz(j, s, k).wait()
        for a in range(2):
            t = self.so[s, a, self.pc.z, hr]
            for k in range(3):
                t = t + self.lz[lax.rem(j, NL), k, a, hr].astype(F32)
            self.ob[s, a, hr] = t
        self.out(j, s, self.ob, self.os, "start")

    def go(self, stage, j):
        (self.r1, self.r2, self.r3, self.r4)[stage - 1](j, lax.rem(j, NS))

    def begin(self, j):
        self.r0(j, lax.rem(j, NS))

    def end(self, j):
        self.drain(j, lax.rem(j, NS))

    def drain(self, j, s):
        self.out(j, s, self.ob, self.os, "wait")


def scatter_scratch(n, h, w):
    return [
        pltpu.VMEM((2, 2, 2, 2, 2, 4, h, w), BF),
        pltpu.VMEM((3, 2, 2, 2, 4, h, w), BF),
        pltpu.VMEM((NL, 2, 2, h, w), BF),
        pltpu.VMEM((NL, 2, 2, h, w), BF),
        pltpu.VMEM((NL, 2, 4, h, w), BF),
        pltpu.VMEM((NL, 2, 4, h, w), BF),
        pltpu.VMEM((NL, 3, 2, h, w), BF),
        pltpu.VMEM((2, 2, 4, h, w), BF),
        pltpu.VMEM((NS, 2, 4, h, w), BF),
        pltpu.VMEM((NS, 2, 4, h, w), BF),
        pltpu.VMEM((NS, 2, 4, h, w), F32),
        pltpu.VMEM((2, 2, 4, h, w), BF),
        pltpu.VMEM((NS, 2, h, w), F32),
        pltpu.SemaphoreType.DMA((n, 8)),
        pltpu.SemaphoreType.DMA((n, 8)),
        pltpu.SemaphoreType.DMA((NS, 2)),
    ]


def inverse_rms(v):
    return lax.rsqrt(jnp.mean(v * v, axis=1, keepdims=True) + epsilon)


def block_kernel(
    tok_ref, cot_ref, doc_ref, count_ref, vec_ref, win_s, wout_s, wgate_s, wup_s, wdown_s,
    out_ref, gtok_ref, ggate_o, gup_o, gdown_o, gout_o, gin_o, small_o,
    win_h, wout_h, wd_h, wgu_h, vec_h, bcx_h, hid_h, mix_h, gdown_h,
    obuf, gn, nf, gf, nm, msk_ref, vec, vown, sm, sml, halo_t, halo_g, edge_s, edge_r,
    vsem, lsem, hsem, esem, gss, grs, *sc,
):
    pc = Place()
    tok, dim = tok_ref.shape
    ff = wgate_s.shape[-1]
    f = 512
    n = ff // f
    tt = 256
    nt_ = tok // tt
    part = sc[0]

    def cols(j, w=f):
        return pl.ds(pl.multiple_of(j * w, w), w)

    def simple(u, src, dst, c0, w):
        at = lambda b, m: dst.at[pl.ds(b, m), :, pl.ds(c0, w)]
        return Gather(pc, [lambda: src.at[:, :, pl.ds(c0, w)]], [at], at, gss.at[u], grs.at[u])

    def down_unit(i):
        rows = ff // 32
        at = lambda b, m: wd_h.at[pl.ds(pl.multiple_of(b * rows, rows), m * rows), pl.ds(256 * i, 256)]
        return Gather(pc, [lambda: wdown_s.at[:, pl.ds(256 * i, 256)]], [at], at, gss.at[5 + i], grs.at[5 + i])

    def gu_unit(j):
        srcs = [lambda: wgate_s.at[:, :, cols(j)], lambda: wup_s.at[:, :, cols(j)]]
        dsts = [lambda b, m: wgu_h.at[pl.ds(b, m), 0, :, cols(j)], lambda b, m: wgu_h.at[pl.ds(b, m), 1, :, cols(j)]]
        return Gather(pc, srcs, dsts, lambda b, m: wgu_h.at[pl.ds(b, m), :, :, cols(j)], gss.at[9 + j], grs.at[9 + j])

    def unit(u):
        if u == 0:
            return simple(0, vown, vec_h, 0, 128)
        if u < 4:
            return simple(u, win_s, win_h, 1024 * (u - 1), 1024)
        if u == 4:
            return simple(4, wout_s, wout_h, 0, 1024)
        if u < 9:
            return down_unit(u - 5)
        return gu_unit(u - 9)

    def small_copies(k):
        peers = [pc.core, pc.xn, pc.yn] + pc.zs
        return [remote(sm, sml.at[q], esem.at[q], esem.at[6 + q], peers[q]) for q in ((0,), (1,), (2,), (3, 4, 5))[k]]

    def small_begin(k):
        for c in small_copies(k):
            c.start()

    def small_end(k):
        for c in small_copies(k):
            c.wait()
        t = sm[...]
        for q in ((0,), (1,), (2,), (3, 4, 5))[k]:
            t = t + sml[q]
        sm[...] = t

    def step(t):
        if t < 11:
            unit(t).s1()
            unit(t + AHEAD).s0()
        if t >= 2 and t < 11:
            unit(t - 1).s2()
        if t >= 3 and t < 12:
            unit(t - 2).s3()
        if t >= 4:
            unit(t - 3).s4()

    ndn = n + 4
    gdown6 = gdown_h.reshape(2, 2, 2, 4, ff // 32, dim)

    def act_on(copies, what):
        for c in copies:
            getattr(c, what)()

    def out_gu(j, s, ob, osem, what):
        act_on([pltpu.make_async_copy(ob.at[s, 0], ggate_o.at[:, cols(j)], osem.at[s, 0]),
                pltpu.make_async_copy(ob.at[s, 1], gup_o.at[:, cols(j)], osem.at[s, 1])], what)

    def out_rows(dst, r0, c0, h):
        def go(j, s, ob, osem, what):
            act_on([pltpu.make_async_copy(ob.at[s, a, pl.ds(0, h)],
                                          dst.at[pl.ds(r0, h), pl.ds(c0 + 512 * a, 512)], osem.at[s, a])
                    for a in range(2)], what)
        return go

    def out_down(j, s, ob, osem, what):
        out_rows(gdown_o, pl.multiple_of((j - n) * 32, 32), 0, 32)(j, s, ob, osem, what)

    def out_mixed(j, s, ob, osem, what):
        pl.when(j < n)(lambda: out_gu(j, s, ob, osem, what))
        pl.when(j >= n)(lambda: out_down(j, s, ob, osem, what))

    eng_gu = Scatter(pc, sc, 32, out_gu)
    eng_mid = Scatter(pc, sc, 32, out_mixed)
    order = (1, 0, 2)

    def eng(u):
        if u < ndn:
            return Scatter(pc, sc, 32, out_down)
        if u == ndn:
            return Scatter(pc, sc, 32, out_rows(gout_o, 0, 0, 32))
        if u < ndn + 4:
            return Scatter(pc, sc, 32, out_rows(gin_o, 0, 1024 * order[u - ndn - 1], 32))
        return Scatter(pc, sc, 16, out_rows(gdown_o, 128, 0, 16))

    pc.greet()
    vown[0] = pltpu.roll(vec_ref[...], 32 * pc.z, 1)
    unit(0).s0()
    unit(1).s0()
    cot_copy = pltpu.make_async_copy(cot_ref, gf, hsem.at[0])
    cot_copy.start()
    tail = remote(tok_ref.at[pl.ds(tok - 16, 16)], halo_t, hsem.at[1], hsem.at[2], pc.zs[0])
    tail.start()
    sm[...] = jnp.zeros_like(sm)
    edge_s[...] = jnp.zeros_like(edge_s)
    gn[...] = jnp.zeros_like(gn)
    row_devs = ROW_LEN // tok
    row = pc.me // row_devs
    lens = jnp.broadcast_to(doc_ref[pl.ds(row, 1), :], (8, 128))
    lane = lax.broadcasted_iota(jnp.int32, (8, 128), 1)
    sums = lens
    for k in (1, 2, 4, 8):
        sums = sums + jnp.where(lane >= k, pltpu.roll(sums, k, 1), 0)
    starts = jnp.where(lane < 16, sums - lens, -8)[0:1, :]
    limit = count_ref[row]
    cot_copy.wait()

    def live_rows(i, _):
        r = cols(i, tt)
        t = i * tt + lax.broadcasted_iota(jnp.int32, (tt, 128), 0)
        place = lax.rem(pc.me, row_devs) * tok + t

        def begins(by):
            return jnp.max(jnp.where(starts == place + by, 1.0, 0.0), axis=1, keepdims=True)

        b0, b1, b2, bm = begins(0), begins(1), begins(2), begins(-1)
        ln = lax.broadcasted_iota(jnp.int32, (tt, 128), 1)
        m = jnp.where(ln == 0, 1.0 - b0, 1.0 - jnp.maximum(b0, bm))
        m = jnp.where(ln == 2, jnp.where(place < limit, 1.0, 0.0), m)
        m = jnp.where(ln == 3, jnp.where(t + 1 < tok, 1.0 - b1, 0.0), m)
        msk_ref[r, :] = jnp.where(ln == 4, jnp.where(t + 2 < tok, 1.0 - jnp.maximum(b2, b1), 0.0), m)
        gf[r, :] = (gf[r, :].astype(F32) * msk_ref[r, 2:3]).astype(BF)
        return 0

    lax.fori_loop(0, nt_, live_rows, 0)
    unit(0).s1()
    unit(2).s0()
    unit(0).s2()
    unit(0).s3()
    unit(1).s1()
    unit(3).s0()
    unit(0).s4()

    def mixer_forward(vbuf, win, wout, st, mst, tb):
        vcopy = pltpu.make_async_copy(vec_h, vbuf, vsem.at[0])
        vcopy.start()
        vcopy.wait()
        for q in range(8):
            v = vbuf[4 * q] + vbuf[4 * q + 1] + vbuf[4 * q + 2] + vbuf[4 * q + 3]
            vec[:, 128 * q : 128 * q + 128] = v
        gain = vec[0:1, :]

        def normed(i, _):
            r = cols(i, tt)
            t = tok_ref[r, :].astype(F32)
            nm[r, :] = (t * inverse_rms(t) * gain).astype(BF)
            return 0

        lax.fori_loop(0, nt_, normed, 0)
        step(2)
        step(3)
        wl = [pltpu.make_async_copy(win_h.at[:, :, pl.ds(1024 * i, 1024)], win.at[i], vsem.at[i]) for i in range(3)]
        wl.append(pltpu.make_async_copy(wout_h, wout, vsem.at[3]))
        for t in (4, 5, 6, 7):
            step(t)
            wl[t - 4].start()
        tail.wait()
        th = halo_t[...].astype(F32)
        nh = (th * inverse_rms(th) * gain).astype(BF)
        for c in wl:
            c.wait()
        hb = dg(nh, win[0].reshape(dim, dim), 1, 0) * dg(nh, win[2].reshape(dim, dim), 1, 0)
        halo_g[...] = hb[8:16, :]
        tb[0:8, :] = halo_g[...]

        def stash(i, s):
            r = cols(i, tt)
            return [pltpu.make_async_copy(st.at[s, k], bcx_h.at[k, r], lsem.at[s, k]) for k in range(3)] + [
                pltpu.make_async_copy(mst.at[s], mix_h.at[r], lsem.at[s, 3]),
                pltpu.make_async_copy(obuf.at[r], hid_h.at[r], lsem.at[s, 4])]

        def tile(i, _):
            r = cols(i, tt)
            s = lax.rem(i, 2)
            pl.when(i >= 2)(lambda: act_on(stash(i - 2, s), "wait"))
            x = nm[r, :]
            bv = dg(x, win[0].reshape(dim, dim), 1, 0)
            st[s, 0] = bv
            xv = dg(x, win[2].reshape(dim, dim), 1, 0)
            st[s, 2] = xv
            tb[8 : 8 + tt, :] = bv * xv
            cv = dg(x, win[1].reshape(dim, dim), 1, 0)
            st[s, 1] = cv
            k1, k2 = msk_ref[r, 0:1], msk_ref[r, 1:2]
            conv = (vec[4:5, :] * tb[8 : 8 + tt, :] + vec[3:4, :] * (k1 * tb[7 : 7 + tt, :])
                    + vec[2:3, :] * (k2 * tb[6 : 6 + tt, :]))
            mixed = (cv * conv).astype(BF)
            mst[s] = mixed
            tb[0:8, :] = tb[tt : tt + 8, :]
            h = tok_ref[r, :].astype(F32) + dg(mixed, wout[...].reshape(dim, dim), 1, 0)
            obuf[r, :] = h
            nf[r, :] = (h * inverse_rms(h) * vec[1:2, :]).astype(BF)
            act_on(stash(i, s), "start")
            for k in range(4):
                pl.when(i == k)(functools.partial(step, 8 + k))
            return 0

        lax.fori_loop(0, nt_, tile, 0)
        for i in (nt_ - 2, nt_ - 1):
            act_on(stash(i, i % 2), "wait")

    pl.run_scoped(
        mixer_forward, pltpu.VMEM((32, 8, 128), F32), pltpu.VMEM((3, 32, 32, dim), BF), pltpu.VMEM((32, 32, dim), BF),
        pltpu.VMEM((2, 3, tt, dim), F32), pltpu.VMEM((2, tt, dim), BF), pltpu.VMEM((tt + 8, dim), F32),
    )
    step(12)

    def put(b3, j, s):
        return pltpu.make_async_copy(b3.at[s], gdown_h.at[cols(j), :], vsem.at[s])

    def ffn(gw, uw, dw, act, gg, gu, nt, b3):
        tm = td = 512

        def fetch(j, s):
            return [pltpu.make_async_copy(wgu_h.at[:, 0, :, cols(j)], gw.at[s], lsem.at[s, 0]),
                    pltpu.make_async_copy(wgu_h.at[:, 1, :, cols(j)], uw.at[s], lsem.at[s, 1]),
                    pltpu.make_async_copy(wd_h.at[cols(j), :], dw.at[s], lsem.at[s, 2])]

        act_on(fetch(0, 0), "start")

        def turned(i, _):
            nt[:, cols(i, tt)] = nf[cols(i, tt), :].T
            return 0

        lax.fori_loop(0, nt_, turned, 0)

        def body(j, carry):
            s = lax.rem(j, 2)

            def stage(fn, k, lo=0):
                pl.when(jnp.logical_and(j + k >= lo, j + k < n))(lambda: fn(j + k))

            act_on(fetch(j, s), "wait")

            def tile(i):
                r = pl.ds(i * tm, tm)
                x = nf[r, :]
                g_w, u_w = gw[s].reshape(dim, f), uw[s].reshape(dim, f)
                g = dg(x, g_w, 1, 0)
                u = dg(x, u_w, 1, 0)
                ga = dg(gf[r, :], dw[s], 1, 1)
                sg = jax.nn.sigmoid(g)
                si = g * sg
                a = (si * u).astype(BF)
                act[r, :] = a
                ggv = (ga * u * sg * (1.0 + g * (1.0 - sg))).astype(BF)
                guv = (ga * si).astype(BF)
                gg[r, :] = ggv
                gu[r, :] = guv
                obuf[r, :] += dg(a, dw[s], 1, 0)
                gn[r, :] += dg(ggv, g_w, 1, 1) + dg(guv, u_w, 1, 1)

            tile(0)
            stage(lambda u: gu_unit(u).s2(), 1, 1)
            stage(lambda u: eng_gu.go(2, u), -1)
            tile(1)
            stage(lambda u: eng_gu.go(4, u), -2)
            stage(lambda u: gu_unit(u).s1(), 2, 2)
            stage(lambda u: gu_unit(u).s0(), 2 + AHEAD, 2 + AHEAD)
            for i in range(dim // td):
                x = nt[i * td : (i + 1) * td, :]
                part[s, 0, i] = dg(x, gg[...], 1, 0).astype(BF).reshape(2, 2, 4, 32, f)
                part[s, 1, i] = dg(x, gu[...], 1, 0).astype(BF).reshape(2, 2, 4, 32, f)
            eng_gu.begin(j)
            stage(lambda u: gu_unit(u).s3(), 1, 1)
            stage(lambda u: gu_unit(u).s4(), 1, 1)
            stage(lambda u: act_on(fetch(u, 1 - s), "start"), 1)
            pl.when(j >= 2)(lambda: put(b3, j - 2, s).wait())
            for i in range(f // 256):
                b3[s, i * 256 : (i + 1) * 256, :] = dg(act[:, i * 256 : (i + 1) * 256].T, gf[...], 1, 0).astype(BF)
            put(b3, j, s).start()
            eng_gu.go(1, j)
            stage(lambda u: eng_gu.go(3, u), -1)
            stage(lambda u: eng_gu.end(u), -2)
            return carry

        lax.fori_loop(0, n, body, 0)
        for j in (n - 2, n - 1):
            put(b3, j, j % 2).wait()

    pl.run_scoped(
        ffn, pltpu.VMEM((2, 32, 32, f), BF), pltpu.VMEM((2, 32, 32, f), BF), pltpu.VMEM((2, f, dim), BF),
        pltpu.VMEM((tok, f), BF), pltpu.VMEM((tok, f), BF), pltpu.VMEM((tok, f), BF),
        pltpu.VMEM((dim, tok), BF), pltpu.VMEM((2, f, dim), BF),
    )

    def load_down(u, r0, h):
        s = lax.rem(u, 2)
        return [pltpu.make_async_copy(gdown6.at[:, :, :, :, pl.ds(r0, h), pl.ds(512 * a, 512)],
                                      part.at[s, a, :, :, :, :, pl.ds(0, h)], vsem.at[2 + a]) for a in range(2)]

    def load_mid(u):
        return load_down(u, pl.multiple_of((u - n) * 32, 32), 32)

    def mixer_backward(gp, turn, wout):
        wcopy = pltpu.make_async_copy(wout_h, wout, vsem.at[0])
        act_on(load_mid(n), "start")
        wcopy.start()
        act_on(load_mid(n), "wait")
        eng_mid.begin(n)

        def turned(i, _):
            turn[:, cols(i, tt)] = nm[cols(i, tt), :].T
            return 0

        lax.fori_loop(0, nt_, turned, 0)
        mcopy = pltpu.make_async_copy(mix_h, nm, vsem.at[1])
        mcopy.start()
        wcopy.wait()

        def advance(u):
            for k, stage in ((0, 1), (1, 2), (2, 3), (3, 4)):
                if u - k < ndn + 5:
                    eng(u - k).go(stage, u - k)

        def grad_in(k, s):
            for i in range(2):
                for a in range(2):
                    t = dg(turn[512 * i : 512 * i + 512, :], gp[:, 1024 * k + 512 * a : 1024 * k + 512 * a + 512], 1, 0)
                    part[s, a, i] = t.astype(BF).reshape(2, 2, 4, 32, 512)

        def part_of(u):
            if u == ndn:
                for i in range(4):
                    t = dg(nm[:, 256 * i : 256 * i + 256].T, nf[...], 1, 0).astype(BF)
                    for a in range(2):
                        part[u % 2, a, i // 2, i % 2] = t[:, 512 * a : 512 * a + 512].reshape(2, 4, 32, 512)
            elif u < ndn + 4:
                grad_in(order[u - ndn - 1], u % 2)
            else:
                act_on(load_down(u, 128, 16), "start")
                act_on(load_down(u, 128, 16), "wait")

        def passes(ld, ost, tb, tb2):
            def fetch(i, s):
                r = cols(i, tt)
                return [pltpu.make_async_copy(bcx_h.at[k, r], ld.at[s, k], lsem.at[s, k]) for k in range(3)] + [
                    pltpu.make_async_copy(hid_h.at[r], ld.at[s, 3], lsem.at[s, 3])]

            def put_out(i):
                return pltpu.make_async_copy(ost, out_ref.at[cols(i, tt)], lsem.at[0, 4])

            act_on(fetch(0, 0), "start")
            tb[0:8, :] = halo_g[...]
            obuf[tok : tok + 8, :] = jnp.zeros((8, dim), F32)

            def two(i, s):
                r = cols(i, tt)
                tb2[...] = obuf[pl.ds(pl.multiple_of(i * tt, tt), tt + 8), :]
                k1, k2 = msk_ref[r, 3:4], msk_ref[r, 4:5]
                tb2[0:tt, :] = (vec[4:5, :] * tb2[0:tt, :] + vec[3:4, :] * (k1 * tb2[1 : 1 + tt, :])
                                + vec[2:3, :] * (k2 * tb2[2 : 2 + tt, :]))

                @pl.when(i == nt_ - 1)
                def _():
                    tb2[tt - 8 : tt, :] += edge_r[...]

                gg = tb2[0:tt, :]
                gp[r, 0:1024] = (gg * ld[s, 2]).astype(BF)
                gp[r, 2048:3072] = (gg * ld[s, 0]).astype(BF)

            def one(i, _):
                u = n + i
                s = lax.rem(i, 2)
                r = cols(i, tt)
                eng_mid.go(1, u)
                eng_mid.go(2, u - 1)
                pl.when(i >= 1)(lambda: eng_mid.go(3, u - 2))
                pl.when(i != 1)(lambda: eng_mid.go(4, jnp.where(i == 0, n - 2, u - 3)))
                pl.when(i + 1 < nt_)(lambda: act_on(load_mid(u + 1), "start"))
                act_on(fetch(i, s), "wait")
                pl.when(i >= 1)(lambda: put_out(i - 1).wait())
                ost[...] = obuf[r, :] * msk_ref[r, 2:3]
                put_out(i).start()
                v = ld[s, 3]
                g = gn[r, :]
                inv = inverse_rms(v)
                a = g * vec[1:2, :]
                dot = jnp.sum(a * v, axis=1, keepdims=True) / dim
                ghid = gf[r, :].astype(F32) + (inv * a - v * (inv * inv * inv) * dot)
                sm[1:2, :] += jnp.sum(g * v * inv, axis=0, keepdims=True)
                gn[r, :] = ghid
                low = ghid.astype(BF)
                nf[r, :] = low
                gm = dg(low, wout[...].reshape(dim, dim), 1, 1)
                tb[8 : 8 + tt, :] = ld[s, 0] * ld[s, 2]
                k1, k2 = msk_ref[r, 0:1], msk_ref[r, 1:2]
                gated, lag1, lag2 = tb[8 : 8 + tt, :], k1 * tb[7 : 7 + tt, :], k2 * tb[6 : 6 + tt, :]
                conv = vec[4:5, :] * gated + vec[3:4, :] * lag1 + vec[2:3, :] * lag2
                gp[r, 1024:2048] = (gm * conv).astype(BF)
                gc = gm * ld[s, 1]
                obuf[r, :] = gc
                sm[2:3, :] += jnp.sum(gc * lag2, axis=0, keepdims=True)
                sm[3:4, :] += jnp.sum(gc * lag1, axis=0, keepdims=True)
                sm[4:5, :] += jnp.sum(gc * gated, axis=0, keepdims=True)
                tb[0:8, :] = tb[tt : tt + 8, :]

                @pl.when(i == 0)
                def _():
                    first, second = obuf[0:1, :], obuf[1:2, :]
                    k1a, k2a, k2b = msk_ref[0:1, 0:1], msk_ref[0:1, 1:2], msk_ref[1:2, 1:2]
                    edge_s[6:7, :] = vec[2:3, :] * (k2a * first)
                    edge_s[7:8, :] = vec[3:4, :] * (k1a * first) + vec[2:3, :] * (k2b * second)
                    edge.start()

                pl.when(i >= 1)(lambda: two(i - 1, 1 - s))

                @pl.when(i + 1 < nt_)
                def _():
                    act_on(fetch(i + 1, 1 - s), "start")
                    act_on(load_mid(u + 1), "wait")
                    eng_mid.begin(u + 1)

                pl.when(i != 1)(lambda: eng_mid.end(jnp.where(i == 0, n - 2, u - 3)))
                return 0

            lax.fori_loop(0, nt_, one, 0)
            mcopy.wait()
            part_of(ndn)
            eng(ndn).begin(ndn)
            put_out(nt_ - 1).wait()
            edge.wait()
            two(nt_ - 1, (nt_ - 1) % 2)

        edge = remote(edge_s, edge_r, hsem.at[3], hsem.at[4], pc.zs[2])
        pl.run_scoped(passes, pltpu.VMEM((2, 4, tt, dim), F32), pltpu.VMEM((tt, dim), F32),
                      pltpu.VMEM((tt + 8, dim), F32), pltpu.VMEM((tt + 8, dim), F32))

        def ending(win, ost):
            wl = [pltpu.make_async_copy(win_h.at[:, :, pl.ds(1024 * i, 1024)], win.at[i], lsem.at[0, i]) for i in range(3)]
            act_on(wl, "start")

            def put_tok(i, s):
                return pltpu.make_async_copy(ost.at[s], gtok_ref.at[cols(i, tt)], lsem.at[s, 4])

            def grad_tok(i, _):
                s = lax.rem(i, 2)
                r = cols(i, tt)
                g = dg(gp[r, 0:1024], win[0].reshape(dim, dim), 1, 1)
                g = g + dg(gp[r, 1024:2048], win[1].reshape(dim, dim), 1, 1)
                g = g + dg(gp[r, 2048:3072], win[2].reshape(dim, dim), 1, 1)
                v = tok_ref[r, :].astype(F32)
                inv = inverse_rms(v)
                a = g * vec[0:1, :]
                dot = jnp.sum(a * v, axis=1, keepdims=True) / dim
                pl.when(i >= 2)(lambda: put_tok(i - 2, s).wait())
                ost[s] = gn[r, :] + (inv * a - v * (inv * inv * inv) * dot)
                put_tok(i, s).start()
                sm[0:1, :] += jnp.sum(g * v * inv, axis=0, keepdims=True)
                return 0

            for u in range(ndn, ndn + 8):
                advance(u)
                if u < ndn + 4:
                    part_of(u + 1)
                    eng(u + 1).begin(u + 1)
                if u == ndn:
                    act_on(wl, "wait")
                if u in (ndn + 1, ndn + 2):
                    lax.fori_loop(2 * (u - ndn - 1), 2 * (u - ndn), grad_tok, 0)
                if u == ndn + 2:
                    small_begin(0)
                elif u > ndn + 2 and u < ndn + 6:
                    small_end(u - ndn - 3)
                    small_begin(u - ndn - 2)
                elif u == ndn + 6:
                    small_end(3)
                    outs = pltpu.make_async_copy(sm, small_o, hsem.at[0])
                    outs.start()
                eng(u - 3).end(u - 3)
            outs.wait()
            for i in (nt_ - 2, nt_ - 1):
                put_tok(i, i % 2).wait()

        pl.run_scoped(ending, pltpu.VMEM((3, 32, 32, dim), BF), pltpu.VMEM((2, tt, dim), F32))

    pl.run_scoped(mixer_backward, pltpu.VMEM((tok, 3 * dim), BF), pltpu.VMEM((dim, tok), BF), pltpu.VMEM((32, 32, dim), BF))

    for u in range(9):
        unit(u).fin()

    def last(j, carry):
        gu_unit(j).fin()
        return carry

    lax.fori_loop(0, n, last, 0)


def block_call(tokens, cot, lengths, counts, vecs, w_in, w_out, w_gate, w_up, w_down):
    tok, dim = tokens.shape
    ff = w_gate.shape[1]
    n = ff // 512
    sd = jax.ShapeDtypeStruct
    outs = [
        sd((tok, dim), F32), sd((tok, dim), F32), sd((32, ff), F32), sd((32, ff), F32), sd((ff // 32, dim), F32),
        sd((32, dim), F32), sd((32, 3 * dim), F32), sd((8, dim), F32),
        sd((32, 32, 3 * dim), BF), sd((32, 32, dim), BF), sd((ff, dim), BF), sd((32, 2, 32, ff), BF),
        sd((32, 8, 128), F32), sd((3, tok, dim), F32), sd((tok, dim), F32), sd((tok, dim), BF), sd((ff, dim), BF),
    ]
    return pl.pallas_call(
        block_kernel,
        out_shape=outs,
        in_specs=[VM, ANY, VM, pl.BlockSpec(memory_space=pltpu.SMEM), VM, ANY, ANY, ANY, ANY, ANY],
        out_specs=[ANY] * len(outs),
        scratch_shapes=[
            pltpu.VMEM((tok + 8, dim), F32),
            pltpu.VMEM((tok, dim), F32),
            pltpu.VMEM((tok, dim), BF),
            pltpu.VMEM((tok, dim), BF),
            pltpu.VMEM((tok, dim), BF),
            pltpu.VMEM((tok, 128), F32),
            pltpu.VMEM((8, dim), F32),
            pltpu.VMEM((1, 8, 128), F32),
            pltpu.VMEM((8, dim), F32),
            pltpu.VMEM((6, 8, dim), F32),
            pltpu.VMEM((16, dim), BF),
            pltpu.VMEM((8, dim), F32),
            pltpu.VMEM((8, dim), F32),
            pltpu.VMEM((8, dim), F32),
            pltpu.SemaphoreType.DMA((4,)),
            pltpu.SemaphoreType.DMA((2, 5)),
            pltpu.SemaphoreType.DMA((5,)),
            pltpu.SemaphoreType.DMA((12,)),
            pltpu.SemaphoreType.DMA((n + 9, NG)),
            pltpu.SemaphoreType.DMA((n + 9, NG)),
        ] + scatter_scratch(n + 9, 32, 512),
        name="block",
        compiler_params=pltpu.CompilerParams(collective_id=1, has_side_effects=True, vmem_limit_bytes=62 * 2**20 + 2**19),
    )(tokens, cot, lengths, counts, vecs, w_in[None], w_out[None], w_gate[None], w_up[None], w_down)


def passed_along(array, axis, by):
    size = lax.axis_size(axis)
    pairs = [(i, i + by) for i in range(size) if 0 <= i + by < size]
    return lax.ppermute(array, axis, pairs)


def rms_forward(values, gain_vec):
    inv_rms = lax.rsqrt(jnp.mean(values * values, axis=1, keepdims=True) + epsilon)
    return (values * inv_rms * gain_vec[None, :], inv_rms)


def rms_backward(values, inv_rms, gain_vec, grad_normed):
    weighted = grad_normed * gain_vec[None, :]
    features = values.shape[1]
    total_dot = jnp.sum(weighted * values, axis=1, keepdims=True)
    grad_values = inv_rms * weighted - values * (inv_rms * inv_rms * inv_rms) * total_dot / features
    grad_gain = jnp.sum(grad_normed * values * inv_rms, axis=0)
    return (grad_values, grad_gain)


def outer_sum(left, right):
    return lax.dot_general(
        left, right, (((0,), (0,)), ((), ())), preferred_element_type=jnp.float32
    )


def back_product(grad_low, weight_mat):
    return lax.dot_general(
        grad_low, weight_mat, (((1,), (1,)), ((), ())), preferred_element_type=jnp.float32
    )


def doc_masks(doc_lengths, valid_count, first_pos, tok_count):
    packed_row = first_pos // ROW_LEN
    lengths = lax.dynamic_index_in_dim(doc_lengths, packed_row, 0, keepdims=False)
    limit_count = lax.dynamic_index_in_dim(valid_count, packed_row, 0, keepdims=False)
    offsets = jnp.cumsum(lengths) - lengths
    places = first_pos % ROW_LEN + jnp.arange(tok_count, dtype=jnp.int32)
    begins = jnp.any(offsets[None, :] == places[:, None], axis=1)
    before = jnp.any(offsets[None, :] == places[:, None] - 1, axis=1)
    keep_one = jnp.where(begins, 0.0, 1.0).astype(jnp.float32)
    keep_two = jnp.where(begins | before, 0.0, 1.0).astype(jnp.float32)
    live_mask = jnp.where(places < limit_count, 1.0, 0.0).astype(jnp.float32)
    return (keep_one[:, None], keep_two[:, None], live_mask[:, None])


def shards_plain(
    tokens,
    cotangent,
    gain_mix,
    in_weight,
    conv_taps,
    out_weight,
    gain_ffn,
    gate_weight,
    up_weight,
    down_weight,
    doc_lengths,
    valid_count,
):
    tok_count = tokens.shape[0]
    first_pos = lax.axis_index(("wide", "narrow")) * tok_count
    keep_one, keep_two, live_mask = doc_masks(doc_lengths, valid_count, first_pos, tok_count)
    full_gm, w_in, full_taps, w_out, full_gf, w_gate, w_up, w_down = (
        lax.all_gather(gain_mix, ("wide", "narrow"), axis=0, tiled=True),
        lax.all_gather(in_weight, ("wide", "narrow"), axis=0, tiled=True),
        lax.all_gather(conv_taps, ("wide", "narrow"), axis=1, tiled=True),
        lax.all_gather(out_weight, ("wide", "narrow"), axis=0, tiled=True),
        lax.all_gather(gain_ffn, ("wide", "narrow"), axis=0, tiled=True),
        lax.all_gather(gate_weight, ("wide", "narrow"), axis=0, tiled=True),
        lax.all_gather(up_weight, ("wide", "narrow"), axis=0, tiled=True),
        lax.all_gather(down_weight, ("wide", "narrow"), axis=0, tiled=True),
    )
    mix_gain = full_gm.astype(jnp.float32)
    ffn_gain = full_gf.astype(jnp.float32)
    taps = full_taps.astype(jnp.float32)
    features = tokens.shape[1]
    tok_float = tokens.astype(jnp.float32)
    normed_mix, inv_mix = rms_forward(tok_float, mix_gain)
    normed_low = normed_mix.astype(jnp.bfloat16)
    projected = jnp.dot(normed_low, w_in, preferred_element_type=jnp.float32)
    b_part = projected[:, :features]
    c_part = projected[:, features : 2 * features]
    x_part = projected[:, 2 * features :]
    gated = b_part * x_part
    edge_rows = passed_along(gated[-2:], "narrow", 1)
    extended = jnp.concatenate([edge_rows, gated], axis=0)
    lag_one = keep_one * extended[1:-1]
    lag_two = keep_two * extended[:-2]
    conv_out = taps[2][None, :] * gated + taps[1][None, :] * lag_one + taps[0][None, :] * lag_two
    mixed_low = (c_part * conv_out).astype(jnp.bfloat16)
    hidden_res = tok_float + jnp.dot(mixed_low, w_out, preferred_element_type=jnp.float32)
    normed_ffn, inv_ffn = rms_forward(hidden_res, ffn_gain)
    ffn_low = normed_ffn.astype(jnp.bfloat16)
    gate_val = jnp.dot(ffn_low, w_gate, preferred_element_type=jnp.float32)
    up_val = jnp.dot(ffn_low, w_up, preferred_element_type=jnp.float32)
    sigmoid_gate = jax.nn.sigmoid(gate_val)
    silu_val = gate_val * sigmoid_gate
    act_low = (silu_val * up_val).astype(jnp.bfloat16)
    ffn_out = jnp.dot(act_low, w_down, preferred_element_type=jnp.float32)
    output = live_mask * (hidden_res + ffn_out)
    again_gm, w_in, again_taps, w_out, again_gf, w_gate, w_up, w_down = (
        lax.all_gather(gain_mix, ("wide", "narrow"), axis=0, tiled=True),
        lax.all_gather(in_weight, ("wide", "narrow"), axis=0, tiled=True),
        lax.all_gather(conv_taps, ("wide", "narrow"), axis=1, tiled=True),
        lax.all_gather(out_weight, ("wide", "narrow"), axis=0, tiled=True),
        lax.all_gather(gain_ffn, ("wide", "narrow"), axis=0, tiled=True),
        lax.all_gather(gate_weight, ("wide", "narrow"), axis=0, tiled=True),
        lax.all_gather(up_weight, ("wide", "narrow"), axis=0, tiled=True),
        lax.all_gather(down_weight, ("wide", "narrow"), axis=0, tiled=True),
    )
    mix_gain = again_gm.astype(jnp.float32)
    ffn_gain = again_gf.astype(jnp.float32)
    taps = again_taps.astype(jnp.float32)
    grad_res = live_mask * cotangent.astype(jnp.float32)
    grad_ffn_low = grad_res.astype(jnp.bfloat16)
    grad_down = outer_sum(act_low, grad_ffn_low)
    grad_act = back_product(grad_ffn_low, w_down)
    grad_gate_low = (
        grad_act * up_val * sigmoid_gate * (1.0 + gate_val * (1.0 - sigmoid_gate))
    ).astype(jnp.bfloat16)
    grad_up_low = (grad_act * silu_val).astype(jnp.bfloat16)
    grad_gate = outer_sum(ffn_low, grad_gate_low)
    grad_up = outer_sum(ffn_low, grad_up_low)
    grad_nffn = back_product(grad_gate_low, w_gate) + back_product(grad_up_low, w_up)
    grad_hnorm, grad_gf = rms_backward(hidden_res, inv_ffn, ffn_gain, grad_nffn)
    grad_hidden = grad_res + grad_hnorm
    grad_mix_low = grad_hidden.astype(jnp.bfloat16)
    grad_out = outer_sum(mixed_low, grad_mix_low)
    grad_mixed = back_product(grad_mix_low, w_out)
    grad_c = grad_mixed * conv_out
    grad_conv = grad_mixed * c_part
    grad_taps = jnp.stack(
        [
            jnp.sum(grad_conv * lag_two, axis=0),
            jnp.sum(grad_conv * lag_one, axis=0),
            jnp.sum(grad_conv * gated, axis=0),
        ],
        axis=0,
    )
    lag_grad_one = taps[1][None, :] * keep_one * grad_conv
    lag_grad_two = taps[0][None, :] * keep_two * grad_conv
    grad_ext = (
        jnp.pad(taps[2][None, :] * grad_conv, ((2, 0), (0, 0)))
        + jnp.pad(lag_grad_one, ((1, 1), (0, 0)))
        + jnp.pad(lag_grad_two, ((0, 2), (0, 0)))
    )
    from_right = passed_along(grad_ext[:2], "narrow", -1)
    grad_gated = jnp.concatenate([grad_ext[2:-2], grad_ext[-2:] + from_right], axis=0)
    grad_b = grad_gated * x_part
    grad_x = grad_gated * b_part
    grad_proj_low = jnp.concatenate([grad_b, grad_c, grad_x], axis=1).astype(jnp.bfloat16)
    grad_in = outer_sum(normed_low, grad_proj_low)
    grad_nmix = back_product(grad_proj_low, w_in)
    grad_tnorm, grad_gm = rms_backward(tok_float, inv_mix, mix_gain, grad_nmix)
    grad_tokens = grad_hidden + grad_tnorm
    sum_gm, sum_in, sum_taps, sum_out, sum_gf, sum_gate, sum_up, sum_down = (
        lax.psum_scatter(grad_gm, ("wide", "narrow"), scatter_dimension=0, tiled=True),
        lax.psum_scatter(grad_in, ("wide", "narrow"), scatter_dimension=0, tiled=True),
        lax.psum_scatter(grad_taps, ("wide", "narrow"), scatter_dimension=1, tiled=True),
        lax.psum_scatter(grad_out, ("wide", "narrow"), scatter_dimension=0, tiled=True),
        lax.psum_scatter(grad_gf, ("wide", "narrow"), scatter_dimension=0, tiled=True),
        lax.psum_scatter(grad_gate, ("wide", "narrow"), scatter_dimension=0, tiled=True),
        lax.psum_scatter(grad_up, ("wide", "narrow"), scatter_dimension=0, tiled=True),
        lax.psum_scatter(grad_down, ("wide", "narrow"), scatter_dimension=0, tiled=True),
    )
    return (
        output,
        grad_tokens,
        sum_gm,
        sum_in,
        sum_taps,
        sum_out,
        sum_gf,
        sum_gate,
        sum_up,
        sum_down,
    )


def shards(
    tokens, cotangent, gain_mix, in_weight, conv_taps, out_weight, gain_ffn,
    gate_weight, up_weight, down_weight, doc_lengths, valid_count,
):
    me = lax.axis_index(("wide", "narrow"))
    own = gain_mix.shape[0]
    vecs = jnp.concatenate([gain_mix[None], gain_ffn[None], conv_taps], axis=0).astype(F32)
    vecs = jnp.pad(vecs, ((0, 3), (0, 128 - own)))
    lengths = jnp.pad(doc_lengths, ((0, 0), (0, 128 - doc_lengths.shape[1])))
    output, grad_tokens, sum_gate, sum_up, sum_down, sum_out, sum_in, all_small = block_call(
        tokens, cotangent, lengths, valid_count, vecs, in_weight, out_weight, gate_weight, up_weight, down_weight
    )[:8]
    mine = lax.dynamic_slice_in_dim(all_small, me * own, own, 1)
    return (output, grad_tokens, mine[0], sum_in, mine[2:5], sum_out, mine[1], sum_gate, sum_up, sum_down)


def solution(mesh):
    both = ("wide", "narrow")
    rows, vec, flat = P(both, None), P(both), P(None, both)
    step = shards if (mesh.shape["wide"], mesh.shape["narrow"]) == (8, 4) else shards_plain
    return jax.shard_map(
        step,
        mesh=mesh,
        in_specs=(rows, rows, vec, rows, flat, rows, vec, rows, rows, rows, P(), P()),
        out_specs=(rows, rows, vec, rows, flat, rows, vec, rows, rows, rows),
        check_vma=False,
    )
```

```python
import functools

import jax
import jax.numpy as jnp
from jax import lax
from jax.experimental import pallas as pl
from jax.experimental.pallas import tpu as pltpu
from jax.sharding import PartitionSpec as P

ROW_LEN = 4096
epsilon = 1e-05
F32 = jnp.float32
BF = jnp.bfloat16
MESH = pl.DeviceIdType.MESH
ANY = pl.BlockSpec(memory_space=pl.ANY)
VM = pl.BlockSpec(memory_space=pltpu.VMEM)


def dg(a, b, ca, cb):
    return lax.dot_general(a, b, (((ca,), (cb,)), ((), ())), preferred_element_type=F32)


class Place:
    def __init__(self):
        w = lax.axis_index("wide")
        z = lax.axis_index("narrow")
        c = lax.rem(w, 2)
        x = lax.rem(w // 2, 2)
        y = w // 4
        self.w, self.z, self.c, self.x, self.y = w, z, c, x, y
        self.core = (w + 1 - 2 * c, z)
        self.xn = (w + 2 - 4 * x, z)
        self.yn = (w + 4 - 8 * y, z)
        self.zs = [(w, lax.rem(z + k, 4)) for k in (1, 2, 3)]
        self.zto = [lax.rem(z + k, 4) for k in (1, 2, 3)]
        self.zfrom = [lax.rem(z + 4 - k, 4) for k in (1, 2, 3)]

        def base(yy, xx, cc):
            return 16 * yy + 8 * xx + 4 * cc

        self.own, self.xb = base(y, x, c), base(y, 1 - x, c)
        self.yb, self.db = base(1 - y, x, c), base(1 - y, 1 - x, c)
        self.sown, self.sxb = base(y, x, 1 - c), base(y, 1 - x, 1 - c)
        self.syb, self.sdb = base(1 - y, x, 1 - c), base(1 - y, 1 - x, 1 - c)
        self.me = self.own + z

    def greet(self):
        bar = pltpu.get_barrier_semaphore()
        peers = [self.core, self.xn, self.yn] + self.zs
        for p in peers:
            pl.semaphore_signal(bar, inc=1, device_id=p, device_id_type=MESH)
        pl.semaphore_wait(bar, len(peers))


def remote(src, dst, ss, rs, dev):
    return pltpu.make_async_remote_copy(
        src_ref=src, dst_ref=dst, send_sem=ss, recv_sem=rs, device_id=dev, device_id_type=MESH
    )


class Gather:
    def __init__(self, pc, src, dst, full, ss, rs):
        self.pc, self.src, self.dst, self.full, self.ss, self.rs = pc, src, dst, full, ss, rs
        self.parts = range(len(src))

    def zc(self, i, k):
        q = 3 * i + k
        return remote(self.src[i](), self.dst[i](self.pc.me, 1), self.ss.at[q], self.rs.at[q], self.pc.zs[k])

    def zr(self, i, k):
        q = 3 * i + k
        v = self.dst[i](self.pc.own + self.pc.zfrom[k], 1)
        return remote(v, v, self.ss.at[q], self.rs.at[q], self.pc.zs[k])

    def loc(self, i):
        return pltpu.make_async_copy(self.src[i](), self.dst[i](self.pc.me, 1), self.ss.at[14 + i])

    def cp(self, k, b, n, dev):
        v = self.full(b, n)
        return remote(v, v, self.ss.at[k], self.rs.at[k], dev)

    def s0(self):
        for i in self.parts:
            self.loc(i).start()
            for k in range(3):
                self.zc(i, k).start()

    def s1(self):
        p = self.pc
        for i in self.parts:
            self.loc(i).wait()
            for k in range(3):
                self.zr(i, k).wait_recv()
        self.cp(6, p.own, 4, p.xn).start()
        self.cp(7, p.own, 4, p.yn).start()
        self.cp(8, p.own, 4, p.core).start()

    def s2(self):
        p = self.pc
        self.cp(6, p.xb, 4, p.xn).wait_recv()
        self.cp(9, p.xb, 2, p.yn).start()
        self.cp(10, p.xb, 4, p.core).start()
        self.cp(7, p.yb, 4, p.yn).wait_recv()
        self.cp(11, p.yb + 2, 2, p.xn).start()
        self.cp(12, p.yb, 4, p.core).start()

    def s3(self):
        p = self.pc
        self.cp(9, p.db, 2, p.yn).wait_recv()
        self.cp(11, p.db + 2, 2, p.xn).wait_recv()
        self.cp(13, p.db, 4, p.core).start()

    def s4(self):
        p = self.pc
        for k, b in ((8, p.sown), (10, p.sxb), (12, p.syb), (13, p.sdb)):
            self.cp(k, b, 4, p.core).wait_recv()

    def fin(self):
        p = self.pc
        for i in self.parts:
            for k in range(3):
                self.zc(i, k).wait_send()
        for k, b, n in (
            (6, p.own, 4), (7, p.own, 4), (8, p.own, 4), (9, p.xb, 2),
            (10, p.xb, 4), (11, p.yb + 2, 2), (12, p.yb, 4), (13, p.db, 4),
        ):
            self.cp(k, b, n, p.core).wait_send()


class GatherLate:
    def __init__(self, pc, src, view, ss, rs):
        self.pc, self.src, self.view, self.ss, self.rs = pc, src, view, ss, rs

    def at(self, flip_y=0, flip_x=0, p=None):
        pc = self.pc
        return self.view(1 - pc.y if flip_y else pc.y, 1 - pc.x if flip_x else pc.x, pc.z, pc.c, p)

    def four(self, z, c=None):
        both = slice(None)
        return self.view(both, both, z, self.pc.c if c is None else c, None)

    def r(self, k, v, dev, src=None):
        return remote(v if src is None else src, v, self.ss.at[k], self.rs.at[k], dev)

    def loc(self, p):
        return pltpu.make_async_copy(self.src[p](), self.at(p=p), self.ss.at[14 + p])

    def own(self, p):
        v, src = self.at(p=p), self.src[p]()
        return [self.r(p, v, self.pc.xn, src), self.r(2 + p, v, self.pc.yn, src)]

    def s0(self):
        for p in (0, 1):
            self.loc(p).start()
            for c in self.own(p):
                c.start()

    def s1(self):
        pc = self.pc
        self.r(0, self.at(0, 1, 0), pc.xn).wait_recv()
        self.r(4, self.at(0, 1, 0), pc.yn).start()
        self.r(3, self.at(1, 0, 1), pc.yn).wait_recv()
        self.r(5, self.at(1, 0, 1), pc.xn).start()

    def s2(self):
        pc = self.pc
        for p in (0, 1):
            self.loc(p).wait()
        self.r(1, self.at(0, 1, 1), pc.xn).wait_recv()
        self.r(2, self.at(1, 0, 0), pc.yn).wait_recv()
        self.r(4, self.at(1, 1, 0), pc.yn).wait_recv()
        self.r(5, self.at(1, 1, 1), pc.xn).wait_recv()
        self.r(9, self.four(pc.z), pc.core).start()

    def piece(self, q):
        pc = self.pc
        k, i = lax.rem(q, 3), q // 3
        v = self.view(i // 2, lax.rem(i, 2), pc.z, pc.c, None)
        self.r(6 + k, v, (pc.w, lax.rem(pc.z + 1 + k, 4))).start()

    def s3(self):
        pc = self.pc
        for k in range(3):
            self.r(6 + k, self.four(pc.zfrom[k]), pc.zs[k]).wait_recv()
            self.r(10 + k, self.four(pc.zfrom[k]), pc.core).start()

    def s4(self):
        pc = self.pc
        self.r(9, self.four(pc.z, 1 - pc.c), pc.core).wait_recv()
        for k in range(3):
            self.r(10 + k, self.four(pc.zfrom[k], 1 - pc.c), pc.core).wait_recv()

    def fin(self):
        pc = self.pc
        for p in (0, 1):
            for c in self.own(p):
                c.wait_send()
        self.r(4, self.at(0, 1, 0), pc.yn).wait_send()
        self.r(5, self.at(1, 0, 1), pc.xn).wait_send()
        for k in range(3):
            self.r(6 + k, self.four(pc.z), pc.zs[k]).wait_send()
            self.r(10 + k, self.four(pc.zfrom[k]), pc.core).wait_send()
        self.r(9, self.four(pc.z), pc.core).wait_send()


NG = 16
NL = 4
AHEAD = 2
NS = 4


class Scatter:
    def __init__(self, pc, bufs, h, out):
        self.pc, self.h, self.out = pc, h, out
        (self.part, self.l0, self.ldx, self.ldy, self.lx, self.ly, self.lz,
         self.sd, self.sx, self.sy, self.so, self.sz, self.ob, self.ss, self.rs, self.os) = bufs

    def hr(self):
        return pl.ds(0, self.h)

    def c0(self, j, s):
        p = self.pc
        return remote(self.part.at[lax.rem(j, 2), :, :, :, 1 - p.c, :, self.hr()], self.l0.at[lax.rem(j, 3), :, :, :, :, self.hr()],
                      self.ss.at[j, 0], self.rs.at[j, 0], p.core)

    def cdx(self, j, s):
        return remote(self.sd.at[lax.rem(j, 2), :, pl.ds(0, 2), self.hr()], self.ldx.at[lax.rem(j, NL), :, :, self.hr()],
                      self.ss.at[j, 1], self.rs.at[j, 1], self.pc.xn)

    def cdy(self, j, s):
        return remote(self.sd.at[lax.rem(j, 2), :, pl.ds(2, 2), self.hr()], self.ldy.at[lax.rem(j, NL), :, :, self.hr()],
                      self.ss.at[j, 2], self.rs.at[j, 2], self.pc.yn)

    def cx(self, j, s):
        return remote(self.sx.at[s, :, :, self.hr()], self.lx.at[lax.rem(j, NL), :, :, self.hr()],
                      self.ss.at[j, 3], self.rs.at[j, 3], self.pc.xn)

    def cy(self, j, s):
        return remote(self.sy.at[s, :, :, self.hr()], self.ly.at[lax.rem(j, NL), :, :, self.hr()],
                      self.ss.at[j, 4], self.rs.at[j, 4], self.pc.yn)

    def cz(self, j, s, k):
        return remote(self.sz.at[lax.rem(j, 2), :, self.pc.zto[k], self.hr()], self.lz.at[lax.rem(j, NL), k, :, self.hr()],
                      self.ss.at[j, 5 + k], self.rs.at[j, 5 + k], self.pc.zs[k])

    def r0(self, j, s):
        self.c0(j, s).start()

    def q(self, j, s, a, yy, xx):
        hr = self.hr()
        return (self.part[lax.rem(j, 2), a, yy, xx, self.pc.c, :, hr].astype(F32)
                + self.l0[lax.rem(j, 3), a, yy, xx, :, hr].astype(F32))

    def r1(self, j, s):
        p, hr = self.pc, self.hr()
        self.c0(j, s).wait()
        for a in range(2):
            self.sd[lax.rem(j, 2), a, :, hr] = self.q(j, s, a, 1 - p.y, 1 - p.x).astype(BF)
        self.cdx(j, s).start()
        self.cdy(j, s).start()
        for a in range(2):
            self.sx[s, a, :, hr] = self.q(j, s, a, p.y, 1 - p.x).astype(BF)
            self.sy[s, a, :, hr] = self.q(j, s, a, 1 - p.y, p.x).astype(BF)
            self.so[s, a, :, hr] = self.q(j, s, a, p.y, p.x)

    def r2(self, j, s):
        hr = self.hr()
        lo, hi = pl.ds(0, 2), pl.ds(2, 2)
        self.cdx(j, s).wait()
        for a in range(2):
            self.sy[s, a, lo, hr] = (self.sy[s, a, lo, hr].astype(F32) + self.ldx[lax.rem(j, NL), a, :, hr].astype(F32)).astype(BF)
        self.cy(j, s).start()
        self.cdy(j, s).wait()
        for a in range(2):
            self.sx[s, a, hi, hr] = (self.sx[s, a, hi, hr].astype(F32) + self.ldy[lax.rem(j, NL), a, :, hr].astype(F32)).astype(BF)
        self.cx(j, s).start()

    def r3(self, j, s):
        hr = self.hr()
        self.cy(j, s).wait()
        self.cx(j, s).wait()
        for a in range(2):
            t = self.so[s, a, :, hr] + self.lx[lax.rem(j, NL), a, :, hr].astype(F32) + self.ly[lax.rem(j, NL), a, :, hr].astype(F32)
            self.so[s, a, :, hr] = t
            self.sz[lax.rem(j, 2), a, :, hr] = t.astype(BF)
        for k in range(3):
            self.cz(j, s, k).start()

    def r4(self, j, s):
        hr = self.hr()
        for k in range(3):
            self.cz(j, s, k).wait()
        for a in range(2):
            t = self.so[s, a, self.pc.z, hr]
            for k in range(3):
                t = t + self.lz[lax.rem(j, NL), k, a, hr].astype(F32)
            self.ob[s, a, hr] = t
        self.out(j, s, self.ob, self.os, "start")

    def go(self, stage, j):
        (self.r1, self.r2, self.r3, self.r4)[stage - 1](j, lax.rem(j, NS))

    def begin(self, j):
        self.r0(j, lax.rem(j, NS))

    def end(self, j):
        self.drain(j, lax.rem(j, NS))

    def drain(self, j, s):
        self.out(j, s, self.ob, self.os, "wait")


def scatter_scratch(n, h, w):
    return [
        pltpu.VMEM((2, 2, 2, 2, 2, 4, h, w), BF),
        pltpu.VMEM((3, 2, 2, 2, 4, h, w), BF),
        pltpu.VMEM((NL, 2, 2, h, w), BF),
        pltpu.VMEM((NL, 2, 2, h, w), BF),
        pltpu.VMEM((NL, 2, 4, h, w), BF),
        pltpu.VMEM((NL, 2, 4, h, w), BF),
        pltpu.VMEM((NL, 3, 2, h, w), BF),
        pltpu.VMEM((2, 2, 4, h, w), BF),
        pltpu.VMEM((NS, 2, 4, h, w), BF),
        pltpu.VMEM((NS, 2, 4, h, w), BF),
        pltpu.VMEM((NS, 2, 4, h, w), F32),
        pltpu.VMEM((2, 2, 4, h, w), BF),
        pltpu.VMEM((NS, 2, h, w), F32),
        pltpu.SemaphoreType.DMA((n, 8)),
        pltpu.SemaphoreType.DMA((n, 8)),
        pltpu.SemaphoreType.DMA((NS, 2)),
    ]


def inverse_rms(v):
    return lax.rsqrt(jnp.mean(v * v, axis=1, keepdims=True) + epsilon)


def block_kernel(
    tok_ref, cot_ref, doc_ref, count_ref, vec_ref, win_s, wout_s, wgate_s, wup_s, wdown_s,
    out_ref, gtok_ref, ggate_o, gup_o, gdown_o, gout_o, gin_o, small_o,
    win_h, wout_h, wd_h, wgu_h, vec_h, bcx_h, hid_h, mix_h, gdown_h,
    obuf, gn, nf, gf, nm, msk_ref, dlen, vec, vown, sm, sml, halo_t, halo_g, edge_s, edge_r,
    vsem, lsem, hsem, esem, gss, grs, *sc,
):
    pc = Place()
    tok, dim = tok_ref.shape
    ff = wgate_s.shape[-1]
    f = 512
    n = ff // f
    tt = 256
    nt_ = tok // tt
    part = sc[0]

    def cols(j, w=f):
        return pl.ds(pl.multiple_of(j * w, w), w)

    def simple(u, src, dst, c0, w):
        at = lambda b, m: dst.at[pl.ds(b, m), :, pl.ds(c0, w)]
        return Gather(pc, [lambda: src.at[:, :, pl.ds(c0, w)]], [at], at, gss.at[u], grs.at[u])

    def down_unit(i):
        rows = ff // 32
        at = lambda b, m: wd_h.at[pl.ds(pl.multiple_of(b * rows, rows), m * rows), pl.ds(256 * i, 256)]
        return Gather(pc, [lambda: wdown_s.at[:, pl.ds(256 * i, 256)]], [at], at, gss.at[5 + i], grs.at[5 + i])

    def gu_unit(j):
        srcs = [lambda: wgate_s.at[:, :, cols(j)], lambda: wup_s.at[:, :, cols(j)]]
        dsts = [lambda b, m: wgu_h.at[pl.ds(b, m), 0, :, cols(j)], lambda b, m: wgu_h.at[pl.ds(b, m), 1, :, cols(j)]]
        return Gather(pc, srcs, dsts, lambda b, m: wgu_h.at[pl.ds(b, m), :, :, cols(j)], gss.at[9 + j], grs.at[9 + j])

    def unit(u):
        if u == 0:
            return simple(0, vown, vec_h, 0, 128)
        if u < 4:
            return simple(u, win_s, win_h, 1024 * (u - 1), 1024)
        if u == 4:
            return simple(4, wout_s, wout_h, 0, 1024)
        if u < 9:
            return down_unit(u - 5)
        return gu_unit(u - 9)

    wd6 = wd_h.reshape(2, 2, 2, 4, ff // 32, dim)
    wgu7 = wgu_h.reshape(2, 2, 2, 4, 2, 32, ff)

    def down_view(y, x, z, c, p):
        return wd6.at[y, x, c, z, :, pl.ds(768, 256) if p is None else pl.ds(768 + 128 * p, 128)]

    def gu_view(y, x, z, c, p):
        return wgu7.at[y, x, c, z, slice(None) if p is None else p, :, pl.ds(ff - f, f)]

    late_down = GatherLate(pc, [lambda: wdown_s.at[:, pl.ds(768, 128)], lambda: wdown_s.at[:, pl.ds(896, 128)]],
                           down_view, gss.at[8], grs.at[8])
    late_gu = GatherLate(pc, [lambda: wgate_s.at[0, :, pl.ds(ff - f, f)], lambda: wup_s.at[0, :, pl.ds(ff - f, f)]],
                         gu_view, gss.at[8 + n], grs.at[8 + n])

    def small_copies(k):
        peers = [pc.core, pc.xn, pc.yn] + pc.zs
        return [remote(sm, sml.at[q], esem.at[q], esem.at[6 + q], peers[q]) for q in ((0,), (1,), (2,), (3, 4, 5))[k]]

    def small_begin(k):
        for c in small_copies(k):
            c.start()

    def small_end(k):
        for c in small_copies(k):
            c.wait()
        t = sm[...]
        for q in ((0,), (1,), (2,), (3, 4, 5))[k]:
            t = t + sml[q]
        sm[...] = t

    turn_of = [0, 1, 2, 3, 4, 5, 6, 7, 9, 10, 11, 12]

    def step(t):
        if t < 10:
            unit(turn_of[t]).s1()
            unit(turn_of[t + AHEAD]).s0()
        if t >= 2 and t < 10:
            unit(turn_of[t - 1]).s2()
        if t >= 3 and t < 11:
            unit(turn_of[t - 2]).s3()
        if t >= 4:
            unit(turn_of[t - 3]).s4()

    ndn = n + 4
    gdown6 = gdown_h.reshape(2, 2, 2, 4, ff // 32, dim)

    def act_on(copies, what):
        for c in copies:
            getattr(c, what)()

    def out_gu(j, s, ob, osem, what):
        act_on([pltpu.make_async_copy(ob.at[s, 0], ggate_o.at[:, cols(j)], osem.at[s, 0]),
                pltpu.make_async_copy(ob.at[s, 1], gup_o.at[:, cols(j)], osem.at[s, 1])], what)

    def out_rows(dst, r0, c0, h):
        def go(j, s, ob, osem, what):
            act_on([pltpu.make_async_copy(ob.at[s, a, pl.ds(0, h)],
                                          dst.at[pl.ds(r0, h), pl.ds(c0 + 512 * a, 512)], osem.at[s, a])
                    for a in range(2)], what)
        return go

    def out_down(j, s, ob, osem, what):
        out_rows(gdown_o, pl.multiple_of((j - n) * 32, 32), 0, 32)(j, s, ob, osem, what)

    def out_mixed(j, s, ob, osem, what):
        pl.when(j < n)(lambda: out_gu(j, s, ob, osem, what))
        pl.when(j >= n)(lambda: out_down(j, s, ob, osem, what))

    eng_gu = Scatter(pc, sc, 32, out_gu)
    eng_mid = Scatter(pc, sc, 32, out_mixed)
    order = (1, 0, 2)

    def eng(u):
        if u < ndn:
            return Scatter(pc, sc, 32, out_down)
        if u == ndn:
            return Scatter(pc, sc, 32, out_rows(gout_o, 0, 0, 32))
        if u < ndn + 4:
            return Scatter(pc, sc, 32, out_rows(gin_o, 0, 1024 * order[u - ndn - 1], 32))
        return Scatter(pc, sc, 16, out_rows(gdown_o, 128, 0, 16))

    pc.greet()
    vown[0] = pltpu.roll(vec_ref[...], 32 * pc.z, 1)
    unit(0).s0()
    unit(1).s0()
    cot_copy = pltpu.make_async_copy(cot_ref, gf, hsem.at[0])
    cot_copy.start()
    tail = remote(tok_ref.at[pl.ds(tok - 16, 16)], halo_t, hsem.at[1], hsem.at[2], pc.zs[0])
    tail.start()
    sm[...] = jnp.zeros_like(sm)
    edge_s[...] = jnp.zeros_like(edge_s)
    gn[...] = jnp.zeros_like(gn)
    row_devs = ROW_LEN // tok
    row = pc.me // row_devs
    dlen[...] = jnp.zeros_like(dlen)
    dlen[0:1, 0:16] = doc_ref[pl.ds(row, 1), :]
    lens = dlen[...]
    lane = lax.broadcasted_iota(jnp.int32, (8, 128), 1)
    sums = lens
    for k in (1, 2, 4, 8):
        sums = sums + jnp.where(lane >= k, pltpu.roll(sums, k, 1), 0)
    starts = jnp.where(lane < 16, sums - lens, -8)[0:1, :]
    limit = count_ref[row]
    cot_copy.wait()

    def live_rows(i, _):
        r = cols(i, tt)
        t = i * tt + lax.broadcasted_iota(jnp.int32, (tt, 128), 0)
        place = lax.rem(pc.me, row_devs) * tok + t

        def begins(by):
            return jnp.max(jnp.where(starts == place + by, 1.0, 0.0), axis=1, keepdims=True)

        b0, b1, b2, bm = begins(0), begins(1), begins(2), begins(-1)
        ln = lax.broadcasted_iota(jnp.int32, (tt, 128), 1)
        m = jnp.where(ln == 0, 1.0 - b0, 1.0 - jnp.maximum(b0, bm))
        m = jnp.where(ln == 2, jnp.where(place < limit, 1.0, 0.0), m)
        m = jnp.where(ln == 3, jnp.where(t + 1 < tok, 1.0 - b1, 0.0), m)
        msk_ref[r, :] = jnp.where(ln == 4, jnp.where(t + 2 < tok, 1.0 - jnp.maximum(b2, b1), 0.0), m)
        gf[r, :] = (gf[r, :].astype(F32) * msk_ref[r, 2:3]).astype(BF)
        return 0

    lax.fori_loop(0, nt_, live_rows, 0)
    unit(0).s1()
    unit(2).s0()
    late_down.s0()
    late_gu.s0()
    unit(1).s1()
    unit(3).s0()
    unit(0).s2()
    step(2)
    unit(0).s3()
    late_down.s1()
    late_gu.s1()
    step(3)
    late_down.s2()
    late_down.piece(0)
    unit(0).s4()

    def mixer_forward(vbuf, win, wout, st, mst, tb):
        vcopy = pltpu.make_async_copy(vec_h, vbuf, vsem.at[0])
        vcopy.start()
        vcopy.wait()
        for q in range(8):
            v = vbuf[4 * q] + vbuf[4 * q + 1] + vbuf[4 * q + 2] + vbuf[4 * q + 3]
            vec[:, 128 * q : 128 * q + 128] = v
        gain = vec[0:1, :]

        def normed(i, _):
            r = cols(i, tt)
            t = tok_ref[r, :].astype(F32)
            nm[r, :] = (t * inverse_rms(t) * gain).astype(BF)
            return 0

        lax.fori_loop(0, nt_, normed, 0)
        wl = [pltpu.make_async_copy(win_h.at[:, :, pl.ds(1024 * i, 1024)], win.at[i], vsem.at[i]) for i in range(3)]
        wl.append(pltpu.make_async_copy(wout_h, wout, vsem.at[3]))
        for t in (4, 5, 6, 7):
            step(t)
            late_down.piece(2 * t - 7)
            late_down.piece(2 * t - 6)
            wl[t - 4].start()
        tail.wait()
        th = halo_t[...].astype(F32)
        nh = (th * inverse_rms(th) * gain).astype(BF)
        for c in wl:
            c.wait()
        hb = dg(nh, win[0].reshape(dim, dim), 1, 0) * dg(nh, win[2].reshape(dim, dim), 1, 0)
        halo_g[...] = hb[8:16, :]
        tb[0:8, :] = halo_g[...]

        def stash(i, s):
            r = cols(i, tt)
            return [pltpu.make_async_copy(st.at[s, k], bcx_h.at[k, r], lsem.at[s, k]) for k in range(3)] + [
                pltpu.make_async_copy(mst.at[s], mix_h.at[r], lsem.at[s, 3]),
                pltpu.make_async_copy(obuf.at[r], hid_h.at[r], lsem.at[s, 4])]

        def tile(i, _):
            r = cols(i, tt)
            s = lax.rem(i, 2)
            pl.when(i >= 2)(lambda: act_on(stash(i - 2, s), "wait"))
            x = nm[r, :]
            bv = dg(x, win[0].reshape(dim, dim), 1, 0)
            st[s, 0] = bv
            xv = dg(x, win[2].reshape(dim, dim), 1, 0)
            st[s, 2] = xv
            tb[8 : 8 + tt, :] = bv * xv
            cv = dg(x, win[1].reshape(dim, dim), 1, 0)
            st[s, 1] = cv
            k1, k2 = msk_ref[r, 0:1], msk_ref[r, 1:2]
            conv = (vec[4:5, :] * tb[8 : 8 + tt, :] + vec[3:4, :] * (k1 * tb[7 : 7 + tt, :])
                    + vec[2:3, :] * (k2 * tb[6 : 6 + tt, :]))
            mixed = (cv * conv).astype(BF)
            mst[s] = mixed
            tb[0:8, :] = tb[tt : tt + 8, :]
            h = tok_ref[r, :].astype(F32) + dg(mixed, wout[...].reshape(dim, dim), 1, 0)
            obuf[r, :] = h
            nf[r, :] = (h * inverse_rms(h) * vec[1:2, :]).astype(BF)
            act_on(stash(i, s), "start")
            for k in range(3):
                pl.when(i == k)(functools.partial(step, 8 + k))
            pl.when(i < 3)(lambda: late_down.piece(9 + i))
            pl.when(i == 3)(late_down.s3)
            return 0

        lax.fori_loop(0, nt_, tile, 0)
        for i in (nt_ - 2, nt_ - 1):
            act_on(stash(i, i % 2), "wait")

    pl.run_scoped(
        mixer_forward, pltpu.VMEM((32, 8, 128), F32), pltpu.VMEM((3, 32, 32, dim), BF), pltpu.VMEM((32, 32, dim), BF),
        pltpu.VMEM((2, 3, tt, dim), F32), pltpu.VMEM((2, tt, dim), BF), pltpu.VMEM((tt + 8, dim), F32),
    )
    step(11)
    late_down.s4()

    def put(b3, j, s):
        return pltpu.make_async_copy(b3.at[s], gdown_h.at[cols(j), :], vsem.at[s])

    def ffn(gw, uw, dw, act, gg, gu, nt, b3):
        tm = td = 512

        def fetch(j, s):
            return [pltpu.make_async_copy(wgu_h.at[:, 0, :, cols(j)], gw.at[s], lsem.at[s, 0]),
                    pltpu.make_async_copy(wgu_h.at[:, 1, :, cols(j)], uw.at[s], lsem.at[s, 1]),
                    pltpu.make_async_copy(wd_h.at[cols(j), :], dw.at[s], lsem.at[s, 2])]

        act_on(fetch(0, 0), "start")

        def turned(i, _):
            nt[:, cols(i, tt)] = nf[cols(i, tt), :].T
            return 0

        lax.fori_loop(0, nt_, turned, 0)

        def body(j, carry):
            s = lax.rem(j, 2)

            def stage(fn, k, lo=0, hi=n):
                pl.when(jnp.logical_and(j + k >= lo, j + k < hi))(lambda: fn(j + k))

            act_on(fetch(j, s), "wait")

            def tile(i):
                r = pl.ds(i * tm, tm)
                x = nf[r, :]
                g_w, u_w = gw[s].reshape(dim, f), uw[s].reshape(dim, f)
                g = dg(x, g_w, 1, 0)
                u = dg(x, u_w, 1, 0)
                ga = dg(gf[r, :], dw[s], 1, 1)
                sg = jax.nn.sigmoid(g)
                si = g * sg
                a = (si * u).astype(BF)
                act[r, :] = a
                ggv = (ga * u * sg * (1.0 + g * (1.0 - sg))).astype(BF)
                guv = (ga * si).astype(BF)
                gg[r, :] = ggv
                gu[r, :] = guv
                obuf[r, :] += dg(a, dw[s], 1, 0)
                gn[r, :] += dg(ggv, g_w, 1, 1) + dg(guv, u_w, 1, 1)

            tile(0)
            pl.when(jnp.logical_and(j >= 1, j < 7))(lambda: late_gu.piece(2 * j - 2))
            pl.when(j == n - 2)(late_gu.s3)
            stage(lambda u: gu_unit(u).s2(), 1, 1, n - 1)
            stage(lambda u: eng_gu.go(2, u), -1)
            tile(1)
            stage(lambda u: eng_gu.go(4, u), -2)
            stage(lambda u: gu_unit(u).s1(), 2, 2, n - 1)
            stage(lambda u: gu_unit(u).s0(), 2 + AHEAD, 2 + AHEAD, n - 1)
            pl.when(j == 0)(late_gu.s2)
            pl.when(jnp.logical_and(j >= 1, j < 7))(lambda: late_gu.piece(2 * j - 1))
            for i in range(dim // td):
                x = nt[i * td : (i + 1) * td, :]
                part[s, 0, i] = dg(x, gg[...], 1, 0).astype(BF).reshape(2, 2, 4, 32, f)
                part[s, 1, i] = dg(x, gu[...], 1, 0).astype(BF).reshape(2, 2, 4, 32, f)
            eng_gu.begin(j)
            stage(lambda u: gu_unit(u).s3(), 1, 1, n - 1)
            stage(lambda u: gu_unit(u).s4(), 1, 1, n - 1)
            pl.when(j == n - 2)(late_gu.s4)
            stage(lambda u: act_on(fetch(u, 1 - s), "start"), 1)
            pl.when(j >= 2)(lambda: put(b3, j - 2, s).wait())
            for i in range(f // 256):
                b3[s, i * 256 : (i + 1) * 256, :] = dg(act[:, i * 256 : (i + 1) * 256].T, gf[...], 1, 0).astype(BF)
            put(b3, j, s).start()
            eng_gu.go(1, j)
            stage(lambda u: eng_gu.go(3, u), -1)
            stage(lambda u: eng_gu.end(u), -2)
            return carry

        lax.fori_loop(0, n, body, 0)
        for j in (n - 2, n - 1):
            put(b3, j, j % 2).wait()

    pl.run_scoped(
        ffn, pltpu.VMEM((2, 32, 32, f), BF), pltpu.VMEM((2, 32, 32, f), BF), pltpu.VMEM((2, f, dim), BF),
        pltpu.VMEM((tok, f), BF), pltpu.VMEM((tok, f), BF), pltpu.VMEM((tok, f), BF),
        pltpu.VMEM((dim, tok), BF), pltpu.VMEM((2, f, dim), BF),
    )

    def load_down(u, r0, h):
        s = lax.rem(u, 2)
        return [pltpu.make_async_copy(gdown6.at[:, :, :, :, pl.ds(r0, h), pl.ds(512 * a, 512)],
                                      part.at[s, a, :, :, :, :, pl.ds(0, h)], vsem.at[2 + a]) for a in range(2)]

    def load_mid(u):
        return load_down(u, pl.multiple_of((u - n) * 32, 32), 32)

    def mixer_backward(gp, turn, wout):
        wcopy = pltpu.make_async_copy(wout_h, wout, vsem.at[0])
        act_on(load_mid(n), "start")
        wcopy.start()
        act_on(load_mid(n), "wait")
        eng_mid.begin(n)

        def turned(i, _):
            turn[:, cols(i, tt)] = nm[cols(i, tt), :].T
            return 0

        lax.fori_loop(0, nt_, turned, 0)
        mcopy = pltpu.make_async_copy(mix_h, nm, vsem.at[1])
        mcopy.start()
        wcopy.wait()

        def advance(u):
            for k, stage in ((0, 1), (1, 2), (2, 3), (3, 4)):
                if u - k < ndn + 5:
                    eng(u - k).go(stage, u - k)

        def grad_in(k, s):
            for i in range(2):
                for a in range(2):
                    t = dg(turn[512 * i : 512 * i + 512, :], gp[:, 1024 * k + 512 * a : 1024 * k + 512 * a + 512], 1, 0)
                    part[s, a, i] = t.astype(BF).reshape(2, 2, 4, 32, 512)

        def part_of(u):
            if u == ndn:
                for i in range(4):
                    t = dg(nm[:, 256 * i : 256 * i + 256].T, nf[...], 1, 0).astype(BF)
                    for a in range(2):
                        part[u % 2, a, i // 2, i % 2] = t[:, 512 * a : 512 * a + 512].reshape(2, 4, 32, 512)
            elif u < ndn + 4:
                grad_in(order[u - ndn - 1], u % 2)
            else:
                act_on(load_down(u, 128, 16), "start")
                act_on(load_down(u, 128, 16), "wait")

        def passes(ld, ost, tb, tb2):
            def fetch(i, s):
                r = cols(i, tt)
                return [pltpu.make_async_copy(bcx_h.at[k, r], ld.at[s, k], lsem.at[s, k]) for k in range(3)] + [
                    pltpu.make_async_copy(hid_h.at[r], ld.at[s, 3], lsem.at[s, 3])]

            def put_out(i):
                return pltpu.make_async_copy(ost, out_ref.at[cols(i, tt)], lsem.at[0, 4])

            act_on(fetch(0, 0), "start")
            tb[0:8, :] = halo_g[...]
            obuf[tok : tok + 8, :] = jnp.zeros((8, dim), F32)

            def two(i, s):
                r = cols(i, tt)
                tb2[...] = obuf[pl.ds(pl.multiple_of(i * tt, tt), tt + 8), :]
                k1, k2 = msk_ref[r, 3:4], msk_ref[r, 4:5]
                tb2[0:tt, :] = (vec[4:5, :] * tb2[0:tt, :] + vec[3:4, :] * (k1 * tb2[1 : 1 + tt, :])
                                + vec[2:3, :] * (k2 * tb2[2 : 2 + tt, :]))

                @pl.when(i == nt_ - 1)
                def _():
                    tb2[tt - 8 : tt, :] += edge_r[...]

                gg = tb2[0:tt, :]
                gp[r, 0:1024] = (gg * ld[s, 2]).astype(BF)
                gp[r, 2048:3072] = (gg * ld[s, 0]).astype(BF)

            def one(i, _):
                u = n + i
                s = lax.rem(i, 2)
                r = cols(i, tt)
                eng_mid.go(1, u)
                eng_mid.go(2, u - 1)
                pl.when(i >= 1)(lambda: eng_mid.go(3, u - 2))
                pl.when(i != 1)(lambda: eng_mid.go(4, jnp.where(i == 0, n - 2, u - 3)))
                pl.when(i + 1 < nt_)(lambda: act_on(load_mid(u + 1), "start"))
                act_on(fetch(i, s), "wait")
                pl.when(i >= 1)(lambda: put_out(i - 1).wait())
                ost[...] = obuf[r, :] * msk_ref[r, 2:3]
                put_out(i).start()
                v = ld[s, 3]
                g = gn[r, :]
                inv = inverse_rms(v)
                a = g * vec[1:2, :]
                dot = jnp.sum(a * v, axis=1, keepdims=True) / dim
                ghid = gf[r, :].astype(F32) + (inv * a - v * (inv * inv * inv) * dot)
                sm[1:2, :] += jnp.sum(g * v * inv, axis=0, keepdims=True)
                gn[r, :] = ghid
                low = ghid.astype(BF)
                nf[r, :] = low
                gm = dg(low, wout[...].reshape(dim, dim), 1, 1)
                tb[8 : 8 + tt, :] = ld[s, 0] * ld[s, 2]
                k1, k2 = msk_ref[r, 0:1], msk_ref[r, 1:2]
                gated, lag1, lag2 = tb[8 : 8 + tt, :], k1 * tb[7 : 7 + tt, :], k2 * tb[6 : 6 + tt, :]
                conv = vec[4:5, :] * gated + vec[3:4, :] * lag1 + vec[2:3, :] * lag2
                gp[r, 1024:2048] = (gm * conv).astype(BF)
                gc = gm * ld[s, 1]
                obuf[r, :] = gc
                sm[2:3, :] += jnp.sum(gc * lag2, axis=0, keepdims=True)
                sm[3:4, :] += jnp.sum(gc * lag1, axis=0, keepdims=True)
                sm[4:5, :] += jnp.sum(gc * gated, axis=0, keepdims=True)
                tb[0:8, :] = tb[tt : tt + 8, :]

                @pl.when(i == 0)
                def _():
                    first, second = obuf[0:1, :], obuf[1:2, :]
                    k1a, k2a, k2b = msk_ref[0:1, 0:1], msk_ref[0:1, 1:2], msk_ref[1:2, 1:2]
                    edge_s[6:7, :] = vec[2:3, :] * (k2a * first)
                    edge_s[7:8, :] = vec[3:4, :] * (k1a * first) + vec[2:3, :] * (k2b * second)
                    edge.start()

                pl.when(i >= 1)(lambda: two(i - 1, 1 - s))

                @pl.when(i + 1 < nt_)
                def _():
                    act_on(fetch(i + 1, 1 - s), "start")
                    act_on(load_mid(u + 1), "wait")
                    eng_mid.begin(u + 1)

                pl.when(i != 1)(lambda: eng_mid.end(jnp.where(i == 0, n - 2, u - 3)))
                return 0

            lax.fori_loop(0, nt_, one, 0)
            mcopy.wait()
            part_of(ndn)
            eng(ndn).begin(ndn)
            put_out(nt_ - 1).wait()
            edge.wait()
            two(nt_ - 1, (nt_ - 1) % 2)

        edge = remote(edge_s, edge_r, hsem.at[3], hsem.at[4], pc.zs[2])
        pl.run_scoped(passes, pltpu.VMEM((2, 4, tt, dim), F32), pltpu.VMEM((tt, dim), F32),
                      pltpu.VMEM((tt + 8, dim), F32), pltpu.VMEM((tt + 8, dim), F32))

        def ending(win, ost):
            wl = [pltpu.make_async_copy(win_h.at[:, :, pl.ds(1024 * i, 1024)], win.at[i], lsem.at[0, i]) for i in range(3)]
            act_on(wl, "start")

            def put_tok(i, s):
                return pltpu.make_async_copy(ost.at[s], gtok_ref.at[cols(i, tt)], lsem.at[s, 4])

            def grad_tok(i, _):
                s = lax.rem(i, 2)
                r = cols(i, tt)
                g = dg(gp[r, 0:1024], win[0].reshape(dim, dim), 1, 1)
                g = g + dg(gp[r, 1024:2048], win[1].reshape(dim, dim), 1, 1)
                g = g + dg(gp[r, 2048:3072], win[2].reshape(dim, dim), 1, 1)
                v = tok_ref[r, :].astype(F32)
                inv = inverse_rms(v)
                a = g * vec[0:1, :]
                dot = jnp.sum(a * v, axis=1, keepdims=True) / dim
                pl.when(i >= 2)(lambda: put_tok(i - 2, s).wait())
                ost[s] = gn[r, :] + (inv * a - v * (inv * inv * inv) * dot)
                put_tok(i, s).start()
                sm[0:1, :] += jnp.sum(g * v * inv, axis=0, keepdims=True)
                return 0

            for u in range(ndn, ndn + 8):
                advance(u)
                if u < ndn + 4:
                    part_of(u + 1)
                    eng(u + 1).begin(u + 1)
                if u == ndn:
                    act_on(wl, "wait")
                if u in (ndn + 1, ndn + 2):
                    lax.fori_loop(2 * (u - ndn - 1), 2 * (u - ndn), grad_tok, 0)
                if u == ndn + 2:
                    small_begin(0)
                elif u > ndn + 2 and u < ndn + 6:
                    small_end(u - ndn - 3)
                    small_begin(u - ndn - 2)
                elif u == ndn + 6:
                    small_end(3)
                    outs = pltpu.make_async_copy(sm, small_o, hsem.at[0])
                    outs.start()
                eng(u - 3).end(u - 3)
            outs.wait()
            for i in (nt_ - 2, nt_ - 1):
                put_tok(i, i % 2).wait()

        pl.run_scoped(ending, pltpu.VMEM((3, 32, 32, dim), BF), pltpu.VMEM((2, tt, dim), F32))

    pl.run_scoped(mixer_backward, pltpu.VMEM((tok, 3 * dim), BF), pltpu.VMEM((dim, tok), BF), pltpu.VMEM((32, 32, dim), BF))

    for u in range(8):
        unit(u).fin()
    late_down.fin()
    late_gu.fin()

    def last(j, carry):
        gu_unit(j).fin()
        return carry

    lax.fori_loop(0, n - 1, last, 0)


def block_call(tokens, cot, lengths, counts, vecs, w_in, w_out, w_gate, w_up, w_down):
    tok, dim = tokens.shape
    ff = w_gate.shape[1]
    n = ff // 512
    sd = jax.ShapeDtypeStruct
    outs = [
        sd((tok, dim), F32), sd((tok, dim), F32), sd((32, ff), F32), sd((32, ff), F32), sd((ff // 32, dim), F32),
        sd((32, dim), F32), sd((32, 3 * dim), F32), sd((8, dim), F32),
        sd((32, 32, 3 * dim), BF), sd((32, 32, dim), BF), sd((ff, dim), BF), sd((32, 2, 32, ff), BF),
        sd((32, 8, 128), F32), sd((3, tok, dim), F32), sd((tok, dim), F32), sd((tok, dim), BF), sd((ff, dim), BF),
    ]
    return pl.pallas_call(
        block_kernel,
        out_shape=outs,
        in_specs=[VM, ANY, VM, pl.BlockSpec(memory_space=pltpu.SMEM), VM, ANY, ANY, ANY, ANY, ANY],
        out_specs=[ANY] * len(outs),
        scratch_shapes=[
            pltpu.VMEM((tok + 8, dim), F32),
            pltpu.VMEM((tok, dim), F32),
            pltpu.VMEM((tok, dim), BF),
            pltpu.VMEM((tok, dim), BF),
            pltpu.VMEM((tok, dim), BF),
            pltpu.VMEM((tok, 128), F32),
            pltpu.VMEM((8, 128), jnp.int32),
            pltpu.VMEM((8, dim), F32),
            pltpu.VMEM((1, 8, 128), F32),
            pltpu.VMEM((8, dim), F32),
            pltpu.VMEM((6, 8, dim), F32),
            pltpu.VMEM((16, dim), BF),
            pltpu.VMEM((8, dim), F32),
            pltpu.VMEM((8, dim), F32),
            pltpu.VMEM((8, dim), F32),
            pltpu.SemaphoreType.DMA((4,)),
            pltpu.SemaphoreType.DMA((2, 5)),
            pltpu.SemaphoreType.DMA((5,)),
            pltpu.SemaphoreType.DMA((12,)),
            pltpu.SemaphoreType.DMA((n + 9, NG)),
            pltpu.SemaphoreType.DMA((n + 9, NG)),
        ] + scatter_scratch(n + 9, 32, 512),
        name="block",
        compiler_params=pltpu.CompilerParams(collective_id=1, has_side_effects=True, vmem_limit_bytes=62 * 2**20 + 2**19),
    )(tokens, cot, lengths, counts, vecs, w_in[None], w_out[None], w_gate[None], w_up[None], w_down)


def passed_along(array, axis, by):
    size = lax.axis_size(axis)
    pairs = [(i, i + by) for i in range(size) if 0 <= i + by < size]
    return lax.ppermute(array, axis, pairs)


def rms_forward(values, gain_vec):
    inv_rms = lax.rsqrt(jnp.mean(values * values, axis=1, keepdims=True) + epsilon)
    return (values * inv_rms * gain_vec[None, :], inv_rms)


def rms_backward(values, inv_rms, gain_vec, grad_normed):
    weighted = grad_normed * gain_vec[None, :]
    features = values.shape[1]
    total_dot = jnp.sum(weighted * values, axis=1, keepdims=True)
    grad_values = inv_rms * weighted - values * (inv_rms * inv_rms * inv_rms) * total_dot / features
    grad_gain = jnp.sum(grad_normed * values * inv_rms, axis=0)
    return (grad_values, grad_gain)


def outer_sum(left, right):
    return lax.dot_general(
        left, right, (((0,), (0,)), ((), ())), preferred_element_type=jnp.float32
    )


def back_product(grad_low, weight_mat):
    return lax.dot_general(
        grad_low, weight_mat, (((1,), (1,)), ((), ())), preferred_element_type=jnp.float32
    )


def doc_masks(doc_lengths, valid_count, first_pos, tok_count):
    packed_row = first_pos // ROW_LEN
    lengths = lax.dynamic_index_in_dim(doc_lengths, packed_row, 0, keepdims=False)
    limit_count = lax.dynamic_index_in_dim(valid_count, packed_row, 0, keepdims=False)
    offsets = jnp.cumsum(lengths) - lengths
    places = first_pos % ROW_LEN + jnp.arange(tok_count, dtype=jnp.int32)
    begins = jnp.any(offsets[None, :] == places[:, None], axis=1)
    before = jnp.any(offsets[None, :] == places[:, None] - 1, axis=1)
    keep_one = jnp.where(begins, 0.0, 1.0).astype(jnp.float32)
    keep_two = jnp.where(begins | before, 0.0, 1.0).astype(jnp.float32)
    live_mask = jnp.where(places < limit_count, 1.0, 0.0).astype(jnp.float32)
    return (keep_one[:, None], keep_two[:, None], live_mask[:, None])


def shards_plain(
    tokens,
    cotangent,
    gain_mix,
    in_weight,
    conv_taps,
    out_weight,
    gain_ffn,
    gate_weight,
    up_weight,
    down_weight,
    doc_lengths,
    valid_count,
):
    tok_count = tokens.shape[0]
    first_pos = lax.axis_index(("wide", "narrow")) * tok_count
    keep_one, keep_two, live_mask = doc_masks(doc_lengths, valid_count, first_pos, tok_count)
    full_gm, w_in, full_taps, w_out, full_gf, w_gate, w_up, w_down = (
        lax.all_gather(gain_mix, ("wide", "narrow"), axis=0, tiled=True),
        lax.all_gather(in_weight, ("wide", "narrow"), axis=0, tiled=True),
        lax.all_gather(conv_taps, ("wide", "narrow"), axis=1, tiled=True),
        lax.all_gather(out_weight, ("wide", "narrow"), axis=0, tiled=True),
        lax.all_gather(gain_ffn, ("wide", "narrow"), axis=0, tiled=True),
        lax.all_gather(gate_weight, ("wide", "narrow"), axis=0, tiled=True),
        lax.all_gather(up_weight, ("wide", "narrow"), axis=0, tiled=True),
        lax.all_gather(down_weight, ("wide", "narrow"), axis=0, tiled=True),
    )
    mix_gain = full_gm.astype(jnp.float32)
    ffn_gain = full_gf.astype(jnp.float32)
    taps = full_taps.astype(jnp.float32)
    features = tokens.shape[1]
    tok_float = tokens.astype(jnp.float32)
    normed_mix, inv_mix = rms_forward(tok_float, mix_gain)
    normed_low = normed_mix.astype(jnp.bfloat16)
    projected = jnp.dot(normed_low, w_in, preferred_element_type=jnp.float32)
    b_part = projected[:, :features]
    c_part = projected[:, features : 2 * features]
    x_part = projected[:, 2 * features :]
    gated = b_part * x_part
    edge_rows = passed_along(gated[-2:], "narrow", 1)
    extended = jnp.concatenate([edge_rows, gated], axis=0)
    lag_one = keep_one * extended[1:-1]
    lag_two = keep_two * extended[:-2]
    conv_out = taps[2][None, :] * gated + taps[1][None, :] * lag_one + taps[0][None, :] * lag_two
    mixed_low = (c_part * conv_out).astype(jnp.bfloat16)
    hidden_res = tok_float + jnp.dot(mixed_low, w_out, preferred_element_type=jnp.float32)
    normed_ffn, inv_ffn = rms_forward(hidden_res, ffn_gain)
    ffn_low = normed_ffn.astype(jnp.bfloat16)
    gate_val = jnp.dot(ffn_low, w_gate, preferred_element_type=jnp.float32)
    up_val = jnp.dot(ffn_low, w_up, preferred_element_type=jnp.float32)
    sigmoid_gate = jax.nn.sigmoid(gate_val)
    silu_val = gate_val * sigmoid_gate
    act_low = (silu_val * up_val).astype(jnp.bfloat16)
    ffn_out = jnp.dot(act_low, w_down, preferred_element_type=jnp.float32)
    output = live_mask * (hidden_res + ffn_out)
    again_gm, w_in, again_taps, w_out, again_gf, w_gate, w_up, w_down = (
        lax.all_gather(gain_mix, ("wide", "narrow"), axis=0, tiled=True),
        lax.all_gather(in_weight, ("wide", "narrow"), axis=0, tiled=True),
        lax.all_gather(conv_taps, ("wide", "narrow"), axis=1, tiled=True),
        lax.all_gather(out_weight, ("wide", "narrow"), axis=0, tiled=True),
        lax.all_gather(gain_ffn, ("wide", "narrow"), axis=0, tiled=True),
        lax.all_gather(gate_weight, ("wide", "narrow"), axis=0, tiled=True),
        lax.all_gather(up_weight, ("wide", "narrow"), axis=0, tiled=True),
        lax.all_gather(down_weight, ("wide", "narrow"), axis=0, tiled=True),
    )
    mix_gain = again_gm.astype(jnp.float32)
    ffn_gain = again_gf.astype(jnp.float32)
    taps = again_taps.astype(jnp.float32)
    grad_res = live_mask * cotangent.astype(jnp.float32)
    grad_ffn_low = grad_res.astype(jnp.bfloat16)
    grad_down = outer_sum(act_low, grad_ffn_low)
    grad_act = back_product(grad_ffn_low, w_down)
    grad_gate_low = (
        grad_act * up_val * sigmoid_gate * (1.0 + gate_val * (1.0 - sigmoid_gate))
    ).astype(jnp.bfloat16)
    grad_up_low = (grad_act * silu_val).astype(jnp.bfloat16)
    grad_gate = outer_sum(ffn_low, grad_gate_low)
    grad_up = outer_sum(ffn_low, grad_up_low)
    grad_nffn = back_product(grad_gate_low, w_gate) + back_product(grad_up_low, w_up)
    grad_hnorm, grad_gf = rms_backward(hidden_res, inv_ffn, ffn_gain, grad_nffn)
    grad_hidden = grad_res + grad_hnorm
    grad_mix_low = grad_hidden.astype(jnp.bfloat16)
    grad_out = outer_sum(mixed_low, grad_mix_low)
    grad_mixed = back_product(grad_mix_low, w_out)
    grad_c = grad_mixed * conv_out
    grad_conv = grad_mixed * c_part
    grad_taps = jnp.stack(
        [
            jnp.sum(grad_conv * lag_two, axis=0),
            jnp.sum(grad_conv * lag_one, axis=0),
            jnp.sum(grad_conv * gated, axis=0),
        ],
        axis=0,
    )
    lag_grad_one = taps[1][None, :] * keep_one * grad_conv
    lag_grad_two = taps[0][None, :] * keep_two * grad_conv
    grad_ext = (
        jnp.pad(taps[2][None, :] * grad_conv, ((2, 0), (0, 0)))
        + jnp.pad(lag_grad_one, ((1, 1), (0, 0)))
        + jnp.pad(lag_grad_two, ((0, 2), (0, 0)))
    )
    from_right = passed_along(grad_ext[:2], "narrow", -1)
    grad_gated = jnp.concatenate([grad_ext[2:-2], grad_ext[-2:] + from_right], axis=0)
    grad_b = grad_gated * x_part
    grad_x = grad_gated * b_part
    grad_proj_low = jnp.concatenate([grad_b, grad_c, grad_x], axis=1).astype(jnp.bfloat16)
    grad_in = outer_sum(normed_low, grad_proj_low)
    grad_nmix = back_product(grad_proj_low, w_in)
    grad_tnorm, grad_gm = rms_backward(tok_float, inv_mix, mix_gain, grad_nmix)
    grad_tokens = grad_hidden + grad_tnorm
    sum_gm, sum_in, sum_taps, sum_out, sum_gf, sum_gate, sum_up, sum_down = (
        lax.psum_scatter(grad_gm, ("wide", "narrow"), scatter_dimension=0, tiled=True),
        lax.psum_scatter(grad_in, ("wide", "narrow"), scatter_dimension=0, tiled=True),
        lax.psum_scatter(grad_taps, ("wide", "narrow"), scatter_dimension=1, tiled=True),
        lax.psum_scatter(grad_out, ("wide", "narrow"), scatter_dimension=0, tiled=True),
        lax.psum_scatter(grad_gf, ("wide", "narrow"), scatter_dimension=0, tiled=True),
        lax.psum_scatter(grad_gate, ("wide", "narrow"), scatter_dimension=0, tiled=True),
        lax.psum_scatter(grad_up, ("wide", "narrow"), scatter_dimension=0, tiled=True),
        lax.psum_scatter(grad_down, ("wide", "narrow"), scatter_dimension=0, tiled=True),
    )
    return (
        output,
        grad_tokens,
        sum_gm,
        sum_in,
        sum_taps,
        sum_out,
        sum_gf,
        sum_gate,
        sum_up,
        sum_down,
    )


def shards(
    tokens, cotangent, gain_mix, in_weight, conv_taps, out_weight, gain_ffn,
    gate_weight, up_weight, down_weight, doc_lengths, valid_count,
):
    me = lax.axis_index(("wide", "narrow"))
    own = gain_mix.shape[0]
    vecs = jnp.concatenate([gain_mix[None], gain_ffn[None], conv_taps], axis=0).astype(F32)
    vecs = jnp.pad(vecs, ((0, 3), (0, 128 - own)))
    output, grad_tokens, sum_gate, sum_up, sum_down, sum_out, sum_in, all_small = block_call(
        tokens, cotangent, doc_lengths, valid_count, vecs, in_weight, out_weight, gate_weight, up_weight, down_weight
    )[:8]
    mine = lax.dynamic_slice_in_dim(all_small, me * own, own, 1)
    return (output, grad_tokens, mine[0], sum_in, mine[2:5], sum_out, mine[1], sum_gate, sum_up, sum_down)


def solution(mesh):
    both = ("wide", "narrow")
    rows, vec, flat = P(both, None), P(both), P(None, both)
    step = shards if (mesh.shape["wide"], mesh.shape["narrow"]) == (8, 4) else shards_plain
    return jax.shard_map(
        step,
        mesh=mesh,
        in_specs=(rows, rows, vec, rows, flat, rows, vec, rows, rows, rows, P(), P()),
        out_specs=(rows, rows, vec, rows, flat, rows, vec, rows, rows, rows),
        check_vma=False,
    )
```

```python
import functools

import jax
import jax.numpy as jnp
from jax import lax
from jax.experimental import pallas as pl
from jax.experimental.pallas import tpu as pltpu
from jax.sharding import PartitionSpec as P

ROW_LEN = 4096
epsilon = 1e-05
F32 = jnp.float32
BF = jnp.bfloat16
MESH = pl.DeviceIdType.MESH
ANY = pl.BlockSpec(memory_space=pl.ANY)
VM = pl.BlockSpec(memory_space=pltpu.VMEM)


def dg(a, b, ca, cb):
    return lax.dot_general(a, b, (((ca,), (cb,)), ((), ())), preferred_element_type=F32)


class Place:
    def __init__(self):
        w = lax.axis_index("wide")
        z = lax.axis_index("narrow")
        c = lax.rem(w, 2)
        x = lax.rem(w // 2, 2)
        y = w // 4
        self.w, self.z, self.c, self.x, self.y = w, z, c, x, y
        self.core = (w + 1 - 2 * c, z)
        self.xn = (w + 2 - 4 * x, z)
        self.yn = (w + 4 - 8 * y, z)
        self.zs = [(w, lax.rem(z + k, 4)) for k in (1, 2, 3)]
        self.zto = [lax.rem(z + k, 4) for k in (1, 2, 3)]
        self.zfrom = [lax.rem(z + 4 - k, 4) for k in (1, 2, 3)]

        def base(yy, xx, cc):
            return 16 * yy + 8 * xx + 4 * cc

        self.own, self.xb = base(y, x, c), base(y, 1 - x, c)
        self.yb, self.db = base(1 - y, x, c), base(1 - y, 1 - x, c)
        self.sown, self.sxb = base(y, x, 1 - c), base(y, 1 - x, 1 - c)
        self.syb, self.sdb = base(1 - y, x, 1 - c), base(1 - y, 1 - x, 1 - c)
        self.me = self.own + z

    def greet(self):
        bar = pltpu.get_barrier_semaphore()
        peers = [self.core, self.xn, self.yn] + self.zs
        for p in peers:
            pl.semaphore_signal(bar, inc=1, device_id=p, device_id_type=MESH)
        pl.semaphore_wait(bar, len(peers))


def remote(src, dst, ss, rs, dev):
    return pltpu.make_async_remote_copy(
        src_ref=src, dst_ref=dst, send_sem=ss, recv_sem=rs, device_id=dev, device_id_type=MESH
    )


class Gather:
    def __init__(self, pc, src, dst, full, ss, rs):
        self.pc, self.src, self.dst, self.full, self.ss, self.rs = pc, src, dst, full, ss, rs
        self.parts = range(len(src))

    def zc(self, i, k):
        q = 3 * i + k
        return remote(self.src[i](), self.dst[i](self.pc.me, 1), self.ss.at[q], self.rs.at[q], self.pc.zs[k])

    def zr(self, i, k):
        q = 3 * i + k
        v = self.dst[i](self.pc.own + self.pc.zfrom[k], 1)
        return remote(v, v, self.ss.at[q], self.rs.at[q], self.pc.zs[k])

    def loc(self, i):
        return pltpu.make_async_copy(self.src[i](), self.dst[i](self.pc.me, 1), self.ss.at[14 + i])

    def cp(self, k, b, n, dev):
        v = self.full(b, n)
        return remote(v, v, self.ss.at[k], self.rs.at[k], dev)

    def s0(self):
        for i in self.parts:
            self.loc(i).start()
            for k in range(3):
                self.zc(i, k).start()

    def s1(self):
        p = self.pc
        for i in self.parts:
            self.loc(i).wait()
            for k in range(3):
                self.zr(i, k).wait_recv()
        self.cp(6, p.own, 4, p.xn).start()
        self.cp(7, p.own, 4, p.yn).start()
        self.cp(8, p.own, 4, p.core).start()

    def s2(self):
        p = self.pc
        self.cp(6, p.xb, 4, p.xn).wait_recv()
        self.cp(9, p.xb, 2, p.yn).start()
        self.cp(10, p.xb, 4, p.core).start()
        self.cp(7, p.yb, 4, p.yn).wait_recv()
        self.cp(11, p.yb + 2, 2, p.xn).start()
        self.cp(12, p.yb, 4, p.core).start()

    def s3(self):
        p = self.pc
        self.cp(9, p.db, 2, p.yn).wait_recv()
        self.cp(11, p.db + 2, 2, p.xn).wait_recv()
        self.cp(13, p.db, 4, p.core).start()

    def s4(self):
        p = self.pc
        for k, b in ((8, p.sown), (10, p.sxb), (12, p.syb), (13, p.sdb)):
            self.cp(k, b, 4, p.core).wait_recv()

    def fin(self):
        p = self.pc
        for i in self.parts:
            for k in range(3):
                self.zc(i, k).wait_send()
        for k, b, n in (
            (6, p.own, 4), (7, p.own, 4), (8, p.own, 4), (9, p.xb, 2),
            (10, p.xb, 4), (11, p.yb + 2, 2), (12, p.yb, 4), (13, p.db, 4),
        ):
            self.cp(k, b, n, p.core).wait_send()


class GatherLate:
    def __init__(self, pc, src, view, ss, rs):
        self.pc, self.src, self.view, self.ss, self.rs = pc, src, view, ss, rs

    def at(self, flip_y=0, flip_x=0, p=None):
        pc = self.pc
        return self.view(1 - pc.y if flip_y else pc.y, 1 - pc.x if flip_x else pc.x, pc.z, pc.c, p)

    def four(self, z, c=None):
        both = slice(None)
        return self.view(both, both, z, self.pc.c if c is None else c, None)

    def r(self, k, v, dev, src=None):
        return remote(v if src is None else src, v, self.ss.at[k], self.rs.at[k], dev)

    def loc(self, p):
        return pltpu.make_async_copy(self.src[p](), self.at(p=p), self.ss.at[14 + p])

    def own(self, p):
        v, src = self.at(p=p), self.src[p]()
        return [self.r(p, v, self.pc.xn, src), self.r(2 + p, v, self.pc.yn, src)]

    def s0(self):
        for p in (0, 1):
            self.loc(p).start()
            for c in self.own(p):
                c.start()

    def s1(self):
        pc = self.pc
        self.r(0, self.at(0, 1, 0), pc.xn).wait_recv()
        self.r(4, self.at(0, 1, 0), pc.yn).start()
        self.r(3, self.at(1, 0, 1), pc.yn).wait_recv()
        self.r(5, self.at(1, 0, 1), pc.xn).start()

    def s2(self):
        pc = self.pc
        for p in (0, 1):
            self.loc(p).wait()
        self.r(1, self.at(0, 1, 1), pc.xn).wait_recv()
        self.r(2, self.at(1, 0, 0), pc.yn).wait_recv()
        self.r(4, self.at(1, 1, 0), pc.yn).wait_recv()
        self.r(5, self.at(1, 1, 1), pc.xn).wait_recv()
        self.r(9, self.four(pc.z), pc.core).start()

    def piece(self, q):
        pc = self.pc
        k, i = lax.rem(q, 3), q // 3
        v = self.view(i // 2, lax.rem(i, 2), pc.z, pc.c, None)
        self.r(6 + k, v, (pc.w, lax.rem(pc.z + 1 + k, 4))).start()

    def s3(self):
        pc = self.pc
        for k in range(3):
            self.r(6 + k, self.four(pc.zfrom[k]), pc.zs[k]).wait_recv()
            self.r(10 + k, self.four(pc.zfrom[k]), pc.core).start()

    def s4(self):
        pc = self.pc
        self.r(9, self.four(pc.z, 1 - pc.c), pc.core).wait_recv()
        for k in range(3):
            self.r(10 + k, self.four(pc.zfrom[k], 1 - pc.c), pc.core).wait_recv()

    def fin(self):
        pc = self.pc
        for p in (0, 1):
            for c in self.own(p):
                c.wait_send()
        self.r(4, self.at(0, 1, 0), pc.yn).wait_send()
        self.r(5, self.at(1, 0, 1), pc.xn).wait_send()
        for k in range(3):
            self.r(6 + k, self.four(pc.z), pc.zs[k]).wait_send()
            self.r(10 + k, self.four(pc.zfrom[k]), pc.core).wait_send()
        self.r(9, self.four(pc.z), pc.core).wait_send()


NG = 16
NL = 4
AHEAD = 2
NS = 4


class Scatter:
    def __init__(self, pc, bufs, h, out):
        self.pc, self.h, self.out = pc, h, out
        (self.part, self.l0, self.ldx, self.ldy, self.lx, self.ly, self.lz,
         self.sd, self.sx, self.sy, self.so, self.sz, self.ob, self.ss, self.rs, self.os) = bufs

    def hr(self):
        return pl.ds(0, self.h)

    def c0(self, j, s):
        p = self.pc
        return remote(self.part.at[lax.rem(j, 2), :, :, :, 1 - p.c, :, self.hr()], self.l0.at[lax.rem(j, 3), :, :, :, :, self.hr()],
                      self.ss.at[j, 0], self.rs.at[j, 0], p.core)

    def cdx(self, j, s):
        return remote(self.sd.at[lax.rem(j, 2), :, pl.ds(0, 2), self.hr()], self.ldx.at[lax.rem(j, NL), :, :, self.hr()],
                      self.ss.at[j, 1], self.rs.at[j, 1], self.pc.xn)

    def cdy(self, j, s):
        return remote(self.sd.at[lax.rem(j, 2), :, pl.ds(2, 2), self.hr()], self.ldy.at[lax.rem(j, NL), :, :, self.hr()],
                      self.ss.at[j, 2], self.rs.at[j, 2], self.pc.yn)

    def cx(self, j, s):
        return remote(self.sx.at[s, :, :, self.hr()], self.lx.at[lax.rem(j, NL), :, :, self.hr()],
                      self.ss.at[j, 3], self.rs.at[j, 3], self.pc.xn)

    def cy(self, j, s):
        return remote(self.sy.at[s, :, :, self.hr()], self.ly.at[lax.rem(j, NL), :, :, self.hr()],
                      self.ss.at[j, 4], self.rs.at[j, 4], self.pc.yn)

    def cz(self, j, s, k):
        return remote(self.sz.at[lax.rem(j, 2), :, self.pc.zto[k], self.hr()], self.lz.at[lax.rem(j, NL), k, :, self.hr()],
                      self.ss.at[j, 5 + k], self.rs.at[j, 5 + k], self.pc.zs[k])

    def r0(self, j, s):
        self.c0(j, s).start()

    def q(self, j, s, a, yy, xx):
        hr = self.hr()
        return (self.part[lax.rem(j, 2), a, yy, xx, self.pc.c, :, hr].astype(F32)
                + self.l0[lax.rem(j, 3), a, yy, xx, :, hr].astype(F32))

    def r1(self, j, s):
        p, hr = self.pc, self.hr()
        self.c0(j, s).wait()
        for a in range(2):
            self.sd[lax.rem(j, 2), a, :, hr] = self.q(j, s, a, 1 - p.y, 1 - p.x).astype(BF)
        self.cdx(j, s).start()
        self.cdy(j, s).start()
        for a in range(2):
            self.sx[s, a, :, hr] = self.q(j, s, a, p.y, 1 - p.x).astype(BF)
            self.sy[s, a, :, hr] = self.q(j, s, a, 1 - p.y, p.x).astype(BF)
            self.so[s, a, :, hr] = self.q(j, s, a, p.y, p.x)

    def r2(self, j, s):
        hr = self.hr()
        lo, hi = pl.ds(0, 2), pl.ds(2, 2)
        self.cdx(j, s).wait()
        for a in range(2):
            self.sy[s, a, lo, hr] = (self.sy[s, a, lo, hr].astype(F32) + self.ldx[lax.rem(j, NL), a, :, hr].astype(F32)).astype(BF)
        self.cy(j, s).start()
        self.cdy(j, s).wait()
        for a in range(2):
            self.sx[s, a, hi, hr] = (self.sx[s, a, hi, hr].astype(F32) + self.ldy[lax.rem(j, NL), a, :, hr].astype(F32)).astype(BF)
        self.cx(j, s).start()

    def r3(self, j, s):
        hr = self.hr()
        self.cy(j, s).wait()
        self.cx(j, s).wait()
        for a in range(2):
            t = self.so[s, a, :, hr] + self.lx[lax.rem(j, NL), a, :, hr].astype(F32) + self.ly[lax.rem(j, NL), a, :, hr].astype(F32)
            self.so[s, a, :, hr] = t
            self.sz[lax.rem(j, 2), a, :, hr] = t.astype(BF)
        for k in range(3):
            self.cz(j, s, k).start()

    def r4(self, j, s):
        hr = self.hr()
        for k in range(3):
            self.cz(j, s, k).wait()
        for a in range(2):
            t = self.so[s, a, self.pc.z, hr]
            for k in range(3):
                t = t + self.lz[lax.rem(j, NL), k, a, hr].astype(F32)
            self.ob[s, a, hr] = t
        self.out(j, s, self.ob, self.os, "start")

    def go(self, stage, j):
        (self.r1, self.r2, self.r3, self.r4)[stage - 1](j, lax.rem(j, NS))

    def begin(self, j):
        self.r0(j, lax.rem(j, NS))

    def end(self, j):
        self.drain(j, lax.rem(j, NS))

    def drain(self, j, s):
        self.out(j, s, self.ob, self.os, "wait")


def scatter_scratch(n, h, w):
    return [
        pltpu.VMEM((2, 2, 2, 2, 2, 4, h, w), BF),
        pltpu.VMEM((3, 2, 2, 2, 4, h, w), BF),
        pltpu.VMEM((NL, 2, 2, h, w), BF),
        pltpu.VMEM((NL, 2, 2, h, w), BF),
        pltpu.VMEM((NL, 2, 4, h, w), BF),
        pltpu.VMEM((NL, 2, 4, h, w), BF),
        pltpu.VMEM((NL, 3, 2, h, w), BF),
        pltpu.VMEM((2, 2, 4, h, w), BF),
        pltpu.VMEM((NS, 2, 4, h, w), BF),
        pltpu.VMEM((NS, 2, 4, h, w), BF),
        pltpu.VMEM((NS, 2, 4, h, w), F32),
        pltpu.VMEM((2, 2, 4, h, w), BF),
        pltpu.VMEM((NS, 2, h, w), F32),
        pltpu.SemaphoreType.DMA((n, 8)),
        pltpu.SemaphoreType.DMA((n, 8)),
        pltpu.SemaphoreType.DMA((NS, 2)),
    ]


def inverse_rms(v):
    return lax.rsqrt(jnp.mean(v * v, axis=1, keepdims=True) + epsilon)


def block_kernel(
    tok_ref, cot_ref, doc_ref, count_ref, vec_ref, win_s, wout_s, wgate_s, wup_s, wdown_s,
    out_ref, gtok_ref, ggate_o, gup_o, gdown_o, gout_o, gin_o, small_o,
    win_h, wout_h, wd_h, wgu_h, vec_h, bcx_h, hid_h, mix_h, gdown_h,
    obuf, gn, nf, gf, nm, msk_ref, dlen, vec, vown, sm, sml, halo_t, halo_g, edge_s, edge_r,
    vsem, lsem, hsem, esem, gss, grs, *sc,
):
    pc = Place()
    tok, dim = tok_ref.shape
    ff = wgate_s.shape[-1]
    f = 512
    n = ff // f
    tt = 256
    nt_ = tok // tt
    part = sc[0]

    def cols(j, w=f):
        return pl.ds(pl.multiple_of(j * w, w), w)

    def simple(u, src, dst, c0, w):
        at = lambda b, m: dst.at[pl.ds(b, m), :, pl.ds(c0, w)]
        return Gather(pc, [lambda: src.at[:, :, pl.ds(c0, w)]], [at], at, gss.at[u], grs.at[u])

    def down_unit(i):
        rows = ff // 32
        at = lambda b, m: wd_h.at[pl.ds(pl.multiple_of(b * rows, rows), m * rows), pl.ds(256 * i, 256)]
        return Gather(pc, [lambda: wdown_s.at[:, pl.ds(256 * i, 256)]], [at], at, gss.at[5 + i], grs.at[5 + i])

    def gu_unit(j):
        srcs = [lambda: wgate_s.at[:, :, cols(j)], lambda: wup_s.at[:, :, cols(j)]]
        dsts = [lambda b, m: wgu_h.at[pl.ds(b, m), 0, :, cols(j)], lambda b, m: wgu_h.at[pl.ds(b, m), 1, :, cols(j)]]
        return Gather(pc, srcs, dsts, lambda b, m: wgu_h.at[pl.ds(b, m), :, :, cols(j)], gss.at[9 + j], grs.at[9 + j])

    def unit(u):
        if u == 0:
            return simple(0, vown, vec_h, 0, 128)
        if u < 4:
            return simple(u, win_s, win_h, 1024 * (u - 1), 1024)
        if u == 4:
            return simple(4, wout_s, wout_h, 0, 1024)
        if u < 9:
            return down_unit(u - 5)
        return gu_unit(u - 9)

    wd6 = wd_h.reshape(2, 2, 2, 4, ff // 32, dim)
    wgu7 = wgu_h.reshape(2, 2, 2, 4, 2, 32, ff)

    def down_view(y, x, z, c, p):
        return wd6.at[y, x, c, z, :, pl.ds(768, 256) if p is None else pl.ds(768 + 128 * p, 128)]

    def gu_view(y, x, z, c, p):
        return wgu7.at[y, x, c, z, slice(None) if p is None else p, :, pl.ds(ff - f, f)]

    late_down = GatherLate(pc, [lambda: wdown_s.at[:, pl.ds(768, 128)], lambda: wdown_s.at[:, pl.ds(896, 128)]],
                           down_view, gss.at[8], grs.at[8])
    late_gu = GatherLate(pc, [lambda: wgate_s.at[0, :, pl.ds(ff - f, f)], lambda: wup_s.at[0, :, pl.ds(ff - f, f)]],
                         gu_view, gss.at[8 + n], grs.at[8 + n])

    def small_copies(k):
        peers = [pc.core, pc.xn, pc.yn] + pc.zs
        return [remote(sm, sml.at[q], esem.at[q], esem.at[6 + q], peers[q]) for q in ((0,), (1,), (2,), (3, 4, 5))[k]]

    def small_begin(k):
        for c in small_copies(k):
            c.start()

    def small_end(k):
        for c in small_copies(k):
            c.wait()
        t = sm[...]
        for q in ((0,), (1,), (2,), (3, 4, 5))[k]:
            t = t + sml[q]
        sm[...] = t

    turn_of = [0, 1, 2, 3, 4, 5, 6, 7, 9, 10, 11, 12]

    def step(t):
        if t < 10:
            unit(turn_of[t]).s1()
            unit(turn_of[t + AHEAD]).s0()
        if t >= 2 and t < 10:
            unit(turn_of[t - 1]).s2()
        if t >= 3 and t < 11:
            unit(turn_of[t - 2]).s3()
        if t >= 4:
            unit(turn_of[t - 3]).s4()

    ndn = n + 4
    gdown6 = gdown_h.reshape(2, 2, 2, 4, ff // 32, dim)

    def act_on(copies, what):
        for c in copies:
            getattr(c, what)()

    def out_gu(j, s, ob, osem, what):
        act_on([pltpu.make_async_copy(ob.at[s, 0], ggate_o.at[:, cols(j)], osem.at[s, 0]),
                pltpu.make_async_copy(ob.at[s, 1], gup_o.at[:, cols(j)], osem.at[s, 1])], what)

    def out_rows(dst, r0, c0, h):
        def go(j, s, ob, osem, what):
            act_on([pltpu.make_async_copy(ob.at[s, a, pl.ds(0, h)],
                                          dst.at[pl.ds(r0, h), pl.ds(c0 + 512 * a, 512)], osem.at[s, a])
                    for a in range(2)], what)
        return go

    def out_down(j, s, ob, osem, what):
        out_rows(gdown_o, pl.multiple_of((j - n) * 32, 32), 0, 32)(j, s, ob, osem, what)

    def out_mixed(j, s, ob, osem, what):
        pl.when(j < n)(lambda: out_gu(j, s, ob, osem, what))
        pl.when(j >= n)(lambda: out_down(j, s, ob, osem, what))

    eng_gu = Scatter(pc, sc, 32, out_gu)
    eng_mid = Scatter(pc, sc, 32, out_mixed)
    order = (1, 0, 2)

    def eng(u):
        if u < ndn:
            return Scatter(pc, sc, 32, out_down)
        if u == ndn:
            return Scatter(pc, sc, 32, out_rows(gout_o, 0, 0, 32))
        if u < ndn + 4:
            return Scatter(pc, sc, 32, out_rows(gin_o, 0, 1024 * order[u - ndn - 1], 32))
        return Scatter(pc, sc, 16, out_rows(gdown_o, 128, 0, 16))

    pc.greet()
    vown[0] = pltpu.roll(vec_ref[...], 32 * pc.z, 1)
    unit(0).s0()
    unit(1).s0()
    cot_copy = pltpu.make_async_copy(cot_ref, gf, hsem.at[0])
    cot_copy.start()
    tail = remote(tok_ref.at[pl.ds(tok - 16, 16)], halo_t, hsem.at[1], hsem.at[2], pc.zs[0])
    tail.start()
    sm[...] = jnp.zeros_like(sm)
    edge_s[...] = jnp.zeros_like(edge_s)
    gn[...] = jnp.zeros_like(gn)
    row_devs = ROW_LEN // tok
    row = pc.me // row_devs
    dlen[...] = jnp.zeros_like(dlen)
    dlen[0:1, 0:16] = doc_ref[pl.ds(row, 1), :]
    lens = dlen[...]
    lane = lax.broadcasted_iota(jnp.int32, (8, 128), 1)
    sums = lens
    for k in (1, 2, 4, 8):
        sums = sums + jnp.where(lane >= k, pltpu.roll(sums, k, 1), 0)
    starts = jnp.where(lane < 16, sums - lens, -8)[0:1, :]
    limit = count_ref[row]
    cot_copy.wait()

    def live_rows(i, _):
        r = cols(i, tt)
        t = i * tt + lax.broadcasted_iota(jnp.int32, (tt, 128), 0)
        place = lax.rem(pc.me, row_devs) * tok + t

        def begins(by):
            return jnp.max(jnp.where(starts == place + by, 1.0, 0.0), axis=1, keepdims=True)

        b0, b1, b2, bm = begins(0), begins(1), begins(2), begins(-1)
        ln = lax.broadcasted_iota(jnp.int32, (tt, 128), 1)
        m = jnp.where(ln == 0, 1.0 - b0, 1.0 - jnp.maximum(b0, bm))
        m = jnp.where(ln == 2, jnp.where(place < limit, 1.0, 0.0), m)
        m = jnp.where(ln == 3, jnp.where(t + 1 < tok, 1.0 - b1, 0.0), m)
        msk_ref[r, :] = jnp.where(ln == 4, jnp.where(t + 2 < tok, 1.0 - jnp.maximum(b2, b1), 0.0), m)
        gf[r, :] = (gf[r, :].astype(F32) * msk_ref[r, 2:3]).astype(BF)
        return 0

    lax.fori_loop(0, nt_, live_rows, 0)
    unit(0).s1()
    unit(2).s0()
    late_down.s0()
    late_gu.s0()
    unit(1).s1()
    unit(3).s0()
    unit(0).s2()
    step(2)
    unit(0).s3()
    late_down.s1()
    late_gu.s1()
    step(3)
    late_down.s2()
    late_down.piece(0)
    unit(0).s4()

    def mixer_forward(vbuf, win, wout, st, mst, tb):
        vcopy = pltpu.make_async_copy(vec_h, vbuf, vsem.at[0])
        vcopy.start()
        vcopy.wait()
        for q in range(8):
            v = vbuf[4 * q] + vbuf[4 * q + 1] + vbuf[4 * q + 2] + vbuf[4 * q + 3]
            vec[:, 128 * q : 128 * q + 128] = v
        gain = vec[0:1, :]

        def normed(i, _):
            r = cols(i, tt)
            t = tok_ref[r, :].astype(F32)
            nm[r, :] = (t * inverse_rms(t) * gain).astype(BF)
            return 0

        lax.fori_loop(0, nt_, normed, 0)
        wl = [pltpu.make_async_copy(win_h.at[:, :, pl.ds(1024 * i, 1024)], win.at[i], vsem.at[i]) for i in range(3)]
        wl.append(pltpu.make_async_copy(wout_h, wout, vsem.at[3]))
        for t in (4, 5, 6, 7):
            step(t)
            late_down.piece(2 * t - 7)
            late_down.piece(2 * t - 6)
            wl[t - 4].start()
        tail.wait()
        th = halo_t[...].astype(F32)
        nh = (th * inverse_rms(th) * gain).astype(BF)
        for c in wl:
            c.wait()
        hb = dg(nh, win[0].reshape(dim, dim), 1, 0) * dg(nh, win[2].reshape(dim, dim), 1, 0)
        halo_g[...] = hb[8:16, :]
        tb[0:8, :] = halo_g[...]

        def stash(i, s):
            r = cols(i, tt)
            return [pltpu.make_async_copy(st.at[s, k], bcx_h.at[k, r], lsem.at[s, k]) for k in range(3)] + [
                pltpu.make_async_copy(mst.at[s], mix_h.at[r], lsem.at[s, 3]),
                pltpu.make_async_copy(obuf.at[r], hid_h.at[r], lsem.at[s, 4])]

        def tile(i, _):
            r = cols(i, tt)
            s = lax.rem(i, 2)
            pl.when(i >= 2)(lambda: act_on(stash(i - 2, s), "wait"))
            x = nm[r, :]
            bv = dg(x, win[0].reshape(dim, dim), 1, 0)
            st[s, 0] = bv
            xv = dg(x, win[2].reshape(dim, dim), 1, 0)
            st[s, 2] = xv
            tb[8 : 8 + tt, :] = bv * xv
            cv = dg(x, win[1].reshape(dim, dim), 1, 0)
            st[s, 1] = cv
            k1, k2 = msk_ref[r, 0:1], msk_ref[r, 1:2]
            conv = (vec[4:5, :] * tb[8 : 8 + tt, :] + vec[3:4, :] * (k1 * tb[7 : 7 + tt, :])
                    + vec[2:3, :] * (k2 * tb[6 : 6 + tt, :]))
            mixed = (cv * conv).astype(BF)
            mst[s] = mixed
            tb[0:8, :] = tb[tt : tt + 8, :]
            h = tok_ref[r, :].astype(F32) + dg(mixed, wout[...].reshape(dim, dim), 1, 0)
            obuf[r, :] = h
            nf[r, :] = (h * inverse_rms(h) * vec[1:2, :]).astype(BF)
            act_on(stash(i, s), "start")
            for k, t in ((0, 8), (1, 9), (3, 10)):
                pl.when(i == k)(functools.partial(step, t))
            pl.when(i < 3)(lambda: late_down.piece(9 + i))
            pl.when(i == 3)(late_down.s3)
            return 0

        lax.fori_loop(0, nt_, tile, 0)
        for i in (nt_ - 2, nt_ - 1):
            act_on(stash(i, i % 2), "wait")

    pl.run_scoped(
        mixer_forward, pltpu.VMEM((32, 8, 128), F32), pltpu.VMEM((3, 32, 32, dim), BF), pltpu.VMEM((32, 32, dim), BF),
        pltpu.VMEM((2, 3, tt, dim), F32), pltpu.VMEM((2, tt, dim), BF), pltpu.VMEM((tt + 8, dim), F32),
    )
    step(11)
    late_down.s4()

    def put(b3, j, s):
        return pltpu.make_async_copy(b3.at[s], gdown_h.at[cols(j), :], vsem.at[s])

    def ffn(gw, uw, dw, act, gg, gu, nt, b3):
        tm = td = 512

        def fetch(j, s):
            return [pltpu.make_async_copy(wgu_h.at[:, 0, :, cols(j)], gw.at[s], lsem.at[s, 0]),
                    pltpu.make_async_copy(wgu_h.at[:, 1, :, cols(j)], uw.at[s], lsem.at[s, 1]),
                    pltpu.make_async_copy(wd_h.at[cols(j), :], dw.at[s], lsem.at[s, 2])]

        act_on(fetch(0, 0), "start")

        def turned(i, _):
            nt[:, cols(i, tt)] = nf[cols(i, tt), :].T
            return 0

        lax.fori_loop(0, nt_, turned, 0)

        def body(j, carry):
            s = lax.rem(j, 2)

            def stage(fn, k, lo=0, hi=n):
                pl.when(jnp.logical_and(j + k >= lo, j + k < hi))(lambda: fn(j + k))

            act_on(fetch(j, s), "wait")

            def tile(i):
                r = pl.ds(i * tm, tm)
                x = nf[r, :]
                g_w, u_w = gw[s].reshape(dim, f), uw[s].reshape(dim, f)
                g = dg(x, g_w, 1, 0)
                u = dg(x, u_w, 1, 0)
                ga = dg(gf[r, :], dw[s], 1, 1)
                sg = jax.nn.sigmoid(g)
                si = g * sg
                a = (si * u).astype(BF)
                act[r, :] = a
                ggv = (ga * u * sg * (1.0 + g * (1.0 - sg))).astype(BF)
                guv = (ga * si).astype(BF)
                gg[r, :] = ggv
                gu[r, :] = guv
                obuf[r, :] += dg(a, dw[s], 1, 0)
                gn[r, :] += dg(ggv, g_w, 1, 1) + dg(guv, u_w, 1, 1)

            tile(0)
            pl.when(jnp.logical_and(j >= 1, j < 7))(lambda: late_gu.piece(2 * j - 2))
            pl.when(j == n - 2)(late_gu.s3)
            stage(lambda u: gu_unit(u).s2(), 1, 1, n - 1)
            stage(lambda u: eng_gu.go(2, u), -1)
            tile(1)
            stage(lambda u: eng_gu.go(4, u), -2)
            stage(lambda u: gu_unit(u).s1(), 2, 2, n - 1)
            stage(lambda u: gu_unit(u).s0(), 2 + AHEAD, 2 + AHEAD, n - 1)
            pl.when(j == 0)(late_gu.s2)
            pl.when(jnp.logical_and(j >= 1, j < 7))(lambda: late_gu.piece(2 * j - 1))
            for i in range(dim // td):
                x = nt[i * td : (i + 1) * td, :]
                part[s, 0, i] = dg(x, gg[...], 1, 0).astype(BF).reshape(2, 2, 4, 32, f)
                part[s, 1, i] = dg(x, gu[...], 1, 0).astype(BF).reshape(2, 2, 4, 32, f)
            eng_gu.begin(j)
            stage(lambda u: gu_unit(u).s3(), 1, 1, n - 1)
            stage(lambda u: gu_unit(u).s4(), 1, 1, n - 1)
            pl.when(j == n - 2)(late_gu.s4)
            stage(lambda u: act_on(fetch(u, 1 - s), "start"), 1)
            pl.when(j >= 2)(lambda: put(b3, j - 2, s).wait())
            for i in range(f // 256):
                b3[s, i * 256 : (i + 1) * 256, :] = dg(act[:, i * 256 : (i + 1) * 256].T, gf[...], 1, 0).astype(BF)
            put(b3, j, s).start()
            eng_gu.go(1, j)
            stage(lambda u: eng_gu.go(3, u), -1)
            stage(lambda u: eng_gu.end(u), -2)
            return carry

        lax.fori_loop(0, n, body, 0)
        for j in (n - 2, n - 1):
            put(b3, j, j % 2).wait()

    pl.run_scoped(
        ffn, pltpu.VMEM((2, 32, 32, f), BF), pltpu.VMEM((2, 32, 32, f), BF), pltpu.VMEM((2, f, dim), BF),
        pltpu.VMEM((tok, f), BF), pltpu.VMEM((tok, f), BF), pltpu.VMEM((tok, f), BF),
        pltpu.VMEM((dim, tok), BF), pltpu.VMEM((2, f, dim), BF),
    )

    def load_down(u, r0, h):
        s = lax.rem(u, 2)
        return [pltpu.make_async_copy(gdown6.at[:, :, :, :, pl.ds(r0, h), pl.ds(512 * a, 512)],
                                      part.at[s, a, :, :, :, :, pl.ds(0, h)], vsem.at[2 + a]) for a in range(2)]

    def load_mid(u):
        return load_down(u, pl.multiple_of((u - n) * 32, 32), 32)

    def mixer_backward(gp, turn, wout):
        wcopy = pltpu.make_async_copy(wout_h, wout, vsem.at[0])
        act_on(load_mid(n), "start")
        wcopy.start()
        act_on(load_mid(n), "wait")
        eng_mid.begin(n)

        def turned(i, _):
            turn[:, cols(i, tt)] = nm[cols(i, tt), :].T
            return 0

        lax.fori_loop(0, nt_, turned, 0)
        mcopy = pltpu.make_async_copy(mix_h, nm, vsem.at[1])
        mcopy.start()
        wcopy.wait()

        def advance(u):
            for k, stage in ((0, 1), (1, 2), (2, 3), (3, 4)):
                if u - k < ndn + 5:
                    eng(u - k).go(stage, u - k)

        def grad_in(k, s):
            for i in range(2):
                for a in range(2):
                    t = dg(turn[512 * i : 512 * i + 512, :], gp[:, 1024 * k + 512 * a : 1024 * k + 512 * a + 512], 1, 0)
                    part[s, a, i] = t.astype(BF).reshape(2, 2, 4, 32, 512)

        def part_of(u):
            if u == ndn:
                for i in range(4):
                    t = dg(nm[:, 256 * i : 256 * i + 256].T, nf[...], 1, 0).astype(BF)
                    for a in range(2):
                        part[u % 2, a, i // 2, i % 2] = t[:, 512 * a : 512 * a + 512].reshape(2, 4, 32, 512)
            elif u < ndn + 4:
                grad_in(order[u - ndn - 1], u % 2)
            else:
                act_on(load_down(u, 128, 16), "start")
                act_on(load_down(u, 128, 16), "wait")

        def passes(ld, ost, tb, tb2):
            def fetch(i, s):
                r = cols(i, tt)
                return [pltpu.make_async_copy(bcx_h.at[k, r], ld.at[s, k], lsem.at[s, k]) for k in range(3)] + [
                    pltpu.make_async_copy(hid_h.at[r], ld.at[s, 3], lsem.at[s, 3])]

            def put_out(i):
                return pltpu.make_async_copy(ost, out_ref.at[cols(i, tt)], lsem.at[0, 4])

            act_on(fetch(0, 0), "start")
            tb[0:8, :] = halo_g[...]
            obuf[tok : tok + 8, :] = jnp.zeros((8, dim), F32)

            def two(i, s):
                r = cols(i, tt)
                tb2[...] = obuf[pl.ds(pl.multiple_of(i * tt, tt), tt + 8), :]
                k1, k2 = msk_ref[r, 3:4], msk_ref[r, 4:5]
                tb2[0:tt, :] = (vec[4:5, :] * tb2[0:tt, :] + vec[3:4, :] * (k1 * tb2[1 : 1 + tt, :])
                                + vec[2:3, :] * (k2 * tb2[2 : 2 + tt, :]))

                @pl.when(i == nt_ - 1)
                def _():
                    tb2[tt - 8 : tt, :] += edge_r[...]

                gg = tb2[0:tt, :]
                gp[r, 0:1024] = (gg * ld[s, 2]).astype(BF)
                gp[r, 2048:3072] = (gg * ld[s, 0]).astype(BF)

            def one(i, _):
                u = n + i
                s = lax.rem(i, 2)
                r = cols(i, tt)
                eng_mid.go(1, u)
                eng_mid.go(2, u - 1)
                pl.when(i >= 1)(lambda: eng_mid.go(3, u - 2))
                pl.when(i != 1)(lambda: eng_mid.go(4, jnp.where(i == 0, n - 2, u - 3)))
                pl.when(i + 1 < nt_)(lambda: act_on(load_mid(u + 1), "start"))
                act_on(fetch(i, s), "wait")
                pl.when(i >= 1)(lambda: put_out(i - 1).wait())
                ost[...] = obuf[r, :] * msk_ref[r, 2:3]
                put_out(i).start()
                v = ld[s, 3]
                g = gn[r, :]
                inv = inverse_rms(v)
                a = g * vec[1:2, :]
                dot = jnp.sum(a * v, axis=1, keepdims=True) / dim
                ghid = gf[r, :].astype(F32) + (inv * a - v * (inv * inv * inv) * dot)
                sm[1:2, :] += jnp.sum(g * v * inv, axis=0, keepdims=True)
                gn[r, :] = ghid
                low = ghid.astype(BF)
                nf[r, :] = low
                gm = dg(low, wout[...].reshape(dim, dim), 1, 1)
                tb[8 : 8 + tt, :] = ld[s, 0] * ld[s, 2]
                k1, k2 = msk_ref[r, 0:1], msk_ref[r, 1:2]
                gated, lag1, lag2 = tb[8 : 8 + tt, :], k1 * tb[7 : 7 + tt, :], k2 * tb[6 : 6 + tt, :]
                conv = vec[4:5, :] * gated + vec[3:4, :] * lag1 + vec[2:3, :] * lag2
                gp[r, 1024:2048] = (gm * conv).astype(BF)
                gc = gm * ld[s, 1]
                obuf[r, :] = gc
                sm[2:3, :] += jnp.sum(gc * lag2, axis=0, keepdims=True)
                sm[3:4, :] += jnp.sum(gc * lag1, axis=0, keepdims=True)
                sm[4:5, :] += jnp.sum(gc * gated, axis=0, keepdims=True)
                tb[0:8, :] = tb[tt : tt + 8, :]

                @pl.when(i == 0)
                def _():
                    first, second = obuf[0:1, :], obuf[1:2, :]
                    k1a, k2a, k2b = msk_ref[0:1, 0:1], msk_ref[0:1, 1:2], msk_ref[1:2, 1:2]
                    edge_s[6:7, :] = vec[2:3, :] * (k2a * first)
                    edge_s[7:8, :] = vec[3:4, :] * (k1a * first) + vec[2:3, :] * (k2b * second)
                    edge.start()

                pl.when(i >= 1)(lambda: two(i - 1, 1 - s))

                @pl.when(i + 1 < nt_)
                def _():
                    act_on(fetch(i + 1, 1 - s), "start")
                    act_on(load_mid(u + 1), "wait")
                    eng_mid.begin(u + 1)

                pl.when(i != 1)(lambda: eng_mid.end(jnp.where(i == 0, n - 2, u - 3)))
                return 0

            lax.fori_loop(0, nt_, one, 0)
            mcopy.wait()
            part_of(ndn)
            eng(ndn).begin(ndn)
            put_out(nt_ - 1).wait()
            edge.wait()
            two(nt_ - 1, (nt_ - 1) % 2)

        edge = remote(edge_s, edge_r, hsem.at[3], hsem.at[4], pc.zs[2])
        pl.run_scoped(passes, pltpu.VMEM((2, 4, tt, dim), F32), pltpu.VMEM((tt, dim), F32),
                      pltpu.VMEM((tt + 8, dim), F32), pltpu.VMEM((tt + 8, dim), F32))

        def ending(win, ost):
            wl = [pltpu.make_async_copy(win_h.at[:, :, pl.ds(1024 * i, 1024)], win.at[i], lsem.at[0, i]) for i in range(3)]
            act_on(wl, "start")

            def put_tok(i, s):
                return pltpu.make_async_copy(ost.at[s], gtok_ref.at[cols(i, tt)], lsem.at[s, 4])

            def grad_tok(i, _):
                s = lax.rem(i, 2)
                r = cols(i, tt)
                g = dg(gp[r, 0:1024], win[0].reshape(dim, dim), 1, 1)
                g = g + dg(gp[r, 1024:2048], win[1].reshape(dim, dim), 1, 1)
                g = g + dg(gp[r, 2048:3072], win[2].reshape(dim, dim), 1, 1)
                v = tok_ref[r, :].astype(F32)
                inv = inverse_rms(v)
                a = g * vec[0:1, :]
                dot = jnp.sum(a * v, axis=1, keepdims=True) / dim
                pl.when(i >= 2)(lambda: put_tok(i - 2, s).wait())
                ost[s] = gn[r, :] + (inv * a - v * (inv * inv * inv) * dot)
                put_tok(i, s).start()
                sm[0:1, :] += jnp.sum(g * v * inv, axis=0, keepdims=True)
                return 0

            for u in range(ndn, ndn + 8):
                advance(u)
                if u < ndn + 4:
                    part_of(u + 1)
                    eng(u + 1).begin(u + 1)
                if u == ndn:
                    act_on(wl, "wait")
                if u in (ndn + 1, ndn + 2):
                    lax.fori_loop(2 * (u - ndn - 1), 2 * (u - ndn), grad_tok, 0)
                if u == ndn + 2:
                    small_begin(0)
                elif u > ndn + 2 and u < ndn + 6:
                    small_end(u - ndn - 3)
                    small_begin(u - ndn - 2)
                elif u == ndn + 6:
                    small_end(3)
                    outs = pltpu.make_async_copy(sm, small_o, hsem.at[0])
                    outs.start()
                eng(u - 3).end(u - 3)
            outs.wait()
            for i in (nt_ - 2, nt_ - 1):
                put_tok(i, i % 2).wait()

        pl.run_scoped(ending, pltpu.VMEM((3, 32, 32, dim), BF), pltpu.VMEM((2, tt, dim), F32))

    pl.run_scoped(mixer_backward, pltpu.VMEM((tok, 3 * dim), BF), pltpu.VMEM((dim, tok), BF), pltpu.VMEM((32, 32, dim), BF))

    for u in range(8):
        unit(u).fin()
    late_down.fin()
    late_gu.fin()

    def last(j, carry):
        gu_unit(j).fin()
        return carry

    lax.fori_loop(0, n - 1, last, 0)


def deliver_kernel(pieces, n, *refs):
    ins, outs, bufs, sems = refs[:n], refs[n : 2 * n], refs[2 * n : 3 * n], refs[3 * n]
    every = [(i, r) for i in range(n) for r in pieces[i]]
    load = [pltpu.make_async_copy(ins[i].at[pl.ds(*r)], bufs[i].at[pl.ds(*r)], sems.at[0, q]) for q, (i, r) in enumerate(every)]
    store = [pltpu.make_async_copy(bufs[i].at[pl.ds(*r)], outs[i].at[pl.ds(*r)], sems.at[1, q]) for q, (i, r) in enumerate(every)]
    for c in load:
        c.start()
    for c, d in zip(load, store):
        c.wait()
        d.start()
    for d in store:
        d.wait()


def deliver(arrays):
    n = len(arrays)
    pieces = []
    for a in arrays:
        rows = a.shape[0] // 8 if a.shape[0] % 64 == 0 else a.shape[0]
        pieces.append([(r, rows) for r in range(0, a.shape[0], rows)])
    return pl.pallas_call(
        functools.partial(deliver_kernel, pieces, n),
        out_shape=[jax.ShapeDtypeStruct(a.shape, a.dtype) for a in arrays],
        in_specs=[ANY] * n,
        out_specs=[ANY] * n,
        scratch_shapes=[pltpu.VMEM(a.shape, a.dtype) for a in arrays]
        + [pltpu.SemaphoreType.DMA((2, sum(map(len, pieces))))],
        name="deliver",
        compiler_params=pltpu.CompilerParams(vmem_limit_bytes=60 * 2**20),
    )(*arrays)


def block_call(tokens, cot, lengths, counts, vecs, w_in, w_out, w_gate, w_up, w_down):
    tok, dim = tokens.shape
    ff = w_gate.shape[1]
    n = ff // 512
    sd = jax.ShapeDtypeStruct
    outs = [
        sd((tok, dim), F32), sd((tok, dim), F32), sd((32, ff), F32), sd((32, ff), F32), sd((ff // 32, dim), F32),
        sd((32, dim), F32), sd((32, 3 * dim), F32), sd((8, dim), F32),
        sd((32, 32, 3 * dim), BF), sd((32, 32, dim), BF), sd((ff, dim), BF), sd((32, 2, 32, ff), BF),
        sd((32, 8, 128), F32), sd((3, tok, dim), F32), sd((tok, dim), F32), sd((tok, dim), BF), sd((ff, dim), BF),
    ]
    return pl.pallas_call(
        block_kernel,
        out_shape=outs,
        in_specs=[VM, ANY, VM, pl.BlockSpec(memory_space=pltpu.SMEM), VM, ANY, ANY, ANY, ANY, ANY],
        out_specs=[ANY] * len(outs),
        scratch_shapes=[
            pltpu.VMEM((tok + 8, dim), F32),
            pltpu.VMEM((tok, dim), F32),
            pltpu.VMEM((tok, dim), BF),
            pltpu.VMEM((tok, dim), BF),
            pltpu.VMEM((tok, dim), BF),
            pltpu.VMEM((tok, 128), F32),
            pltpu.VMEM((8, 128), jnp.int32),
            pltpu.VMEM((8, dim), F32),
            pltpu.VMEM((1, 8, 128), F32),
            pltpu.VMEM((8, dim), F32),
            pltpu.VMEM((6, 8, dim), F32),
            pltpu.VMEM((16, dim), BF),
            pltpu.VMEM((8, dim), F32),
            pltpu.VMEM((8, dim), F32),
            pltpu.VMEM((8, dim), F32),
            pltpu.SemaphoreType.DMA((4,)),
            pltpu.SemaphoreType.DMA((2, 5)),
            pltpu.SemaphoreType.DMA((5,)),
            pltpu.SemaphoreType.DMA((12,)),
            pltpu.SemaphoreType.DMA((n + 9, NG)),
            pltpu.SemaphoreType.DMA((n + 9, NG)),
        ] + scatter_scratch(n + 9, 32, 512),
        name="block",
        compiler_params=pltpu.CompilerParams(collective_id=1, has_side_effects=True, vmem_limit_bytes=62 * 2**20 + 2**19),
    )(tokens, cot, lengths, counts, vecs, w_in[None], w_out[None], w_gate[None], w_up[None], w_down)


def passed_along(array, axis, by):
    size = lax.axis_size(axis)
    pairs = [(i, i + by) for i in range(size) if 0 <= i + by < size]
    return lax.ppermute(array, axis, pairs)


def rms_forward(values, gain_vec):
    inv_rms = lax.rsqrt(jnp.mean(values * values, axis=1, keepdims=True) + epsilon)
    return (values * inv_rms * gain_vec[None, :], inv_rms)


def rms_backward(values, inv_rms, gain_vec, grad_normed):
    weighted = grad_normed * gain_vec[None, :]
    features = values.shape[1]
    total_dot = jnp.sum(weighted * values, axis=1, keepdims=True)
    grad_values = inv_rms * weighted - values * (inv_rms * inv_rms * inv_rms) * total_dot / features
    grad_gain = jnp.sum(grad_normed * values * inv_rms, axis=0)
    return (grad_values, grad_gain)


def outer_sum(left, right):
    return lax.dot_general(
        left, right, (((0,), (0,)), ((), ())), preferred_element_type=jnp.float32
    )


def back_product(grad_low, weight_mat):
    return lax.dot_general(
        grad_low, weight_mat, (((1,), (1,)), ((), ())), preferred_element_type=jnp.float32
    )


def doc_masks(doc_lengths, valid_count, first_pos, tok_count):
    packed_row = first_pos // ROW_LEN
    lengths = lax.dynamic_index_in_dim(doc_lengths, packed_row, 0, keepdims=False)
    limit_count = lax.dynamic_index_in_dim(valid_count, packed_row, 0, keepdims=False)
    offsets = jnp.cumsum(lengths) - lengths
    places = first_pos % ROW_LEN + jnp.arange(tok_count, dtype=jnp.int32)
    begins = jnp.any(offsets[None, :] == places[:, None], axis=1)
    before = jnp.any(offsets[None, :] == places[:, None] - 1, axis=1)
    keep_one = jnp.where(begins, 0.0, 1.0).astype(jnp.float32)
    keep_two = jnp.where(begins | before, 0.0, 1.0).astype(jnp.float32)
    live_mask = jnp.where(places < limit_count, 1.0, 0.0).astype(jnp.float32)
    return (keep_one[:, None], keep_two[:, None], live_mask[:, None])


def shards_plain(
    tokens,
    cotangent,
    gain_mix,
    in_weight,
    conv_taps,
    out_weight,
    gain_ffn,
    gate_weight,
    up_weight,
    down_weight,
    doc_lengths,
    valid_count,
):
    tok_count = tokens.shape[0]
    first_pos = lax.axis_index(("wide", "narrow")) * tok_count
    keep_one, keep_two, live_mask = doc_masks(doc_lengths, valid_count, first_pos, tok_count)
    full_gm, w_in, full_taps, w_out, full_gf, w_gate, w_up, w_down = (
        lax.all_gather(gain_mix, ("wide", "narrow"), axis=0, tiled=True),
        lax.all_gather(in_weight, ("wide", "narrow"), axis=0, tiled=True),
        lax.all_gather(conv_taps, ("wide", "narrow"), axis=1, tiled=True),
        lax.all_gather(out_weight, ("wide", "narrow"), axis=0, tiled=True),
        lax.all_gather(gain_ffn, ("wide", "narrow"), axis=0, tiled=True),
        lax.all_gather(gate_weight, ("wide", "narrow"), axis=0, tiled=True),
        lax.all_gather(up_weight, ("wide", "narrow"), axis=0, tiled=True),
        lax.all_gather(down_weight, ("wide", "narrow"), axis=0, tiled=True),
    )
    mix_gain = full_gm.astype(jnp.float32)
    ffn_gain = full_gf.astype(jnp.float32)
    taps = full_taps.astype(jnp.float32)
    features = tokens.shape[1]
    tok_float = tokens.astype(jnp.float32)
    normed_mix, inv_mix = rms_forward(tok_float, mix_gain)
    normed_low = normed_mix.astype(jnp.bfloat16)
    projected = jnp.dot(normed_low, w_in, preferred_element_type=jnp.float32)
    b_part = projected[:, :features]
    c_part = projected[:, features : 2 * features]
    x_part = projected[:, 2 * features :]
    gated = b_part * x_part
    edge_rows = passed_along(gated[-2:], "narrow", 1)
    extended = jnp.concatenate([edge_rows, gated], axis=0)
    lag_one = keep_one * extended[1:-1]
    lag_two = keep_two * extended[:-2]
    conv_out = taps[2][None, :] * gated + taps[1][None, :] * lag_one + taps[0][None, :] * lag_two
    mixed_low = (c_part * conv_out).astype(jnp.bfloat16)
    hidden_res = tok_float + jnp.dot(mixed_low, w_out, preferred_element_type=jnp.float32)
    normed_ffn, inv_ffn = rms_forward(hidden_res, ffn_gain)
    ffn_low = normed_ffn.astype(jnp.bfloat16)
    gate_val = jnp.dot(ffn_low, w_gate, preferred_element_type=jnp.float32)
    up_val = jnp.dot(ffn_low, w_up, preferred_element_type=jnp.float32)
    sigmoid_gate = jax.nn.sigmoid(gate_val)
    silu_val = gate_val * sigmoid_gate
    act_low = (silu_val * up_val).astype(jnp.bfloat16)
    ffn_out = jnp.dot(act_low, w_down, preferred_element_type=jnp.float32)
    output = live_mask * (hidden_res + ffn_out)
    again_gm, w_in, again_taps, w_out, again_gf, w_gate, w_up, w_down = (
        lax.all_gather(gain_mix, ("wide", "narrow"), axis=0, tiled=True),
        lax.all_gather(in_weight, ("wide", "narrow"), axis=0, tiled=True),
        lax.all_gather(conv_taps, ("wide", "narrow"), axis=1, tiled=True),
        lax.all_gather(out_weight, ("wide", "narrow"), axis=0, tiled=True),
        lax.all_gather(gain_ffn, ("wide", "narrow"), axis=0, tiled=True),
        lax.all_gather(gate_weight, ("wide", "narrow"), axis=0, tiled=True),
        lax.all_gather(up_weight, ("wide", "narrow"), axis=0, tiled=True),
        lax.all_gather(down_weight, ("wide", "narrow"), axis=0, tiled=True),
    )
    mix_gain = again_gm.astype(jnp.float32)
    ffn_gain = again_gf.astype(jnp.float32)
    taps = again_taps.astype(jnp.float32)
    grad_res = live_mask * cotangent.astype(jnp.float32)
    grad_ffn_low = grad_res.astype(jnp.bfloat16)
    grad_down = outer_sum(act_low, grad_ffn_low)
    grad_act = back_product(grad_ffn_low, w_down)
    grad_gate_low = (
        grad_act * up_val * sigmoid_gate * (1.0 + gate_val * (1.0 - sigmoid_gate))
    ).astype(jnp.bfloat16)
    grad_up_low = (grad_act * silu_val).astype(jnp.bfloat16)
    grad_gate = outer_sum(ffn_low, grad_gate_low)
    grad_up = outer_sum(ffn_low, grad_up_low)
    grad_nffn = back_product(grad_gate_low, w_gate) + back_product(grad_up_low, w_up)
    grad_hnorm, grad_gf = rms_backward(hidden_res, inv_ffn, ffn_gain, grad_nffn)
    grad_hidden = grad_res + grad_hnorm
    grad_mix_low = grad_hidden.astype(jnp.bfloat16)
    grad_out = outer_sum(mixed_low, grad_mix_low)
    grad_mixed = back_product(grad_mix_low, w_out)
    grad_c = grad_mixed * conv_out
    grad_conv = grad_mixed * c_part
    grad_taps = jnp.stack(
        [
            jnp.sum(grad_conv * lag_two, axis=0),
            jnp.sum(grad_conv * lag_one, axis=0),
            jnp.sum(grad_conv * gated, axis=0),
        ],
        axis=0,
    )
    lag_grad_one = taps[1][None, :] * keep_one * grad_conv
    lag_grad_two = taps[0][None, :] * keep_two * grad_conv
    grad_ext = (
        jnp.pad(taps[2][None, :] * grad_conv, ((2, 0), (0, 0)))
        + jnp.pad(lag_grad_one, ((1, 1), (0, 0)))
        + jnp.pad(lag_grad_two, ((0, 2), (0, 0)))
    )
    from_right = passed_along(grad_ext[:2], "narrow", -1)
    grad_gated = jnp.concatenate([grad_ext[2:-2], grad_ext[-2:] + from_right], axis=0)
    grad_b = grad_gated * x_part
    grad_x = grad_gated * b_part
    grad_proj_low = jnp.concatenate([grad_b, grad_c, grad_x], axis=1).astype(jnp.bfloat16)
    grad_in = outer_sum(normed_low, grad_proj_low)
    grad_nmix = back_product(grad_proj_low, w_in)
    grad_tnorm, grad_gm = rms_backward(tok_float, inv_mix, mix_gain, grad_nmix)
    grad_tokens = grad_hidden + grad_tnorm
    sum_gm, sum_in, sum_taps, sum_out, sum_gf, sum_gate, sum_up, sum_down = (
        lax.psum_scatter(grad_gm, ("wide", "narrow"), scatter_dimension=0, tiled=True),
        lax.psum_scatter(grad_in, ("wide", "narrow"), scatter_dimension=0, tiled=True),
        lax.psum_scatter(grad_taps, ("wide", "narrow"), scatter_dimension=1, tiled=True),
        lax.psum_scatter(grad_out, ("wide", "narrow"), scatter_dimension=0, tiled=True),
        lax.psum_scatter(grad_gf, ("wide", "narrow"), scatter_dimension=0, tiled=True),
        lax.psum_scatter(grad_gate, ("wide", "narrow"), scatter_dimension=0, tiled=True),
        lax.psum_scatter(grad_up, ("wide", "narrow"), scatter_dimension=0, tiled=True),
        lax.psum_scatter(grad_down, ("wide", "narrow"), scatter_dimension=0, tiled=True),
    )
    return (
        output,
        grad_tokens,
        sum_gm,
        sum_in,
        sum_taps,
        sum_out,
        sum_gf,
        sum_gate,
        sum_up,
        sum_down,
    )


def shards(
    tokens, cotangent, gain_mix, in_weight, conv_taps, out_weight, gain_ffn,
    gate_weight, up_weight, down_weight, doc_lengths, valid_count,
):
    me = lax.axis_index(("wide", "narrow"))
    own = gain_mix.shape[0]
    vecs = jnp.concatenate([gain_mix[None], gain_ffn[None], conv_taps], axis=0).astype(F32)
    vecs = jnp.pad(vecs, ((0, 3), (0, 128 - own)))
    output, grad_tokens, sum_gate, sum_up, sum_down, sum_out, sum_in, all_small = block_call(
        tokens, cotangent, doc_lengths, valid_count, vecs, in_weight, out_weight, gate_weight, up_weight, down_weight
    )[:8]
    output, grad_tokens, sum_gate, sum_up, sum_down, sum_out, sum_in = deliver(
        [output, grad_tokens, sum_gate, sum_up, sum_down, sum_out, sum_in]
    )
    mine = lax.dynamic_slice_in_dim(all_small, me * own, own, 1)
    return (output, grad_tokens, mine[0], sum_in, mine[2:5], sum_out, mine[1], sum_gate, sum_up, sum_down)


def solution(mesh):
    both = ("wide", "narrow")
    rows, vec, flat = P(both, None), P(both), P(None, both)
    step = shards if (mesh.shape["wide"], mesh.shape["narrow"]) == (8, 4) else shards_plain
    return jax.shard_map(
        step,
        mesh=mesh,
        in_specs=(rows, rows, vec, rows, flat, rows, vec, rows, rows, rows, P(), P()),
        out_specs=(rows, rows, vec, rows, flat, rows, vec, rows, rows, rows),
        check_vma=False,
    )
```

```python
import functools

import jax
import jax.numpy as jnp
from jax import lax
from jax.experimental import pallas as pl
from jax.experimental.pallas import tpu as pltpu
from jax.sharding import PartitionSpec as P

ROW_LEN = 4096
epsilon = 1e-05
F32 = jnp.float32
BF = jnp.bfloat16
MESH = pl.DeviceIdType.MESH
ANY = pl.BlockSpec(memory_space=pl.ANY)
VM = pl.BlockSpec(memory_space=pltpu.VMEM)


def dg(a, b, ca, cb):
    return lax.dot_general(a, b, (((ca,), (cb,)), ((), ())), preferred_element_type=F32)


class Place:
    def __init__(self):
        w = lax.axis_index("wide")
        z = lax.axis_index("narrow")
        c = lax.rem(w, 2)
        x = lax.rem(w // 2, 2)
        y = w // 4
        self.w, self.z, self.c, self.x, self.y = w, z, c, x, y
        self.core = (w + 1 - 2 * c, z)
        self.xn = (w + 2 - 4 * x, z)
        self.yn = (w + 4 - 8 * y, z)
        self.zs = [(w, lax.rem(z + k, 4)) for k in (1, 2, 3)]
        self.zto = [lax.rem(z + k, 4) for k in (1, 2, 3)]
        self.zfrom = [lax.rem(z + 4 - k, 4) for k in (1, 2, 3)]

        def base(yy, xx, cc):
            return 16 * yy + 8 * xx + 4 * cc

        self.own, self.xb = base(y, x, c), base(y, 1 - x, c)
        self.yb, self.db = base(1 - y, x, c), base(1 - y, 1 - x, c)
        self.sown, self.sxb = base(y, x, 1 - c), base(y, 1 - x, 1 - c)
        self.syb, self.sdb = base(1 - y, x, 1 - c), base(1 - y, 1 - x, 1 - c)
        self.me = self.own + z

    def greet(self):
        bar = pltpu.get_barrier_semaphore()
        peers = [self.core, self.xn, self.yn] + self.zs
        for p in peers:
            pl.semaphore_signal(bar, inc=1, device_id=p, device_id_type=MESH)
        pl.semaphore_wait(bar, len(peers))


def remote(src, dst, ss, rs, dev):
    return pltpu.make_async_remote_copy(
        src_ref=src, dst_ref=dst, send_sem=ss, recv_sem=rs, device_id=dev, device_id_type=MESH
    )


class Gather:
    def __init__(self, pc, src, dst, full, ss, rs):
        self.pc, self.src, self.dst, self.full, self.ss, self.rs = pc, src, dst, full, ss, rs
        self.parts = range(len(src))

    def zc(self, i, k):
        q = 3 * i + k
        return remote(self.src[i](), self.dst[i](self.pc.me, 1), self.ss.at[q], self.rs.at[q], self.pc.zs[k])

    def zr(self, i, k):
        q = 3 * i + k
        v = self.dst[i](self.pc.own + self.pc.zfrom[k], 1)
        return remote(v, v, self.ss.at[q], self.rs.at[q], self.pc.zs[k])

    def loc(self, i):
        return pltpu.make_async_copy(self.src[i](), self.dst[i](self.pc.me, 1), self.ss.at[14 + i])

    def cp(self, k, b, n, dev):
        v = self.full(b, n)
        return remote(v, v, self.ss.at[k], self.rs.at[k], dev)

    def s0(self):
        for i in self.parts:
            self.loc(i).start()
            for k in range(3):
                self.zc(i, k).start()

    def s1(self):
        p = self.pc
        for i in self.parts:
            self.loc(i).wait()
            for k in range(3):
                self.zr(i, k).wait_recv()
        self.cp(6, p.own, 4, p.xn).start()
        self.cp(7, p.own, 4, p.yn).start()
        self.cp(8, p.own, 4, p.core).start()

    def s2(self):
        p = self.pc
        self.cp(6, p.xb, 4, p.xn).wait_recv()
        self.cp(9, p.xb, 2, p.yn).start()
        self.cp(10, p.xb, 4, p.core).start()
        self.cp(7, p.yb, 4, p.yn).wait_recv()
        self.cp(11, p.yb + 2, 2, p.xn).start()
        self.cp(12, p.yb, 4, p.core).start()

    def s3(self):
        p = self.pc
        self.cp(9, p.db, 2, p.yn).wait_recv()
        self.cp(11, p.db + 2, 2, p.xn).wait_recv()
        self.cp(13, p.db, 4, p.core).start()

    def s4(self):
        p = self.pc
        for k, b in ((8, p.sown), (10, p.sxb), (12, p.syb), (13, p.sdb)):
            self.cp(k, b, 4, p.core).wait_recv()

    def fin(self):
        p = self.pc
        for i in self.parts:
            for k in range(3):
                self.zc(i, k).wait_send()
        for k, b, n in (
            (6, p.own, 4), (7, p.own, 4), (8, p.own, 4), (9, p.xb, 2),
            (10, p.xb, 4), (11, p.yb + 2, 2), (12, p.yb, 4), (13, p.db, 4),
        ):
            self.cp(k, b, n, p.core).wait_send()


class GatherLate:
    def __init__(self, pc, src, view, ss, rs):
        self.pc, self.src, self.view, self.ss, self.rs = pc, src, view, ss, rs

    def at(self, flip_y=0, flip_x=0, p=None):
        pc = self.pc
        return self.view(1 - pc.y if flip_y else pc.y, 1 - pc.x if flip_x else pc.x, pc.z, pc.c, p)

    def four(self, z, c=None):
        both = slice(None)
        return self.view(both, both, z, self.pc.c if c is None else c, None)

    def r(self, k, v, dev, src=None):
        return remote(v if src is None else src, v, self.ss.at[k], self.rs.at[k], dev)

    def loc(self, p):
        return pltpu.make_async_copy(self.src[p](), self.at(p=p), self.ss.at[14 + p])

    def own(self, p):
        v, src = self.at(p=p), self.src[p]()
        return [self.r(p, v, self.pc.xn, src), self.r(2 + p, v, self.pc.yn, src)]

    def s0(self):
        for p in (0, 1):
            self.loc(p).start()
            for c in self.own(p):
                c.start()

    def s1(self):
        pc = self.pc
        self.r(0, self.at(0, 1, 0), pc.xn).wait_recv()
        self.r(4, self.at(0, 1, 0), pc.yn).start()
        self.r(3, self.at(1, 0, 1), pc.yn).wait_recv()
        self.r(5, self.at(1, 0, 1), pc.xn).start()

    def s2(self):
        pc = self.pc
        for p in (0, 1):
            self.loc(p).wait()
        self.r(1, self.at(0, 1, 1), pc.xn).wait_recv()
        self.r(2, self.at(1, 0, 0), pc.yn).wait_recv()
        self.r(4, self.at(1, 1, 0), pc.yn).wait_recv()
        self.r(5, self.at(1, 1, 1), pc.xn).wait_recv()
        self.r(9, self.four(pc.z), pc.core).start()

    def piece(self, q):
        pc = self.pc
        k, i = lax.rem(q, 3), q // 3
        v = self.view(i // 2, lax.rem(i, 2), pc.z, pc.c, None)
        self.r(6 + k, v, (pc.w, lax.rem(pc.z + 1 + k, 4))).start()

    def s3(self):
        pc = self.pc
        for k in range(3):
            self.r(6 + k, self.four(pc.zfrom[k]), pc.zs[k]).wait_recv()
            self.r(10 + k, self.four(pc.zfrom[k]), pc.core).start()

    def s4(self):
        pc = self.pc
        self.r(9, self.four(pc.z, 1 - pc.c), pc.core).wait_recv()
        for k in range(3):
            self.r(10 + k, self.four(pc.zfrom[k], 1 - pc.c), pc.core).wait_recv()

    def fin(self):
        pc = self.pc
        for p in (0, 1):
            for c in self.own(p):
                c.wait_send()
        self.r(4, self.at(0, 1, 0), pc.yn).wait_send()
        self.r(5, self.at(1, 0, 1), pc.xn).wait_send()
        for k in range(3):
            self.r(6 + k, self.four(pc.z), pc.zs[k]).wait_send()
            self.r(10 + k, self.four(pc.zfrom[k]), pc.core).wait_send()
        self.r(9, self.four(pc.z), pc.core).wait_send()


NG = 16
NL = 4
AHEAD = 2
NS = 4


class Scatter:
    def __init__(self, pc, bufs, h, out):
        self.pc, self.h, self.out = pc, h, out
        (self.part, self.l0, self.ldx, self.ldy, self.lx, self.ly, self.lz,
         self.sd, self.sx, self.sy, self.so, self.sz, self.ob, self.ss, self.rs, self.os) = bufs

    def hr(self):
        return pl.ds(0, self.h)

    def c0(self, j, s):
        p = self.pc
        return remote(self.part.at[lax.rem(j, 2), :, :, :, 1 - p.c, :, self.hr()], self.l0.at[lax.rem(j, 3), :, :, :, :, self.hr()],
                      self.ss.at[j, 0], self.rs.at[j, 0], p.core)

    def cdx(self, j, s):
        return remote(self.sd.at[lax.rem(j, 2), :, pl.ds(0, 2), self.hr()], self.ldx.at[lax.rem(j, NL), :, :, self.hr()],
                      self.ss.at[j, 1], self.rs.at[j, 1], self.pc.xn)

    def cdy(self, j, s):
        return remote(self.sd.at[lax.rem(j, 2), :, pl.ds(2, 2), self.hr()], self.ldy.at[lax.rem(j, NL), :, :, self.hr()],
                      self.ss.at[j, 2], self.rs.at[j, 2], self.pc.yn)

    def cx(self, j, s):
        return remote(self.sx.at[s, :, :, self.hr()], self.lx.at[lax.rem(j, NL), :, :, self.hr()],
                      self.ss.at[j, 3], self.rs.at[j, 3], self.pc.xn)

    def cy(self, j, s):
        return remote(self.sy.at[s, :, :, self.hr()], self.ly.at[lax.rem(j, NL), :, :, self.hr()],
                      self.ss.at[j, 4], self.rs.at[j, 4], self.pc.yn)

    def cz(self, j, s, k):
        return remote(self.sz.at[lax.rem(j, 2), :, self.pc.zto[k], self.hr()], self.lz.at[lax.rem(j, NL), k, :, self.hr()],
                      self.ss.at[j, 5 + k], self.rs.at[j, 5 + k], self.pc.zs[k])

    def r0(self, j, s):
        self.c0(j, s).start()

    def q(self, j, s, a, yy, xx):
        hr = self.hr()
        return (self.part[lax.rem(j, 2), a, yy, xx, self.pc.c, :, hr].astype(F32)
                + self.l0[lax.rem(j, 3), a, yy, xx, :, hr].astype(F32))

    def r1(self, j, s):
        p, hr = self.pc, self.hr()
        self.c0(j, s).wait()
        for a in range(2):
            self.sd[lax.rem(j, 2), a, :, hr] = self.q(j, s, a, 1 - p.y, 1 - p.x).astype(BF)
        self.cdx(j, s).start()
        self.cdy(j, s).start()
        for a in range(2):
            self.sx[s, a, :, hr] = self.q(j, s, a, p.y, 1 - p.x).astype(BF)
            self.sy[s, a, :, hr] = self.q(j, s, a, 1 - p.y, p.x).astype(BF)
            self.so[s, a, :, hr] = self.q(j, s, a, p.y, p.x)

    def r2(self, j, s):
        hr = self.hr()
        lo, hi = pl.ds(0, 2), pl.ds(2, 2)
        self.cdx(j, s).wait()
        for a in range(2):
            self.sy[s, a, lo, hr] = (self.sy[s, a, lo, hr].astype(F32) + self.ldx[lax.rem(j, NL), a, :, hr].astype(F32)).astype(BF)
        self.cy(j, s).start()
        self.cdy(j, s).wait()
        for a in range(2):
            self.sx[s, a, hi, hr] = (self.sx[s, a, hi, hr].astype(F32) + self.ldy[lax.rem(j, NL), a, :, hr].astype(F32)).astype(BF)
        self.cx(j, s).start()

    def r3(self, j, s):
        hr = self.hr()
        self.cy(j, s).wait()
        self.cx(j, s).wait()
        for a in range(2):
            t = self.so[s, a, :, hr] + self.lx[lax.rem(j, NL), a, :, hr].astype(F32) + self.ly[lax.rem(j, NL), a, :, hr].astype(F32)
            self.so[s, a, :, hr] = t
            self.sz[lax.rem(j, 2), a, :, hr] = t.astype(BF)
        for k in range(3):
            self.cz(j, s, k).start()

    def r4(self, j, s):
        hr = self.hr()
        for k in range(3):
            self.cz(j, s, k).wait()
        for a in range(2):
            t = self.so[s, a, self.pc.z, hr]
            for k in range(3):
                t = t + self.lz[lax.rem(j, NL), k, a, hr].astype(F32)
            self.ob[s, a, hr] = t
        self.out(j, s, self.ob, self.os, "start")

    def go(self, stage, j):
        (self.r1, self.r2, self.r3, self.r4)[stage - 1](j, lax.rem(j, NS))

    def begin(self, j):
        self.r0(j, lax.rem(j, NS))

    def end(self, j):
        self.drain(j, lax.rem(j, NS))

    def drain(self, j, s):
        self.out(j, s, self.ob, self.os, "wait")


def scatter_scratch(n, h, w):
    return [
        pltpu.VMEM((2, 2, 2, 2, 2, 4, h, w), BF),
        pltpu.VMEM((3, 2, 2, 2, 4, h, w), BF),
        pltpu.VMEM((NL, 2, 2, h, w), BF),
        pltpu.VMEM((NL, 2, 2, h, w), BF),
        pltpu.VMEM((NL, 2, 4, h, w), BF),
        pltpu.VMEM((NL, 2, 4, h, w), BF),
        pltpu.VMEM((NL, 3, 2, h, w), BF),
        pltpu.VMEM((2, 2, 4, h, w), BF),
        pltpu.VMEM((NS, 2, 4, h, w), BF),
        pltpu.VMEM((NS, 2, 4, h, w), BF),
        pltpu.VMEM((NS, 2, 4, h, w), F32),
        pltpu.VMEM((2, 2, 4, h, w), BF),
        pltpu.VMEM((NS, 2, h, w), F32),
        pltpu.SemaphoreType.DMA((n, 8)),
        pltpu.SemaphoreType.DMA((n, 8)),
        pltpu.SemaphoreType.DMA((NS, 2)),
    ]


def inverse_rms(v):
    return lax.rsqrt(jnp.mean(v * v, axis=1, keepdims=True) + epsilon)


def block_kernel(
    tok_ref, cot_ref, doc_ref, count_ref, vec_ref, win_s, wout_s, wgate_s, wup_s, wdown_s,
    out_ref, gtok_ref, ggate_o, gup_o, gdown_o, gout_o, gin_o, small_o,
    win_h, wout_h, wd_h, wgu_h, vec_h, bcx_h, hid_h, mix_h, gdown_h,
    obuf, gn, nf, gf, nm, msk_ref, dlen, vec, vown, sm, sml, halo_t, halo_g, edge_s, edge_r,
    vsem, lsem, hsem, esem, gss, grs, *sc,
):
    pc = Place()
    tok, dim = tok_ref.shape
    ff = wgate_s.shape[-1]
    f = 512
    n = ff // f
    tt = 256
    nt_ = tok // tt
    part = sc[0]

    def cols(j, w=f):
        return pl.ds(pl.multiple_of(j * w, w), w)

    def simple(u, src, dst, c0, w):
        at = lambda b, m: dst.at[pl.ds(b, m), :, pl.ds(c0, w)]
        return Gather(pc, [lambda: src.at[:, :, pl.ds(c0, w)]], [at], at, gss.at[u], grs.at[u])

    def down_unit(i):
        rows = ff // 32
        at = lambda b, m: wd_h.at[pl.ds(pl.multiple_of(b * rows, rows), m * rows), pl.ds(256 * i, 256)]
        return Gather(pc, [lambda: wdown_s.at[:, pl.ds(256 * i, 256)]], [at], at, gss.at[5 + i], grs.at[5 + i])

    def gu_unit(j):
        srcs = [lambda: wgate_s.at[:, :, cols(j)], lambda: wup_s.at[:, :, cols(j)]]
        dsts = [lambda b, m: wgu_h.at[pl.ds(b, m), 0, :, cols(j)], lambda b, m: wgu_h.at[pl.ds(b, m), 1, :, cols(j)]]
        return Gather(pc, srcs, dsts, lambda b, m: wgu_h.at[pl.ds(b, m), :, :, cols(j)], gss.at[9 + j], grs.at[9 + j])

    def unit(u):
        if u == 0:
            return simple(0, vown, vec_h, 0, 128)
        if u < 4:
            return simple(u, win_s, win_h, 1024 * (u - 1), 1024)
        if u == 4:
            return simple(4, wout_s, wout_h, 0, 1024)
        if u < 9:
            return down_unit(u - 5)
        return gu_unit(u - 9)

    wd6 = wd_h.reshape(2, 2, 2, 4, ff // 32, dim)
    wgu7 = wgu_h.reshape(2, 2, 2, 4, 2, 32, ff)

    def down_view(y, x, z, c, p):
        return wd6.at[y, x, c, z, :, pl.ds(768, 256) if p is None else pl.ds(768 + 128 * p, 128)]

    def gu_view(y, x, z, c, p):
        return wgu7.at[y, x, c, z, slice(None) if p is None else p, :, pl.ds(ff - f, f)]

    late_down = GatherLate(pc, [lambda: wdown_s.at[:, pl.ds(768, 128)], lambda: wdown_s.at[:, pl.ds(896, 128)]],
                           down_view, gss.at[8], grs.at[8])
    late_gu = GatherLate(pc, [lambda: wgate_s.at[0, :, pl.ds(ff - f, f)], lambda: wup_s.at[0, :, pl.ds(ff - f, f)]],
                         gu_view, gss.at[8 + n], grs.at[8 + n])

    def small_copies(k):
        peers = [pc.core, pc.xn, pc.yn] + pc.zs
        return [remote(sm, sml.at[q], esem.at[q], esem.at[6 + q], peers[q]) for q in ((0,), (1,), (2,), (3, 4, 5))[k]]

    def small_begin(k):
        for c in small_copies(k):
            c.start()

    def small_end(k):
        for c in small_copies(k):
            c.wait()
        t = sm[...]
        for q in ((0,), (1,), (2,), (3, 4, 5))[k]:
            t = t + sml[q]
        sm[...] = t

    turn_of = [0, 1, 2, 3, 4, 5, 6, 7, 9, 10, 11, 12]

    def step(t):
        if t < 10:
            unit(turn_of[t]).s1()
            unit(turn_of[t + AHEAD]).s0()
        if t >= 2 and t < 10:
            unit(turn_of[t - 1]).s2()
        if t >= 3 and t < 11:
            unit(turn_of[t - 2]).s3()
        if t >= 4:
            unit(turn_of[t - 3]).s4()

    ndn = n + 4
    gdown6 = gdown_h.reshape(2, 2, 2, 4, ff // 32, dim)

    def act_on(copies, what):
        for c in copies:
            getattr(c, what)()

    def out_gu(j, s, ob, osem, what):
        act_on([pltpu.make_async_copy(ob.at[s, 0], ggate_o.at[:, cols(j)], osem.at[s, 0]),
                pltpu.make_async_copy(ob.at[s, 1], gup_o.at[:, cols(j)], osem.at[s, 1])], what)

    def out_rows(dst, r0, c0, h):
        def go(j, s, ob, osem, what):
            act_on([pltpu.make_async_copy(ob.at[s, a, pl.ds(0, h)],
                                          dst.at[pl.ds(r0, h), pl.ds(c0 + 512 * a, 512)], osem.at[s, a])
                    for a in range(2)], what)
        return go

    def out_down(j, s, ob, osem, what):
        out_rows(gdown_o, pl.multiple_of((j - n) * 32, 32), 0, 32)(j, s, ob, osem, what)

    def out_mixed(j, s, ob, osem, what):
        pl.when(j < n)(lambda: out_gu(j, s, ob, osem, what))
        pl.when(j >= n)(lambda: out_down(j, s, ob, osem, what))

    eng_gu = Scatter(pc, sc, 32, out_gu)
    eng_mid = Scatter(pc, sc, 32, out_mixed)
    order = (1, 0, 2)

    def eng(u):
        if u < ndn:
            return Scatter(pc, sc, 32, out_down)
        if u == ndn:
            return Scatter(pc, sc, 32, out_rows(gout_o, 0, 0, 32))
        if u < ndn + 4:
            return Scatter(pc, sc, 32, out_rows(gin_o, 0, 1024 * order[u - ndn - 1], 32))
        return Scatter(pc, sc, 16, out_rows(gdown_o, 128, 0, 16))

    pc.greet()
    vown[0] = pltpu.roll(vec_ref[...], 32 * pc.z, 1)
    unit(0).s0()
    unit(1).s0()
    cot_copy = pltpu.make_async_copy(cot_ref, gf, hsem.at[0])
    cot_copy.start()
    tail = remote(tok_ref.at[pl.ds(tok - 16, 16)], halo_t, hsem.at[1], hsem.at[2], pc.zs[0])
    tail.start()
    sm[...] = jnp.zeros_like(sm)
    edge_s[...] = jnp.zeros_like(edge_s)
    gn[...] = jnp.zeros_like(gn)
    row_devs = ROW_LEN // tok
    row = pc.me // row_devs
    dlen[...] = jnp.zeros_like(dlen)
    dlen[0:1, 0:16] = doc_ref[pl.ds(row, 1), :]
    lens = dlen[...]
    lane = lax.broadcasted_iota(jnp.int32, (8, 128), 1)
    sums = lens
    for k in (1, 2, 4, 8):
        sums = sums + jnp.where(lane >= k, pltpu.roll(sums, k, 1), 0)
    starts = jnp.where(lane < 16, sums - lens, -8)[0:1, :]
    limit = count_ref[row]
    cot_copy.wait()

    def live_rows(i, _):
        r = cols(i, tt)
        t = i * tt + lax.broadcasted_iota(jnp.int32, (tt, 128), 0)
        place = lax.rem(pc.me, row_devs) * tok + t

        def begins(by):
            return jnp.max(jnp.where(starts == place + by, 1.0, 0.0), axis=1, keepdims=True)

        b0, b1, b2, bm = begins(0), begins(1), begins(2), begins(-1)
        ln = lax.broadcasted_iota(jnp.int32, (tt, 128), 1)
        m = jnp.where(ln == 0, 1.0 - b0, 1.0 - jnp.maximum(b0, bm))
        m = jnp.where(ln == 2, jnp.where(place < limit, 1.0, 0.0), m)
        m = jnp.where(ln == 3, jnp.where(t + 1 < tok, 1.0 - b1, 0.0), m)
        msk_ref[r, :] = jnp.where(ln == 4, jnp.where(t + 2 < tok, 1.0 - jnp.maximum(b2, b1), 0.0), m)
        gf[r, :] = (gf[r, :].astype(F32) * msk_ref[r, 2:3]).astype(BF)
        return 0

    lax.fori_loop(0, nt_, live_rows, 0)
    unit(0).s1()
    unit(2).s0()
    late_down.s0()
    late_gu.s0()
    unit(1).s1()
    unit(3).s0()
    unit(0).s2()
    step(2)
    unit(0).s3()
    late_down.s1()
    late_gu.s1()
    step(3)
    late_down.s2()
    late_down.piece(0)
    unit(0).s4()

    def mixer_forward(vbuf, win, wout, st, mst, tb):
        vcopy = pltpu.make_async_copy(vec_h, vbuf, vsem.at[0])
        vcopy.start()
        vcopy.wait()
        for q in range(8):
            v = vbuf[4 * q] + vbuf[4 * q + 1] + vbuf[4 * q + 2] + vbuf[4 * q + 3]
            vec[:, 128 * q : 128 * q + 128] = v
        gain = vec[0:1, :]

        def normed(i, _):
            r = cols(i, tt)
            t = tok_ref[r, :].astype(F32)
            nm[r, :] = (t * inverse_rms(t) * gain).astype(BF)
            return 0

        lax.fori_loop(0, nt_, normed, 0)
        wl = [pltpu.make_async_copy(win_h.at[:, :, pl.ds(1024 * i, 1024)], win.at[i], vsem.at[i]) for i in range(3)]
        wl.append(pltpu.make_async_copy(wout_h, wout, vsem.at[3]))
        for t in (4, 5, 6, 7):
            step(t)
            late_down.piece(2 * t - 7)
            late_down.piece(2 * t - 6)
            wl[t - 4].start()
        tail.wait()
        th = halo_t[...].astype(F32)
        nh = (th * inverse_rms(th) * gain).astype(BF)
        for c in wl:
            c.wait()
        hb = dg(nh, win[0].reshape(dim, dim), 1, 0) * dg(nh, win[2].reshape(dim, dim), 1, 0)
        halo_g[...] = hb[8:16, :]
        tb[0:8, :] = halo_g[...]

        def stash(i, s):
            r = cols(i, tt)
            return [pltpu.make_async_copy(st.at[s, k], bcx_h.at[k, r], lsem.at[s, k]) for k in range(3)] + [
                pltpu.make_async_copy(mst.at[s], mix_h.at[r], lsem.at[s, 3]),
                pltpu.make_async_copy(obuf.at[r], hid_h.at[r], lsem.at[s, 4])]

        def tile(i, _):
            r = cols(i, tt)
            s = lax.rem(i, 2)
            pl.when(i >= 2)(lambda: act_on(stash(i - 2, s), "wait"))
            x = nm[r, :]
            bv = dg(x, win[0].reshape(dim, dim), 1, 0)
            st[s, 0] = bv
            xv = dg(x, win[2].reshape(dim, dim), 1, 0)
            st[s, 2] = xv
            tb[8 : 8 + tt, :] = bv * xv
            cv = dg(x, win[1].reshape(dim, dim), 1, 0)
            st[s, 1] = cv
            k1, k2 = msk_ref[r, 0:1], msk_ref[r, 1:2]
            conv = (vec[4:5, :] * tb[8 : 8 + tt, :] + vec[3:4, :] * (k1 * tb[7 : 7 + tt, :])
                    + vec[2:3, :] * (k2 * tb[6 : 6 + tt, :]))
            mixed = (cv * conv).astype(BF)
            mst[s] = mixed
            tb[0:8, :] = tb[tt : tt + 8, :]
            h = tok_ref[r, :].astype(F32) + dg(mixed, wout[...].reshape(dim, dim), 1, 0)
            obuf[r, :] = h
            nf[r, :] = (h * inverse_rms(h) * vec[1:2, :]).astype(BF)
            act_on(stash(i, s), "start")
            for k, t in ((0, 8), (1, 9), (3, 10)):
                pl.when(i == k)(functools.partial(step, t))
            pl.when(i < 3)(lambda: late_down.piece(9 + i))
            pl.when(i == 3)(late_down.s3)
            return 0

        lax.fori_loop(0, nt_, tile, 0)
        for i in (nt_ - 2, nt_ - 1):
            act_on(stash(i, i % 2), "wait")

    pl.run_scoped(
        mixer_forward, pltpu.VMEM((32, 8, 128), F32), pltpu.VMEM((3, 32, 32, dim), BF), pltpu.VMEM((32, 32, dim), BF),
        pltpu.VMEM((2, 3, tt, dim), F32), pltpu.VMEM((2, tt, dim), BF), pltpu.VMEM((tt + 8, dim), F32),
    )
    step(11)
    late_down.s4()

    def put(b3, j, s):
        return pltpu.make_async_copy(b3.at[s], gdown_h.at[cols(j), :], vsem.at[s])

    def ffn(gw, uw, dw, act, gg, gu, nt, b3):
        tm = td = 512

        def fetch(j, s):
            return [pltpu.make_async_copy(wgu_h.at[:, 0, :, cols(j)], gw.at[s], lsem.at[s, 0]),
                    pltpu.make_async_copy(wgu_h.at[:, 1, :, cols(j)], uw.at[s], lsem.at[s, 1]),
                    pltpu.make_async_copy(wd_h.at[cols(j), :], dw.at[s], lsem.at[s, 2])]

        act_on(fetch(0, 0), "start")

        def turned(i, _):
            nt[:, cols(i, tt)] = nf[cols(i, tt), :].T
            return 0

        lax.fori_loop(0, nt_, turned, 0)

        def body(j, carry):
            s = lax.rem(j, 2)

            def stage(fn, k, lo=0, hi=n):
                pl.when(jnp.logical_and(j + k >= lo, j + k < hi))(lambda: fn(j + k))

            act_on(fetch(j, s), "wait")

            def tile(i):
                r = pl.ds(i * tm, tm)
                x = nf[r, :]
                g_w, u_w = gw[s].reshape(dim, f), uw[s].reshape(dim, f)
                g = dg(x, g_w, 1, 0)
                u = dg(x, u_w, 1, 0)
                ga = dg(gf[r, :], dw[s], 1, 1)
                sg = jax.nn.sigmoid(g)
                si = g * sg
                a = (si * u).astype(BF)
                act[r, :] = a
                ggv = (ga * u * sg * (1.0 + g * (1.0 - sg))).astype(BF)
                guv = (ga * si).astype(BF)
                gg[r, :] = ggv
                gu[r, :] = guv
                obuf[r, :] += dg(a, dw[s], 1, 0)
                gn[r, :] += dg(ggv, g_w, 1, 1) + dg(guv, u_w, 1, 1)

            tile(0)
            pl.when(jnp.logical_and(j >= 1, j < 7))(lambda: late_gu.piece(2 * j - 2))
            pl.when(j == n - 2)(late_gu.s3)
            stage(lambda u: gu_unit(u).s2(), 1, 1, n - 1)
            stage(lambda u: eng_gu.go(2, u), -1)
            stage(lambda u: gu_unit(u).s1(), 2, 2, n - 1)
            tile(1)
            stage(lambda u: eng_gu.go(4, u), -2)
            stage(lambda u: gu_unit(u).s0(), 2 + AHEAD, 2 + AHEAD, n - 1)
            pl.when(j == 0)(late_gu.s2)
            pl.when(jnp.logical_and(j >= 1, j < 7))(lambda: late_gu.piece(2 * j - 1))
            for i in range(dim // td):
                x = nt[i * td : (i + 1) * td, :]
                part[s, 0, i] = dg(x, gg[...], 1, 0).astype(BF).reshape(2, 2, 4, 32, f)
                part[s, 1, i] = dg(x, gu[...], 1, 0).astype(BF).reshape(2, 2, 4, 32, f)
            eng_gu.begin(j)
            stage(lambda u: gu_unit(u).s3(), 1, 1, n - 1)
            stage(lambda u: gu_unit(u).s4(), 1, 1, n - 1)
            pl.when(j == n - 2)(late_gu.s4)
            stage(lambda u: act_on(fetch(u, 1 - s), "start"), 1)
            pl.when(j >= 2)(lambda: put(b3, j - 2, s).wait())
            for i in range(f // 256):
                b3[s, i * 256 : (i + 1) * 256, :] = dg(act[:, i * 256 : (i + 1) * 256].T, gf[...], 1, 0).astype(BF)
            put(b3, j, s).start()
            stage(lambda u: eng_gu.go(3, u), -1)
            eng_gu.go(1, j)
            stage(lambda u: eng_gu.end(u), -2)
            return carry

        lax.fori_loop(0, n, body, 0)
        for j in (n - 2, n - 1):
            put(b3, j, j % 2).wait()

    pl.run_scoped(
        ffn, pltpu.VMEM((2, 32, 32, f), BF), pltpu.VMEM((2, 32, 32, f), BF), pltpu.VMEM((2, f, dim), BF),
        pltpu.VMEM((tok, f), BF), pltpu.VMEM((tok, f), BF), pltpu.VMEM((tok, f), BF),
        pltpu.VMEM((dim, tok), BF), pltpu.VMEM((2, f, dim), BF),
    )

    def load_down(u, r0, h):
        s = lax.rem(u, 2)
        return [pltpu.make_async_copy(gdown6.at[:, :, :, :, pl.ds(r0, h), pl.ds(512 * a, 512)],
                                      part.at[s, a, :, :, :, :, pl.ds(0, h)], vsem.at[2 + a]) for a in range(2)]

    def load_mid(u):
        return load_down(u, pl.multiple_of((u - n) * 32, 32), 32)

    def mixer_backward(gp, turn, wout):
        wcopy = pltpu.make_async_copy(wout_h, wout, vsem.at[0])
        act_on(load_mid(n), "start")
        wcopy.start()
        act_on(load_mid(n), "wait")
        eng_mid.begin(n)

        def turned(i, _):
            turn[:, cols(i, tt)] = nm[cols(i, tt), :].T
            return 0

        lax.fori_loop(0, nt_, turned, 0)
        mcopy = pltpu.make_async_copy(mix_h, nm, vsem.at[1])
        mcopy.start()
        wcopy.wait()

        def advance(u):
            for k, stage in ((1, 2), (0, 1), (2, 3), (3, 4)):
                if u - k < ndn + 5:
                    eng(u - k).go(stage, u - k)

        def grad_in(k, s):
            for i in range(2):
                for a in range(2):
                    t = dg(turn[512 * i : 512 * i + 512, :], gp[:, 1024 * k + 512 * a : 1024 * k + 512 * a + 512], 1, 0)
                    part[s, a, i] = t.astype(BF).reshape(2, 2, 4, 32, 512)

        def part_of(u):
            if u == ndn:
                for i in range(4):
                    t = dg(nm[:, 256 * i : 256 * i + 256].T, nf[...], 1, 0).astype(BF)
                    for a in range(2):
                        part[u % 2, a, i // 2, i % 2] = t[:, 512 * a : 512 * a + 512].reshape(2, 4, 32, 512)
            elif u < ndn + 4:
                grad_in(order[u - ndn - 1], u % 2)
            else:
                act_on(load_down(u, 128, 16), "start")
                act_on(load_down(u, 128, 16), "wait")

        def passes(ld, ost, tb, tb2):
            def fetch(i, s):
                r = cols(i, tt)
                return [pltpu.make_async_copy(bcx_h.at[k, r], ld.at[s, k], lsem.at[s, k]) for k in range(3)] + [
                    pltpu.make_async_copy(hid_h.at[r], ld.at[s, 3], lsem.at[s, 3])]

            def put_out(i):
                return pltpu.make_async_copy(ost, out_ref.at[cols(i, tt)], lsem.at[0, 4])

            act_on(fetch(0, 0), "start")
            tb[0:8, :] = halo_g[...]
            obuf[tok : tok + 8, :] = jnp.zeros((8, dim), F32)

            def two(i, s):
                r = cols(i, tt)
                tb2[...] = obuf[pl.ds(pl.multiple_of(i * tt, tt), tt + 8), :]
                k1, k2 = msk_ref[r, 3:4], msk_ref[r, 4:5]
                tb2[0:tt, :] = (vec[4:5, :] * tb2[0:tt, :] + vec[3:4, :] * (k1 * tb2[1 : 1 + tt, :])
                                + vec[2:3, :] * (k2 * tb2[2 : 2 + tt, :]))

                @pl.when(i == nt_ - 1)
                def _():
                    tb2[tt - 8 : tt, :] += edge_r[...]

                gg = tb2[0:tt, :]
                gp[r, 0:1024] = (gg * ld[s, 2]).astype(BF)
                gp[r, 2048:3072] = (gg * ld[s, 0]).astype(BF)

            def one(i, _):
                u = n + i
                s = lax.rem(i, 2)
                r = cols(i, tt)
                eng_mid.go(2, u - 1)
                eng_mid.go(1, u)
                pl.when(i >= 1)(lambda: eng_mid.go(3, u - 2))
                pl.when(i != 1)(lambda: eng_mid.go(4, jnp.where(i == 0, n - 2, u - 3)))
                pl.when(i + 1 < nt_)(lambda: act_on(load_mid(u + 1), "start"))
                act_on(fetch(i, s), "wait")
                pl.when(i >= 1)(lambda: put_out(i - 1).wait())
                ost[...] = obuf[r, :] * msk_ref[r, 2:3]
                put_out(i).start()
                v = ld[s, 3]
                g = gn[r, :]
                inv = inverse_rms(v)
                a = g * vec[1:2, :]
                dot = jnp.sum(a * v, axis=1, keepdims=True) / dim
                ghid = gf[r, :].astype(F32) + (inv * a - v * (inv * inv * inv) * dot)
                sm[1:2, :] += jnp.sum(g * v * inv, axis=0, keepdims=True)
                gn[r, :] = ghid
                low = ghid.astype(BF)
                nf[r, :] = low
                gm = dg(low, wout[...].reshape(dim, dim), 1, 1)
                tb[8 : 8 + tt, :] = ld[s, 0] * ld[s, 2]
                k1, k2 = msk_ref[r, 0:1], msk_ref[r, 1:2]
                gated, lag1, lag2 = tb[8 : 8 + tt, :], k1 * tb[7 : 7 + tt, :], k2 * tb[6 : 6 + tt, :]
                conv = vec[4:5, :] * gated + vec[3:4, :] * lag1 + vec[2:3, :] * lag2
                gp[r, 1024:2048] = (gm * conv).astype(BF)
                gc = gm * ld[s, 1]
                obuf[r, :] = gc
                sm[2:3, :] += jnp.sum(gc * lag2, axis=0, keepdims=True)
                sm[3:4, :] += jnp.sum(gc * lag1, axis=0, keepdims=True)
                sm[4:5, :] += jnp.sum(gc * gated, axis=0, keepdims=True)
                tb[0:8, :] = tb[tt : tt + 8, :]

                @pl.when(i == 0)
                def _():
                    first, second = obuf[0:1, :], obuf[1:2, :]
                    k1a, k2a, k2b = msk_ref[0:1, 0:1], msk_ref[0:1, 1:2], msk_ref[1:2, 1:2]
                    edge_s[6:7, :] = vec[2:3, :] * (k2a * first)
                    edge_s[7:8, :] = vec[3:4, :] * (k1a * first) + vec[2:3, :] * (k2b * second)
                    edge.start()

                pl.when(i >= 1)(lambda: two(i - 1, 1 - s))

                @pl.when(i + 1 < nt_)
                def _():
                    act_on(fetch(i + 1, 1 - s), "start")
                    act_on(load_mid(u + 1), "wait")
                    eng_mid.begin(u + 1)

                pl.when(i != 1)(lambda: eng_mid.end(jnp.where(i == 0, n - 2, u - 3)))
                return 0

            lax.fori_loop(0, nt_, one, 0)
            mcopy.wait()
            part_of(ndn)
            eng(ndn).begin(ndn)
            put_out(nt_ - 1).wait()
            edge.wait()
            two(nt_ - 1, (nt_ - 1) % 2)

        edge = remote(edge_s, edge_r, hsem.at[3], hsem.at[4], pc.zs[2])
        pl.run_scoped(passes, pltpu.VMEM((2, 4, tt, dim), F32), pltpu.VMEM((tt, dim), F32),
                      pltpu.VMEM((tt + 8, dim), F32), pltpu.VMEM((tt + 8, dim), F32))

        def ending(win, ost):
            wl = [pltpu.make_async_copy(win_h.at[:, :, pl.ds(1024 * i, 1024)], win.at[i], lsem.at[0, i]) for i in range(3)]
            act_on(wl, "start")

            def put_tok(i, s):
                return pltpu.make_async_copy(ost.at[s], gtok_ref.at[cols(i, tt)], lsem.at[s, 4])

            def grad_tok(i, _):
                s = lax.rem(i, 2)
                r = cols(i, tt)
                g = dg(gp[r, 0:1024], win[0].reshape(dim, dim), 1, 1)
                g = g + dg(gp[r, 1024:2048], win[1].reshape(dim, dim), 1, 1)
                g = g + dg(gp[r, 2048:3072], win[2].reshape(dim, dim), 1, 1)
                v = tok_ref[r, :].astype(F32)
                inv = inverse_rms(v)
                a = g * vec[0:1, :]
                dot = jnp.sum(a * v, axis=1, keepdims=True) / dim
                pl.when(i >= 2)(lambda: put_tok(i - 2, s).wait())
                ost[s] = gn[r, :] + (inv * a - v * (inv * inv * inv) * dot)
                put_tok(i, s).start()
                sm[0:1, :] += jnp.sum(g * v * inv, axis=0, keepdims=True)
                return 0

            for u in range(ndn, ndn + 8):
                advance(u)
                if u < ndn + 4:
                    part_of(u + 1)
                    eng(u + 1).begin(u + 1)
                if u == ndn:
                    act_on(wl, "wait")
                if u in (ndn + 1, ndn + 2):
                    lax.fori_loop(2 * (u - ndn - 1), 2 * (u - ndn), grad_tok, 0)
                if u == ndn + 2:
                    small_begin(0)
                elif u > ndn + 2 and u < ndn + 6:
                    small_end(u - ndn - 3)
                    small_begin(u - ndn - 2)
                elif u == ndn + 6:
                    small_end(3)
                    outs = pltpu.make_async_copy(sm, small_o, hsem.at[0])
                    outs.start()
                eng(u - 3).end(u - 3)
            outs.wait()
            for i in (nt_ - 2, nt_ - 1):
                put_tok(i, i % 2).wait()

        pl.run_scoped(ending, pltpu.VMEM((3, 32, 32, dim), BF), pltpu.VMEM((2, tt, dim), F32))

    pl.run_scoped(mixer_backward, pltpu.VMEM((tok, 3 * dim), BF), pltpu.VMEM((dim, tok), BF), pltpu.VMEM((32, 32, dim), BF))

    for u in range(8):
        unit(u).fin()
    late_down.fin()
    late_gu.fin()

    def last(j, carry):
        gu_unit(j).fin()
        return carry

    lax.fori_loop(0, n - 1, last, 0)


def deliver_kernel(pieces, n, *refs):
    ins, outs, bufs, sems = refs[:n], refs[n : 2 * n], refs[2 * n : 3 * n], refs[3 * n]
    every = [(i, r) for i in range(n) for r in pieces[i]]
    load = [pltpu.make_async_copy(ins[i].at[pl.ds(*r)], bufs[i].at[pl.ds(*r)], sems.at[0, q]) for q, (i, r) in enumerate(every)]
    store = [pltpu.make_async_copy(bufs[i].at[pl.ds(*r)], outs[i].at[pl.ds(*r)], sems.at[1, q]) for q, (i, r) in enumerate(every)]
    for c in load:
        c.start()
    for c, d in zip(load, store):
        c.wait()
        d.start()
    for d in store:
        d.wait()


def deliver(arrays):
    n = len(arrays)
    pieces = []
    for a in arrays:
        rows = a.shape[0] // 8 if a.shape[0] % 64 == 0 else a.shape[0]
        pieces.append([(r, rows) for r in range(0, a.shape[0], rows)])
    return pl.pallas_call(
        functools.partial(deliver_kernel, pieces, n),
        out_shape=[jax.ShapeDtypeStruct(a.shape, a.dtype) for a in arrays],
        in_specs=[ANY] * n,
        out_specs=[ANY] * n,
        scratch_shapes=[pltpu.VMEM(a.shape, a.dtype) for a in arrays]
        + [pltpu.SemaphoreType.DMA((2, sum(map(len, pieces))))],
        name="deliver",
        compiler_params=pltpu.CompilerParams(vmem_limit_bytes=60 * 2**20),
    )(*arrays)


def block_call(tokens, cot, lengths, counts, vecs, w_in, w_out, w_gate, w_up, w_down):
    tok, dim = tokens.shape
    ff = w_gate.shape[1]
    n = ff // 512
    sd = jax.ShapeDtypeStruct
    outs = [
        sd((tok, dim), F32), sd((tok, dim), F32), sd((32, ff), F32), sd((32, ff), F32), sd((ff // 32, dim), F32),
        sd((32, dim), F32), sd((32, 3 * dim), F32), sd((8, dim), F32),
        sd((32, 32, 3 * dim), BF), sd((32, 32, dim), BF), sd((ff, dim), BF), sd((32, 2, 32, ff), BF),
        sd((32, 8, 128), F32), sd((3, tok, dim), F32), sd((tok, dim), F32), sd((tok, dim), BF), sd((ff, dim), BF),
    ]
    return pl.pallas_call(
        block_kernel,
        out_shape=outs,
        in_specs=[VM, ANY, VM, pl.BlockSpec(memory_space=pltpu.SMEM), VM, ANY, ANY, ANY, ANY, ANY],
        out_specs=[ANY] * len(outs),
        scratch_shapes=[
            pltpu.VMEM((tok + 8, dim), F32),
            pltpu.VMEM((tok, dim), F32),
            pltpu.VMEM((tok, dim), BF),
            pltpu.VMEM((tok, dim), BF),
            pltpu.VMEM((tok, dim), BF),
            pltpu.VMEM((tok, 128), F32),
            pltpu.VMEM((8, 128), jnp.int32),
            pltpu.VMEM((8, dim), F32),
            pltpu.VMEM((1, 8, 128), F32),
            pltpu.VMEM((8, dim), F32),
            pltpu.VMEM((6, 8, dim), F32),
            pltpu.VMEM((16, dim), BF),
            pltpu.VMEM((8, dim), F32),
            pltpu.VMEM((8, dim), F32),
            pltpu.VMEM((8, dim), F32),
            pltpu.SemaphoreType.DMA((4,)),
            pltpu.SemaphoreType.DMA((2, 5)),
            pltpu.SemaphoreType.DMA((5,)),
            pltpu.SemaphoreType.DMA((12,)),
            pltpu.SemaphoreType.DMA((n + 9, NG)),
            pltpu.SemaphoreType.DMA((n + 9, NG)),
        ] + scatter_scratch(n + 9, 32, 512),
        name="block",
        compiler_params=pltpu.CompilerParams(collective_id=1, has_side_effects=True, vmem_limit_bytes=62 * 2**20 + 2**19),
    )(tokens, cot, lengths, counts, vecs, w_in[None], w_out[None], w_gate[None], w_up[None], w_down)


def passed_along(array, axis, by):
    size = lax.axis_size(axis)
    pairs = [(i, i + by) for i in range(size) if 0 <= i + by < size]
    return lax.ppermute(array, axis, pairs)


def rms_forward(values, gain_vec):
    inv_rms = lax.rsqrt(jnp.mean(values * values, axis=1, keepdims=True) + epsilon)
    return (values * inv_rms * gain_vec[None, :], inv_rms)


def rms_backward(values, inv_rms, gain_vec, grad_normed):
    weighted = grad_normed * gain_vec[None, :]
    features = values.shape[1]
    total_dot = jnp.sum(weighted * values, axis=1, keepdims=True)
    grad_values = inv_rms * weighted - values * (inv_rms * inv_rms * inv_rms) * total_dot / features
    grad_gain = jnp.sum(grad_normed * values * inv_rms, axis=0)
    return (grad_values, grad_gain)


def outer_sum(left, right):
    return lax.dot_general(
        left, right, (((0,), (0,)), ((), ())), preferred_element_type=jnp.float32
    )


def back_product(grad_low, weight_mat):
    return lax.dot_general(
        grad_low, weight_mat, (((1,), (1,)), ((), ())), preferred_element_type=jnp.float32
    )


def doc_masks(doc_lengths, valid_count, first_pos, tok_count):
    packed_row = first_pos // ROW_LEN
    lengths = lax.dynamic_index_in_dim(doc_lengths, packed_row, 0, keepdims=False)
    limit_count = lax.dynamic_index_in_dim(valid_count, packed_row, 0, keepdims=False)
    offsets = jnp.cumsum(lengths) - lengths
    places = first_pos % ROW_LEN + jnp.arange(tok_count, dtype=jnp.int32)
    begins = jnp.any(offsets[None, :] == places[:, None], axis=1)
    before = jnp.any(offsets[None, :] == places[:, None] - 1, axis=1)
    keep_one = jnp.where(begins, 0.0, 1.0).astype(jnp.float32)
    keep_two = jnp.where(begins | before, 0.0, 1.0).astype(jnp.float32)
    live_mask = jnp.where(places < limit_count, 1.0, 0.0).astype(jnp.float32)
    return (keep_one[:, None], keep_two[:, None], live_mask[:, None])


def shards_plain(
    tokens,
    cotangent,
    gain_mix,
    in_weight,
    conv_taps,
    out_weight,
    gain_ffn,
    gate_weight,
    up_weight,
    down_weight,
    doc_lengths,
    valid_count,
):
    tok_count = tokens.shape[0]
    first_pos = lax.axis_index(("wide", "narrow")) * tok_count
    keep_one, keep_two, live_mask = doc_masks(doc_lengths, valid_count, first_pos, tok_count)
    full_gm, w_in, full_taps, w_out, full_gf, w_gate, w_up, w_down = (
        lax.all_gather(gain_mix, ("wide", "narrow"), axis=0, tiled=True),
        lax.all_gather(in_weight, ("wide", "narrow"), axis=0, tiled=True),
        lax.all_gather(conv_taps, ("wide", "narrow"), axis=1, tiled=True),
        lax.all_gather(out_weight, ("wide", "narrow"), axis=0, tiled=True),
        lax.all_gather(gain_ffn, ("wide", "narrow"), axis=0, tiled=True),
        lax.all_gather(gate_weight, ("wide", "narrow"), axis=0, tiled=True),
        lax.all_gather(up_weight, ("wide", "narrow"), axis=0, tiled=True),
        lax.all_gather(down_weight, ("wide", "narrow"), axis=0, tiled=True),
    )
    mix_gain = full_gm.astype(jnp.float32)
    ffn_gain = full_gf.astype(jnp.float32)
    taps = full_taps.astype(jnp.float32)
    features = tokens.shape[1]
    tok_float = tokens.astype(jnp.float32)
    normed_mix, inv_mix = rms_forward(tok_float, mix_gain)
    normed_low = normed_mix.astype(jnp.bfloat16)
    projected = jnp.dot(normed_low, w_in, preferred_element_type=jnp.float32)
    b_part = projected[:, :features]
    c_part = projected[:, features : 2 * features]
    x_part = projected[:, 2 * features :]
    gated = b_part * x_part
    edge_rows = passed_along(gated[-2:], "narrow", 1)
    extended = jnp.concatenate([edge_rows, gated], axis=0)
    lag_one = keep_one * extended[1:-1]
    lag_two = keep_two * extended[:-2]
    conv_out = taps[2][None, :] * gated + taps[1][None, :] * lag_one + taps[0][None, :] * lag_two
    mixed_low = (c_part * conv_out).astype(jnp.bfloat16)
    hidden_res = tok_float + jnp.dot(mixed_low, w_out, preferred_element_type=jnp.float32)
    normed_ffn, inv_ffn = rms_forward(hidden_res, ffn_gain)
    ffn_low = normed_ffn.astype(jnp.bfloat16)
    gate_val = jnp.dot(ffn_low, w_gate, preferred_element_type=jnp.float32)
    up_val = jnp.dot(ffn_low, w_up, preferred_element_type=jnp.float32)
    sigmoid_gate = jax.nn.sigmoid(gate_val)
    silu_val = gate_val * sigmoid_gate
    act_low = (silu_val * up_val).astype(jnp.bfloat16)
    ffn_out = jnp.dot(act_low, w_down, preferred_element_type=jnp.float32)
    output = live_mask * (hidden_res + ffn_out)
    again_gm, w_in, again_taps, w_out, again_gf, w_gate, w_up, w_down = (
        lax.all_gather(gain_mix, ("wide", "narrow"), axis=0, tiled=True),
        lax.all_gather(in_weight, ("wide", "narrow"), axis=0, tiled=True),
        lax.all_gather(conv_taps, ("wide", "narrow"), axis=1, tiled=True),
        lax.all_gather(out_weight, ("wide", "narrow"), axis=0, tiled=True),
        lax.all_gather(gain_ffn, ("wide", "narrow"), axis=0, tiled=True),
        lax.all_gather(gate_weight, ("wide", "narrow"), axis=0, tiled=True),
        lax.all_gather(up_weight, ("wide", "narrow"), axis=0, tiled=True),
        lax.all_gather(down_weight, ("wide", "narrow"), axis=0, tiled=True),
    )
    mix_gain = again_gm.astype(jnp.float32)
    ffn_gain = again_gf.astype(jnp.float32)
    taps = again_taps.astype(jnp.float32)
    grad_res = live_mask * cotangent.astype(jnp.float32)
    grad_ffn_low = grad_res.astype(jnp.bfloat16)
    grad_down = outer_sum(act_low, grad_ffn_low)
    grad_act = back_product(grad_ffn_low, w_down)
    grad_gate_low = (
        grad_act * up_val * sigmoid_gate * (1.0 + gate_val * (1.0 - sigmoid_gate))
    ).astype(jnp.bfloat16)
    grad_up_low = (grad_act * silu_val).astype(jnp.bfloat16)
    grad_gate = outer_sum(ffn_low, grad_gate_low)
    grad_up = outer_sum(ffn_low, grad_up_low)
    grad_nffn = back_product(grad_gate_low, w_gate) + back_product(grad_up_low, w_up)
    grad_hnorm, grad_gf = rms_backward(hidden_res, inv_ffn, ffn_gain, grad_nffn)
    grad_hidden = grad_res + grad_hnorm
    grad_mix_low = grad_hidden.astype(jnp.bfloat16)
    grad_out = outer_sum(mixed_low, grad_mix_low)
    grad_mixed = back_product(grad_mix_low, w_out)
    grad_c = grad_mixed * conv_out
    grad_conv = grad_mixed * c_part
    grad_taps = jnp.stack(
        [
            jnp.sum(grad_conv * lag_two, axis=0),
            jnp.sum(grad_conv * lag_one, axis=0),
            jnp.sum(grad_conv * gated, axis=0),
        ],
        axis=0,
    )
    lag_grad_one = taps[1][None, :] * keep_one * grad_conv
    lag_grad_two = taps[0][None, :] * keep_two * grad_conv
    grad_ext = (
        jnp.pad(taps[2][None, :] * grad_conv, ((2, 0), (0, 0)))
        + jnp.pad(lag_grad_one, ((1, 1), (0, 0)))
        + jnp.pad(lag_grad_two, ((0, 2), (0, 0)))
    )
    from_right = passed_along(grad_ext[:2], "narrow", -1)
    grad_gated = jnp.concatenate([grad_ext[2:-2], grad_ext[-2:] + from_right], axis=0)
    grad_b = grad_gated * x_part
    grad_x = grad_gated * b_part
    grad_proj_low = jnp.concatenate([grad_b, grad_c, grad_x], axis=1).astype(jnp.bfloat16)
    grad_in = outer_sum(normed_low, grad_proj_low)
    grad_nmix = back_product(grad_proj_low, w_in)
    grad_tnorm, grad_gm = rms_backward(tok_float, inv_mix, mix_gain, grad_nmix)
    grad_tokens = grad_hidden + grad_tnorm
    sum_gm, sum_in, sum_taps, sum_out, sum_gf, sum_gate, sum_up, sum_down = (
        lax.psum_scatter(grad_gm, ("wide", "narrow"), scatter_dimension=0, tiled=True),
        lax.psum_scatter(grad_in, ("wide", "narrow"), scatter_dimension=0, tiled=True),
        lax.psum_scatter(grad_taps, ("wide", "narrow"), scatter_dimension=1, tiled=True),
        lax.psum_scatter(grad_out, ("wide", "narrow"), scatter_dimension=0, tiled=True),
        lax.psum_scatter(grad_gf, ("wide", "narrow"), scatter_dimension=0, tiled=True),
        lax.psum_scatter(grad_gate, ("wide", "narrow"), scatter_dimension=0, tiled=True),
        lax.psum_scatter(grad_up, ("wide", "narrow"), scatter_dimension=0, tiled=True),
        lax.psum_scatter(grad_down, ("wide", "narrow"), scatter_dimension=0, tiled=True),
    )
    return (
        output,
        grad_tokens,
        sum_gm,
        sum_in,
        sum_taps,
        sum_out,
        sum_gf,
        sum_gate,
        sum_up,
        sum_down,
    )


def shards(
    tokens, cotangent, gain_mix, in_weight, conv_taps, out_weight, gain_ffn,
    gate_weight, up_weight, down_weight, doc_lengths, valid_count,
):
    me = lax.axis_index(("wide", "narrow"))
    own = gain_mix.shape[0]
    vecs = jnp.concatenate([gain_mix[None], gain_ffn[None], conv_taps], axis=0).astype(F32)
    vecs = jnp.pad(vecs, ((0, 3), (0, 128 - own)))
    output, grad_tokens, sum_gate, sum_up, sum_down, sum_out, sum_in, all_small = block_call(
        tokens, cotangent, doc_lengths, valid_count, vecs, in_weight, out_weight, gate_weight, up_weight, down_weight
    )[:8]
    output, grad_tokens, sum_gate, sum_up, sum_down, sum_out, sum_in = deliver(
        [output, grad_tokens, sum_gate, sum_up, sum_down, sum_out, sum_in]
    )
    mine = lax.dynamic_slice_in_dim(all_small, me * own, own, 1)
    return (output, grad_tokens, mine[0], sum_in, mine[2:5], sum_out, mine[1], sum_gate, sum_up, sum_down)


def solution(mesh):
    both = ("wide", "narrow")
    rows, vec, flat = P(both, None), P(both), P(None, both)
    step = shards if (mesh.shape["wide"], mesh.shape["narrow"]) == (8, 4) else shards_plain
    return jax.shard_map(
        step,
        mesh=mesh,
        in_specs=(rows, rows, vec, rows, flat, rows, vec, rows, rows, rows, P(), P()),
        out_specs=(rows, rows, vec, rows, flat, rows, vec, rows, rows, rows),
        check_vma=False,
    )
```
